128 devices in a mesh: vrow: 8 (over z, y_hi), img: 16 (over x, y_lo, core).
Axes of the slice: x: 4, y: 4 (y_hi: 2, y_lo: 2; y = y_hi * 2 + y_lo), z: 4, core: 2. Of those that a mesh axis runs over, the one named last changes fastest.
Arguments:
- features: bfloat16 [8, 16, 128, 1024], P('vrow', None, 'img'), may hold values from -6 to 6
- weight_h: bfloat16 [64, 64, 3, 3], replicated, may hold values from -0.25 to 0.25
- weight_v: bfloat16 [64, 64, 3, 3], replicated, may hold values from -0.25 to 0.25
- beta_h: float32 [5, 64], replicated, may hold values from 0.2 to 1
- beta_v: float32 [5, 64], replicated, may hold values from 0.2 to 1
- shear_set: int32 [5], replicated, may hold values from -2 to 2
- cotangent: bfloat16 [16, 128, 8192], P('vrow', 'img'), may hold values from -6 to 6
Outputs:
- output: bfloat16 [16, 128, 8192], P('vrow', 'img')
- grad_features: bfloat16 [8, 16, 128, 1024], P('vrow', None, 'img')
- grad_weight_h: float32 [64, 64, 3, 3], replicated
- grad_weight_v: float32 [64, 64, 3, 3], replicated
- grad_beta_h: float32 [5, 64], replicated
- grad_beta_v: float32 [5, 64], replicated
The draws below stay inside these ranges and needn't reach their ends.
All inputs are finite; a program needn't handle non-finite values.
Results may differ from the reference program's by a relative error of at most 0.0057.
Values may be sent and summed in bfloat16 or wider, within the bound.
No kernel may reach another device: no remote copies, remote signals or barrier semaphores. Data moves between devices by JAX's collectives and lax.ppermute only.
A program may use at most 128 MiB of HBM per device.

```python
import jax
import jax.numpy as jnp
from jax import lax

C = 64
SHEARS = 5
SHIFT_MAX = 2
Y = 16
U = 8
V = 16
X = 128


def with_ends(values, key, least, top_value):
    extent = values.shape
    place = [jax.random.randint(jax.random.fold_in(key, axis), (), 0, extent[axis]) for axis in range(len(extent))]
    values = values.at[tuple(place)].set(least)
    longest = extent.index(max(extent))
    place[longest] = (place[longest] + 1) % extent[longest]
    return values.at[tuple(place)].set(top_value)


def steps_of(rng, shape, shards, smallest, high):
    factor_of, own = 1.0, jax.random.fold_in(rng, 6)
    for dim, parts in shards:
        steps = jnp.exp(jax.random.uniform(jax.random.fold_in(own, dim), (parts,), jnp.float32, smallest / len(shards), high / len(shards)))
        factor_of = factor_of * jnp.repeat(steps, shape[dim] // parts).reshape([-1 if axis == dim else 1 for axis in range(len(shape))])
    return factor_of


def gaussian(own_key, shape, scale, most, shards=(), held_as=jnp.bfloat16):
    factor_of = steps_of(own_key, shape, shards, -0.22, 0.18) if shards else 1.0
    values = jax.random.normal(own_key, shape, jnp.float32) * scale * factor_of
    return jnp.minimum(jnp.maximum(values, -most), most).astype(held_as)


def setup_inputs(seed: int = 0) -> dict:
    splits = jax.random.split(jax.random.key(seed), 8)
    features = gaussian(splits[0], (U, Y, X, V * C), 1.0, 6.0, ((0, 8), (2, 16)))
    weight_h = gaussian(splits[1], (C, C, 3, 3), (9 * C) ** -0.5, 0.25)
    weight_v = gaussian(splits[2], (C, C, 3, 3), (9 * C) ** -0.5, 0.25)
    beta_h = jnp.clip(jax.random.uniform(splits[3], (SHEARS, C), jnp.float32, 0.2, 1.0), 0.2, 1.0)
    beta_v = jnp.clip(jax.random.uniform(splits[4], (SHEARS, C), jnp.float32, 0.2, 1.0), 0.2, 1.0)
    shear_set = with_ends(jax.random.randint(splits[5], (SHEARS,), -SHIFT_MAX, SHIFT_MAX + 1), jax.random.fold_in(splits[5], 1), -SHIFT_MAX, SHIFT_MAX).astype(jnp.int32)
    cotangent = gaussian(splits[6], (V, X, U * Y * C), 1.0, 6.0, ((0, 8), (1, 16)))
    return {"features": features, "weight_h": weight_h, "weight_v": weight_v, "beta_h": beta_h, "beta_v": beta_v, "shear_set": shear_set, "cotangent": cotangent}


def shear(source, amounts):
    columns = source.shape[3]
    target = jnp.arange(columns, dtype=jnp.int32)[None, :] + amounts[:, None]
    inside = (target >= 0) & (target < columns)
    target = jnp.clip(target, 0, columns - 1).astype(jnp.int32)
    picked = jnp.take_along_axis(source, jnp.broadcast_to(target[None, None], source.shape), axis=3)
    return picked * inside[None, None].astype(source.dtype)


def conv_forward(source, kernel):
    return lax.conv_general_dilated(source.astype(jnp.float32), kernel.astype(jnp.float32), (1, 1), ((1, 1), (1, 1)), dimension_numbers=("NCHW", "OIHW", "NCHW"), precision=lax.Precision.HIGHEST)


def conv_inputs(grads, kernel):
    return lax.conv_general_dilated(grads.astype(jnp.float32), kernel.astype(jnp.float32)[:, :, ::-1, ::-1], (1, 1), ((1, 1), (1, 1)), dimension_numbers=("NCHW", "IOHW", "NCHW"), precision=lax.Precision.HIGHEST)


def conv_kernel(grads, source):
    result = lax.conv_general_dilated(source.astype(jnp.float32), grads.astype(jnp.float32), (1, 1), ((1, 1), (1, 1)), dimension_numbers=("CNHW", "IOHW", "NCHW"), precision=lax.Precision.HIGHEST)
    return jnp.transpose(result, (1, 0, 2, 3))


def offsets_of(count):
    return jnp.arange(count, dtype=jnp.int32) - count // 2


def epi_forward(source, kernel, blend, shear_set):
    offsets = offsets_of(source.shape[2])
    branch = jnp.zeros(source.shape, jnp.float32)
    for shear_idx in range(SHEARS):
        amounts = (shear_set[shear_idx] * offsets).astype(jnp.int32)
        sheared = shear(source, amounts)
        preact = conv_forward(sheared, kernel)
        branch = branch + blend[shear_idx][None, :, None, None] * shear(jax.nn.silu(preact), -amounts)
    return (source.astype(jnp.float32) + branch).astype(jnp.bfloat16)


def epi_backward(source, kernel, blend, shear_set, grads):
    offsets = offsets_of(source.shape[2])
    total = grads
    kernel_grad = jnp.zeros((C, C, 3, 3), jnp.float32)
    blend_rows = []
    for shear_idx in range(SHEARS):
        amounts = (shear_set[shear_idx] * offsets).astype(jnp.int32)
        sheared = shear(source, amounts)
        preact = conv_forward(sheared, kernel)
        blend_rows.append(jnp.sum(grads * shear(jax.nn.silu(preact), -amounts), axis=(0, 2, 3)))
        sigma = jax.nn.sigmoid(preact)
        slope = sigma * (1.0 + preact * (1.0 - sigma))
        dpre = (shear(blend[shear_idx][None, :, None, None] * grads, amounts) * slope).astype(jnp.bfloat16)
        kernel_grad = kernel_grad + conv_kernel(dpre, sheared)
        total = total + shear(conv_inputs(dpre, kernel), -amounts)
    return total.astype(jnp.bfloat16), kernel_grad, jnp.stack(blend_rows)


def reference(features, weight_h, weight_v, beta_h, beta_v, shear_set, cotangent):
    u_all, y_all, x_all, merged = features.shape
    channels = weight_h.shape[0]
    v_all = merged // channels
    layout = jnp.transpose(features.reshape(u_all, y_all, x_all, v_all, channels), (0, 1, 4, 3, 2))
    rows_flat = layout.reshape(u_all * y_all, channels, v_all, x_all)
    hfeat = epi_forward(rows_flat, weight_h, beta_h, shear_set)
    vert_in = jnp.transpose(hfeat.reshape(u_all, y_all, channels, v_all, x_all), (3, 4, 2, 0, 1)).reshape(v_all * x_all, channels, u_all, y_all)
    vout = epi_forward(vert_in, weight_v, beta_v, shear_set)
    output = jnp.transpose(vout.reshape(v_all, x_all, channels, u_all, y_all), (0, 1, 3, 4, 2)).reshape(v_all, x_all, u_all * y_all * channels)
    grad_v = jnp.transpose(cotangent.reshape(v_all, x_all, u_all, y_all, channels), (0, 1, 4, 2, 3)).reshape(v_all * x_all, channels, u_all, y_all).astype(jnp.float32)
    dvert, raw_weight_v, raw_beta_v = epi_backward(vert_in, weight_v, beta_v, shear_set, grad_v)
    grad_h = jnp.transpose(dvert.reshape(v_all, x_all, channels, u_all, y_all), (3, 4, 2, 0, 1)).reshape(u_all * y_all, channels, v_all, x_all).astype(jnp.float32)
    dhor, raw_weight_h, raw_beta_h = epi_backward(rows_flat, weight_h, beta_h, shear_set, grad_h)
    grad_features = jnp.transpose(dhor.reshape(u_all, y_all, channels, v_all, x_all), (0, 1, 4, 3, 2)).reshape(u_all, y_all, x_all, v_all * channels)
    factor = float(u_all * v_all * y_all * x_all) ** -0.5
    return output, grad_features, raw_weight_h * factor, raw_weight_v * factor, raw_beta_h * factor, raw_beta_v * factor
```

```python
import jax
import jax.numpy as jnp
from jax import lax
from jax.experimental import pallas as pl
from jax.experimental.pallas import tpu as pltpu
from jax.sharding import PartitionSpec as P

BF = jnp.bfloat16
F32 = jnp.float32
LANES = 128
HALF = 64
TAPS = 9
REACH = 3
VMEM_BYTES = 60 * 1024 * 1024
NT = (((1,), (1,)), ((), ()))
NN = (((1,), (0,)), ((), ()))
TN = (((0,), (0,)), ((), ()))


def mm(lhs, rhs, dims):
    return lax.dot_general(lhs, rhs, dims, preferred_element_type=F32)


def lanes_of(shape):
    return lax.broadcasted_iota(jnp.int32, shape, len(shape) - 1)


def swap(value):
    return pltpu.roll(value, HALF, axis=value.ndim - 1)


def low(shape):
    return lanes_of(shape) < HALF


def sigmoid(value):
    return 0.5 * jnp.tanh(0.5 * value) + 0.5


def fill_weights(w_ref, wt_ref):
    zero = jnp.zeros((HALF, HALF), BF)
    for tap in range(TAPS):
        w = w_ref[tap]
        wt_ref[pl.ds(tap * LANES, HALF), :] = jnp.concatenate([w, zero], axis=1)
        wt_ref[pl.ds(tap * LANES + HALF, HALF), :] = jnp.concatenate([zero, w], axis=1)


def pack_grads(blocks, blend_ref, pay_ref):
    first = low((HALF, LANES))
    rows = lax.broadcasted_iota(jnp.int32, (HALF, LANES), 0)
    blend = jnp.zeros((HALF, LANES), F32)
    for k in range(blend_ref.shape[0]):
        line = jnp.sum(blend_ref[k], axis=0, keepdims=True)
        line = line + swap(line)
        blend = blend + jnp.where(rows == k, line, 0.0)
    for pair in range(5):
        even = blocks[2 * pair]
        left = even[:HALF] + swap(even[HALF:])
        if pair < 4:
            odd = blocks[2 * pair + 1]
            right = swap(odd[:HALF]) + odd[HALF:]
        else:
            right = blend
        pay_ref[pl.ds(pair * HALF, HALF), :] = jnp.where(first, left, right)


def h_forward(shear, base, beta, w_ref, fl, fm, fr, hfeat, pre_ref, f0_out, fm_out, fp_out, stage, f0, fmi, fpl, taps, wt):
    shears = shear.shape[0]
    fill_weights(w_ref, wt)
    first16 = low((16, LANES))

    @pl.loop(0, 16)
    def _(y):
        for part, ref in enumerate((fl, fm, fr)):
            for q in range(8):
                stage[q, pl.ds(y * 24 + 8 * part, 8), :] = ref[y, :, pl.ds(q * LANES, LANES)].astype(F32)

    @pl.loop(0, 20)
    def _(x):
        own = [stage[q, pl.ds(x + 2, 16, stride=24), :] for q in range(8)]
        turned = [swap(a) for a in own]
        zero = jnp.zeros((16, LANES), F32)
        moved = [
            jnp.where(first16, turned[q - 1] if q > 0 else zero, turned[q] if q < 8 else zero).astype(BF)
            for q in range(9)
        ]
        for q in range(8):
            at = pl.ds(x * LANES + q * 16, 16)
            f0[at, :] = own[q].astype(BF)
            fmi[at, :] = moved[q]
            fpl[at, :] = moved[q + 1]
        at = pl.ds(pl.multiple_of(x * LANES, LANES), LANES)
        for side, ref in enumerate((fmi, f0, fpl)):
            product = mm(ref[at, :], wt[pl.ds(side * 384, 384), :], NT)
            for j in range(3):
                taps[3 * side + j, x] = product[:, j * LANES : (j + 1) * LANES]

    f0_out[...] = f0[pl.ds(6 * LANES, 1024), :]
    fm_out[...] = fmi[pl.ds(6 * LANES, 1024), :]
    fp_out[...] = fpl[pl.ds(6 * LANES, 1024), :]

    half = (lanes_of((16, LANES)) >= HALF).astype(jnp.int32)

    def body(xe, q, local):
        rows = pl.ds(pl.multiple_of(q * 16, 16), 16)
        center = xe + 3
        vrel = half + (2 * q - 8)
        xg = base[0] + xe - REACH
        mid = taps[4, center, rows, :]
        left = taps[3, center - 1, rows, :]
        right = taps[5, center + 1, rows, :]
        branch = jnp.zeros((16, LANES), F32)
        for k in range(shears):
            d = shear[k]
            xs = xg - d * vrel
            a, b = center - d, center + d
            main = mid + taps[1, a, rows, :] + taps[7, b, rows, :]
            minus = left + taps[0, a - 1, rows, :] + taps[6, b - 1, rows, :]
            plus = right + taps[2, a + 1, rows, :] + taps[8, b + 1, rows, :]
            pre = main + jnp.where(xs >= 1, minus, 0.0) + jnp.where(xs <= LANES - 2, plus, 0.0)
            pre_ref[k, xe, q] = pre
            if local:
                keep = (xs >= 0) & (xs < LANES)
                branch = branch + beta[pl.ds(k, 1), :] * jnp.where(keep, pre * sigmoid(pre), 0.0)
        if local:
            own = f0[pl.ds(pl.multiple_of(center * LANES + q * 16, 16), 16), :].astype(F32)
            hfeat[q, xe - REACH] = (own + branch).astype(BF)

    @pl.loop(0, 64)
    def _(n):
        body(n // 8 + REACH, n % 8, True)

    @pl.loop(0, 48)
    def _(n):
        xe = n // 8
        body(jnp.where(xe < REACH, xe, xe + 8), n % 8, False)


def h_backward(shear, base, beta, w_ref, pre_ref, f0, fmi, fpl, gm, gl, gr, out, pay, dps, sums, edges, dfs, stage, blend, wt):
    shears = shear.shape[0]
    fill_weights(w_ref, wt)
    half = (lanes_of((16, LANES)) >= HALF).astype(jnp.int32)
    blend[...] = jnp.zeros(blend.shape, F32)

    def body(xe, q, g, local):
        vrel = half + (2 * q - 8)
        xg = base[0] + xe - REACH
        total = [jnp.zeros((16, LANES), F32) for _ in range(3)]
        for k in range(shears):
            xs = xg - shear[k] * vrel
            pre = pre_ref[k, xe, q]
            s = sigmoid(pre)
            slope = s * (1.0 + pre * (1.0 - s))
            gk = jnp.where((xs >= 0) & (xs < LANES), g, 0.0)
            dp = (beta[pl.ds(k, 1), :] * gk * slope).astype(BF).astype(F32)
            parts = (jnp.where(xs >= 1, dp, 0.0), dp, jnp.where(xs <= LANES - 2, dp, 0.0))
            for j in range(3):
                dps[j, k, xe, q] = parts[j]
                total[j] = total[j] + parts[j]
            if local:
                blend[k] += gk * (pre * s)
        for j in range(3):
            sums[j, xe, q] = total[j]

    @pl.loop(0, 64)
    def _(n):
        x, q = n // 8, n % 8
        body(x + REACH, q, gm[q, x].astype(F32), True)

    @pl.loop(0, 24)
    def _(n):
        x, q = n // 8, n % 8
        body(x, q, gl[q, x].astype(F32), False)
        body(x + 8 + REACH, q, gr[q, x].astype(F32), False)

    @pl.loop(0, 64)
    def _(n):
        x, q = n // 8, n % 8
        xe = x + REACH
        at = pl.ds(pl.multiple_of(n * 16, 16), 16)
        for j in range(3):
            below = jnp.zeros((16, LANES), F32)
            above = jnp.zeros((16, LANES), F32)
            for k in range(shears):
                d = shear[k]
                below = below + dps[j, k, xe + d - (j - 1), q]
                above = above + dps[j, k, xe - d - (j - 1), q]
            lanes = pl.ds(j * LANES, LANES)
            edges[0, at, lanes] = below.astype(BF)
            edges[1, at, lanes] = sums[j, xe - (j - 1), q].astype(BF)
            edges[2, at, lanes] = above.astype(BF)

    blocks = []
    for side, ref in enumerate((fmi, f0, fpl)):
        grad = mm(edges[side], ref[...], TN)
        blocks += [grad[j * LANES : (j + 1) * LANES] for j in range(3)]
    pack_grads(blocks, blend, pay)

    @pl.loop(0, 8)
    def _(x):
        at = pl.ds(pl.multiple_of(x * LANES, LANES), LANES)
        for side in range(3):
            dfs[side, at, :] = mm(edges[side, at, :], wt[pl.ds(side * 384, 384), :], NN)

    first16 = low((16, LANES))

    @pl.loop(0, 8)
    def _(x):
        def piece(side, q):
            if q < 0 or q > 7:
                return jnp.zeros((16, LANES), F32)
            return dfs[side, pl.ds(x * LANES + q * 16, 16), :]

        for q in range(8):
            upper = piece(0, q) + piece(2, q - 1)
            lower = piece(0, q + 1) + piece(2, q)
            turned = swap(jnp.where(first16, lower, upper))
            total = gm[q, x].astype(F32) + piece(1, q) + turned
            stage[q, pl.ds(x * 16, 16), :] = total

    @pl.loop(0, 16)
    def _(y):
        for q in range(8):
            out[y, :, pl.ds(q * LANES, LANES)] = stage[q, pl.ds(y, 8, stride=16), :].astype(BF)


def v_both(shear, beta, w_ref, h_ref, cot, out, dvert, pay, own, fv, taps, dps, sums, grads, outs, edges, blend, wt):
    shears = shear.shape[0]
    fill_weights(w_ref, wt)
    blend[...] = jnp.zeros(blend.shape, F32)
    first8 = low((8, LANES))

    for tap in range(TAPS):
        for u in (0, 9):
            taps[tap, u] = jnp.zeros((22, 8, LANES), F32)

    @pl.loop(0, 10)
    def _(u):
        rim = jnp.zeros((REACH, 8, LANES), F32)
        for tap in range(TAPS):
            taps[tap, u, pl.ds(0, REACH)] = rim
            taps[tap, u, pl.ds(16 + REACH, REACH)] = rim
        for j in range(3):
            sums[j, u, pl.ds(0, REACH)] = rim
            sums[j, u, pl.ds(16 + REACH, REACH)] = rim
            for k in range(shears):
                dps[j, k, u, pl.ds(0, REACH)] = rim
                dps[j, k, u, pl.ds(16 + REACH, REACH)] = rim

    for j in range(3):
        for k in range(shears):
            for u in (0, 9):
                dps[j, k, u] = jnp.zeros((22, 8, LANES), F32)

    @pl.loop(0, 8)
    def _(u):
        for x in range(8):
            own[u, pl.ds(x * 16, 16), :] = h_ref[u, x].astype(F32)
        for y in range(0, 16, 2):
            pair = [own[u, pl.ds(y + e, 8, stride=16), :] for e in range(2)]
            fv[pl.ds(pl.multiple_of(u * LANES + y * 8, 16), 16), :] = jnp.concatenate(pair, axis=0).astype(BF)
        rows = pl.ds(pl.multiple_of(u * LANES, LANES), LANES)
        for side in range(3):
            product = mm(fv[rows, :], wt[pl.ds(side * 384, 384), :], NT)
            for j in range(3):
                taps[3 * side + j, u + 1, pl.ds(REACH, 16)] = product[:, j * LANES : (j + 1) * LANES].reshape(16, 8, LANES)
        for q in range(8):
            lanes = pl.ds(pl.multiple_of((u * 8 + q) * LANES, LANES), LANES)
            a, b = cot[0, :, lanes].astype(F32), cot[1, :, lanes].astype(F32)
            grads[u, 2 * q] = jnp.where(first8, a, swap(b))
            grads[u, 2 * q + 1] = jnp.where(first8, swap(a), b)

    def body(u, y):
        up, yp = u + 1, y + REACH
        g = grads[u, y]
        mid = taps[4, up, yp]
        left = taps[3, up, yp - 1]
        right = taps[5, up, yp + 1]
        branch = jnp.zeros((8, LANES), F32)
        total = [jnp.zeros((8, LANES), F32) for _ in range(3)]
        for k in range(shears):
            d = shear[k]
            ys = y - d * (u - 4)
            keep = ((ys >= 0) & (ys < 16)).astype(F32)
            has_minus = (ys >= 1).astype(F32)
            has_plus = (ys <= 14).astype(F32)
            a, b = yp - d, yp + d
            main = mid + taps[1, u, a] + taps[7, up + 1, b]
            minus = left + taps[0, u, a - 1] + taps[6, up + 1, b - 1]
            plus = right + taps[2, u, a + 1] + taps[8, up + 1, b + 1]
            pre = main + has_minus * minus + has_plus * plus
            s = sigmoid(pre)
            act = keep * (pre * s)
            slope = s * (1.0 + pre * (1.0 - s))
            bk = beta[pl.ds(k, 1), :]
            branch = branch + bk * act
            blend[k] += g * act
            dp = (bk * (keep * g) * slope).astype(BF).astype(F32)
            parts = (has_minus * dp, dp, has_plus * dp)
            for j in range(3):
                dps[j, k, up, yp] = parts[j]
                total[j] = total[j] + parts[j]
        for j in range(3):
            sums[j, up, yp] = total[j]
        outs[u, y] = own[u, pl.ds(y, 8, stride=16), :] + branch

    @pl.loop(0, 128)
    def _(n):
        body(n // 16, n % 16)

    @pl.loop(0, 64)
    def _(n):
        u, y = n // 8, (n % 8) * 2
        at = pl.ds(pl.multiple_of(n * 16, 16), 16)
        for j in range(3):
            cells = []
            for e in range(2):
                yp = y + e + REACH
                below = jnp.zeros((8, LANES), F32)
                above = jnp.zeros((8, LANES), F32)
                for k in range(shears):
                    d = shear[k]
                    below = below + dps[j, k, u + 2, yp + d - (j - 1)]
                    above = above + dps[j, k, u, yp - d - (j - 1)]
                cells.append((below, sums[j, u + 1, yp - (j - 1)], above))
            for side in range(3):
                value = jnp.concatenate([cells[0][side], cells[1][side]], axis=0)
                edges[at, pl.ds((3 * side + j) * LANES, LANES)] = value.astype(BF)

    blocks = []
    for side in range(3):
        grad = mm(edges[:, pl.ds(side * 384, 384)], fv[...], TN)
        blocks += [grad[j * LANES : (j + 1) * LANES] for j in range(3)]
    pack_grads(blocks, blend, pay)

    @pl.loop(0, 8)
    def _(u):
        rows = pl.ds(pl.multiple_of(u * LANES, LANES), LANES)
        back = mm(edges[rows, :], wt[...], NN)
        own[u] = grads[u].reshape(LANES, LANES) + back
        for x in range(8):
            dvert[u, x] = own[u, pl.ds(x, 16, stride=8), :].astype(BF)
        for q in range(8):
            lanes = pl.ds(pl.multiple_of((u * 8 + q) * LANES, LANES), LANES)
            a, b = outs[u, 2 * q], outs[u, 2 * q + 1]
            out[0, :, lanes] = jnp.where(first8, a, swap(b)).astype(BF)
            out[1, :, lanes] = jnp.where(first8, swap(a), b).astype(BF)


def call(body, operands, out_shapes, scratch, smem, cost):
    vmem = pl.BlockSpec(memory_space=pltpu.VMEM)
    specs = [pl.BlockSpec(memory_space=pltpu.SMEM)] * smem + [vmem] * (len(operands) - smem)
    return pl.pallas_call(
        body,
        out_shape=out_shapes,
        in_specs=specs,
        out_specs=[vmem] * len(out_shapes),
        scratch_shapes=scratch,
        compiler_params=pltpu.CompilerParams(vmem_limit_bytes=VMEM_BYTES),
        cost_estimate=pl.CostEstimate(flops=cost, bytes_accessed=4_000_000, transcendentals=1_000_000),
    )(*operands)


def reduce_all(pay):
    part = lax.all_to_all(pay.reshape(16, 40, LANES), "img", 0, 0, tiled=True).sum(0)
    part = lax.all_to_all(part.reshape(8, 5, LANES), "vrow", 0, 0, tiled=True).sum(0)
    part = lax.all_to_all(jnp.broadcast_to(part[None], (8, 5, LANES)), "vrow", 0, 0, tiled=True).reshape(40, LANES)
    return lax.all_to_all(jnp.broadcast_to(part[None], (16, 40, LANES)), "img", 0, 0, tiled=True).reshape(640, LANES)


def per_device(features, weight_h, weight_v, beta_h, beta_v, shear_set, cotangent):
    shears = shear_set.shape[0]
    img = lax.axis_size("img")
    sds = jax.ShapeDtypeStruct
    own = features.reshape(16, 8, 1024)
    to_right = [(i, i + 1) for i in range(img - 1)]
    to_left = [(i + 1, i) for i in range(img - 1)]
    from_left = lax.ppermute(own, "img", to_right)
    from_right = lax.ppermute(own, "img", to_left)
    base = (lax.axis_index("img") * 8).astype(jnp.int32).reshape(1)
    wide_h = jnp.concatenate([beta_h, beta_h], axis=1)
    wide_v = jnp.concatenate([beta_v, beta_v], axis=1)
    w_h = jnp.transpose(weight_h, (2, 3, 0, 1)).reshape(TAPS, HALF, HALF)
    w_v = jnp.transpose(weight_v, (2, 3, 0, 1)).reshape(TAPS, HALF, HALF)

    hfeat, pre, f0, fmi, fpl = call(
        h_forward,
        (shear_set, base, wide_h, w_h, from_left, own, from_right),
        [sds((8, 8, 16, LANES), BF), sds((shears, 14, 8, 16, LANES), F32)] + [sds((1024, LANES), BF)] * 3,
        [pltpu.VMEM((8, 384, LANES), F32)]
        + [pltpu.VMEM((20 * LANES, LANES), BF)] * 3
        + [pltpu.VMEM((TAPS, 20, LANES, LANES), F32), pltpu.VMEM((TAPS * LANES, LANES), BF)],
        2,
        2 * 2560 * LANES * TAPS * LANES,
    )
    moved = lax.all_to_all(hfeat, "vrow", 0, 0, tiled=True)
    output, dvert, pay_v = call(
        v_both,
        (shear_set, wide_v, w_v, moved, cotangent),
        [sds((2, 8, 8192), BF), sds((8, 8, 16, LANES), BF), sds((320, LANES), F32)],
        [
            pltpu.VMEM((8, LANES, LANES), F32),
            pltpu.VMEM((1024, LANES), BF),
            pltpu.VMEM((TAPS, 10, 22, 8, LANES), F32),
            pltpu.VMEM((3, shears, 10, 22, 8, LANES), F32),
            pltpu.VMEM((3, 10, 22, 8, LANES), F32),
            pltpu.VMEM((8, 16, 8, LANES), F32),
            pltpu.VMEM((8, 16, 8, LANES), F32),
            pltpu.VMEM((1024, TAPS * LANES), BF),
            pltpu.VMEM((shears, 8, LANES), F32),
            pltpu.VMEM((TAPS * LANES, LANES), BF),
        ],
        1,
        6 * 1024 * LANES * TAPS * LANES,
    )
    grad = lax.all_to_all(dvert, "vrow", 0, 0, tiled=True)
    grad_right = lax.ppermute(grad[:, :REACH], "img", to_left)
    grad_left = lax.ppermute(grad[:, 8 - REACH :], "img", to_right)
    grad_features, pay_h = call(
        h_backward,
        (shear_set, base, wide_h, w_h, pre, f0, fmi, fpl, grad, grad_left, grad_right),
        [sds((16, 8, 1024), BF), sds((320, LANES), F32)],
        [
            pltpu.VMEM((3, shears, 14, 8, 16, LANES), F32),
            pltpu.VMEM((3, 14, 8, 16, LANES), F32),
            pltpu.VMEM((3, 1024, 384), BF),
            pltpu.VMEM((3, 1024, LANES), F32),
            pltpu.VMEM((8, LANES, LANES), F32),
            pltpu.VMEM((shears, 16, LANES), F32),
            pltpu.VMEM((TAPS * LANES, LANES), BF),
        ],
        2,
        4 * 1024 * LANES * TAPS * LANES,
    )
    total = reduce_all(jnp.concatenate([pay_h, pay_v], axis=0)) * (262144.0**-0.5)

    def unpack(block):
        pairs = jnp.stack([block[:, :HALF].reshape(5, HALF, HALF), block[:, HALF:].reshape(5, HALF, HALF)], axis=1)
        weight = jnp.transpose(pairs.reshape(10, HALF, HALF)[:TAPS].reshape(3, 3, HALF, HALF), (2, 3, 0, 1))
        return weight, block[4 * HALF : 4 * HALF + shears, HALF:]

    weight_grad_h, beta_grad_h = unpack(total[:320])
    weight_grad_v, beta_grad_v = unpack(total[320:])
    return (
        output,
        grad_features.reshape(features.shape),
        weight_grad_h,
        weight_grad_v,
        beta_grad_h,
        beta_grad_v,
    )


def solution(mesh):
    placed = (P("vrow", None, "img", None), P(), P(), P(), P(), P(), P("vrow", "img", None))
    return jax.shard_map(
        per_device,
        mesh=mesh,
        in_specs=placed,
        out_specs=(P("vrow", "img", None), P("vrow", None, "img", None), P(), P(), P(), P()),
        check_vma=False,
    )
```

```python
import jax
import jax.numpy as jnp
from jax import lax
from jax.experimental import pallas as pl
from jax.experimental.pallas import tpu as pltpu
from jax.sharding import PartitionSpec as P

BF = jnp.bfloat16
F32 = jnp.float32
LANES = 128
HALF = 64
TAPS = 9
REACH = 3
VMEM_BYTES = 36 * 1024 * 1024
NT = (((1,), (1,)), ((), ()))
NN = (((1,), (0,)), ((), ()))
TN = (((0,), (0,)), ((), ()))


def mm(lhs, rhs, dims):
    return lax.dot_general(lhs, rhs, dims, preferred_element_type=F32)


def lanes_of(shape):
    return lax.broadcasted_iota(jnp.int32, shape, len(shape) - 1)


def swap(value):
    return pltpu.roll(value, HALF, axis=value.ndim - 1)


def low(shape):
    return lanes_of(shape) < HALF


def fill_weights(w_ref, wt_ref):
    zero = jnp.zeros((HALF, HALF), BF)
    for tap in range(TAPS):
        w = w_ref[tap]
        wt_ref[pl.ds(tap * LANES, HALF), :] = jnp.concatenate([w, zero], axis=1)
        wt_ref[pl.ds(tap * LANES + HALF, HALF), :] = jnp.concatenate([zero, w], axis=1)


def spread(beta_ref, beta):
    for k in range(beta.shape[0]):
        line = beta_ref[pl.ds(k, 1), :]
        beta[k] = jnp.broadcast_to(jnp.concatenate([line, line], axis=1), (8, LANES))


def pack_grads(grads, blend_ref, pay_ref):
    first = low((HALF, LANES))
    rows = lax.broadcasted_iota(jnp.int32, (HALF, LANES), 0)
    blend = jnp.zeros((HALF, LANES), F32)
    for k in range(blend_ref.shape[0]):
        line = jnp.sum(blend_ref[k], axis=0, keepdims=True)
        blend = blend + jnp.where(rows == k, line + swap(line), 0.0)

    def tap_of(tap):
        block = grads[tap // 3][:, (tap % 3) * LANES : (tap % 3 + 1) * LANES]
        return block[:HALF] + swap(block[HALF:])

    for pair in range(5):
        even = tap_of(2 * pair)
        odd = tap_of(2 * pair + 1) if pair < 4 else even
        both = jnp.transpose(jnp.where(first, even, swap(odd)))
        value = jnp.concatenate([both[:HALF], both[HALF:]], axis=1)
        if pair == 4:
            value = jnp.where(first, value, blend)
        pay_ref[pl.ds(pair * HALF, HALF), :] = value


def gate(pre):
    s = 0.5 * jnp.tanh(0.5 * pre) + 0.5
    act = pre * s
    return act, s + act * (1.0 - s)


def halves():
    return (lanes_of((1, 8, LANES)) >= HALF).astype(jnp.int32)


def h_forward(shear, base, beta_ref, w_ref, fl, fm, fr, hfeat, pre_ref, f0_out, fm_out, fp_out, beta, stage, f0, fmi, fpl, taps, wt):
    shears = shear.shape[0]
    spread(beta_ref, beta)
    fill_weights(w_ref, wt)
    first16 = low((16, LANES))

    @pl.loop(0, 16)
    def _(y):
        for part, ref in enumerate((fl, fm, fr)):
            for q in range(8):
                stage[q, pl.ds(y * 24 + 8 * part, 8), :] = ref[y, :, pl.ds(q * LANES, LANES)].astype(F32)

    @pl.loop(0, 20)
    def _(x):
        own = [stage[q, pl.ds(x + 2, 16, stride=24), :] for q in range(8)]
        turned = [swap(a) for a in own]
        zero = jnp.zeros((16, LANES), F32)
        moved = [
            jnp.where(first16, turned[q - 1] if q > 0 else zero, turned[q] if q < 8 else zero).astype(BF)
            for q in range(9)
        ]
        for q in range(8):
            at = pl.ds(pl.multiple_of(x * LANES + q * 16, 16), 16)
            f0[at, :] = own[q].astype(BF)
            fmi[at, :] = moved[q]
            fpl[at, :] = moved[q + 1]

    @pl.loop(0, 5)
    def _(n):
        at = pl.ds(pl.multiple_of(n * 512, 512), 512)
        for side, ref in enumerate((fmi, f0, fpl)):
            product = mm(ref[at, :], wt[pl.ds(side * 384, 384), :], NT)
            for j in range(3):
                part = product[:, j * LANES : (j + 1) * LANES].reshape(32, 2, 8, LANES)
                taps[pl.ds((3 * side + j) * 160 + n * 32, 32)] = part

    f0_out[...] = f0[pl.ds(6 * LANES, 1024), :]
    fm_out[...] = fmi[pl.ds(6 * LANES, 1024), :]
    fp_out[...] = fpl[pl.ds(6 * LANES, 1024), :]

    half = halves()

    def body(xe, q, local):
        here = (xe + 3) * 8 + q
        vrel = half + (2 * q - 8)
        xg = base[0] + xe - REACH
        mid = taps[4 * 160 + here]
        left = taps[3 * 160 - 8 + here]
        right = taps[5 * 160 + 8 + here]
        branch = jnp.zeros((2, 8, LANES), F32)
        for k in range(shears):
            d = shear[k]
            xs = xg - d * vrel
            a, b = here - d * 8, here + d * 8
            main = mid + (taps[160 + a] + taps[7 * 160 + b])
            minus = left + (taps[a - 8] + taps[6 * 160 - 8 + b])
            plus = right + (taps[2 * 160 + 8 + a] + taps[8 * 160 + 8 + b])
            pre = main + jnp.where(xs >= 1, minus, 0.0) + jnp.where(xs <= LANES - 2, plus, 0.0)
            pre_ref[k * 112 + xe * 8 + q] = pre
            if local:
                keep = (xs >= 0) & (xs < LANES)
                branch = branch + jnp.where(keep, beta[k] * gate(pre)[0], 0.0)
        if local:
            own = f0[pl.ds(pl.multiple_of(here * 16, 16), 16), :].astype(F32)
            hfeat[q, xe - REACH] = (own + branch.reshape(16, LANES)).astype(BF)

    @pl.loop(0, 64)
    def _(n):
        body(n // 8 + REACH, n % 8, True)

    @pl.loop(0, 24)
    def _(n):
        body(n // 8, n % 8, False)
        body(n // 8 + 8 + REACH, n % 8, False)


def h_backward(shear, base, beta_ref, w_ref, pre_ref, f0, fmi, fpl, gm, gl, gr, pay_v, out, pay, beta, dps, sums, edges, dfs, stage, blend, wt):
    shears = shear.shape[0]
    step = shears * 112
    spread(beta_ref, beta)
    fill_weights(w_ref, wt)
    half = halves()
    blend[...] = jnp.zeros(blend.shape, F32)

    def body(xe, q, g, local):
        here = xe * 8 + q
        g = g.astype(F32).reshape(2, 8, LANES)
        vrel = half + (2 * q - 8)
        xg = base[0] + xe - REACH
        total = [jnp.zeros((2, 8, LANES), F32) for _ in range(3)]
        for k in range(shears):
            xs = xg - shear[k] * vrel
            act, slope = gate(pre_ref[k * 112 + here])
            gk = jnp.where((xs >= 0) & (xs < LANES), g, 0.0)
            dp = (beta[k] * gk * slope).astype(BF).astype(F32)
            parts = (jnp.where(xs >= 1, dp, 0.0), dp, jnp.where(xs <= LANES - 2, dp, 0.0))
            for j in range(3):
                dps[j * step + k * 112 + here] = parts[j]
                total[j] = total[j] + parts[j]
            if local:
                blend[k] += jnp.sum(gk * act, axis=0)
        for j in range(3):
            sums[j * 112 + here] = total[j]

    @pl.loop(0, 64)
    def _(n):
        x, q = n // 8, n % 8
        body(x + REACH, q, gm[q, x], True)

    @pl.loop(0, 24)
    def _(n):
        x, q = n // 8, n % 8
        body(x, q, gl[q, x], False)
        body(x + 8 + REACH, q, gr[q, x], False)

    @pl.loop(0, 64)
    def _(n):
        here = n + REACH * 8
        at = pl.ds(pl.multiple_of(n * 16, 16), 16)
        below = [jnp.zeros((2, 8, LANES), F32) for _ in range(3)]
        above = [jnp.zeros((2, 8, LANES), F32) for _ in range(3)]
        for k in range(shears):
            d = shear[k]
            up, down = here + d * 8, here - d * 8
            for j in range(3):
                below[j] = below[j] + dps[j * step + k * 112 - (j - 1) * 8 + up]
                above[j] = above[j] + dps[j * step + k * 112 - (j - 1) * 8 + down]
        for j in range(3):
            lanes = pl.ds(j * LANES, LANES)
            edges[0, at, lanes] = below[j].reshape(16, LANES).astype(BF)
            edges[1, at, lanes] = sums[j * 112 - (j - 1) * 8 + here].reshape(16, LANES).astype(BF)
            edges[2, at, lanes] = above[j].reshape(16, LANES).astype(BF)

    pack_grads([mm(ref[...], edges[side], TN) for side, ref in enumerate((fmi, f0, fpl))], blend, pay)
    pay[pl.ds(5 * HALF, 5 * HALF), :] = pay_v[...]

    @pl.loop(0, 4)
    def _(x):
        at = pl.ds(pl.multiple_of(x * 256, 256), 256)
        for side in range(3):
            dfs[side, at, :] = mm(edges[side, at, :], wt[pl.ds(side * 384, 384), :], NN)

    first16 = low((16, LANES))

    @pl.loop(0, 8)
    def _(x):
        def piece(side, q):
            if q < 0 or q > 7:
                return jnp.zeros((16, LANES), F32)
            return dfs[side, pl.ds(pl.multiple_of(x * LANES + q * 16, 16), 16), :]

        for q in range(8):
            upper = piece(0, q) + piece(2, q - 1)
            lower = piece(0, q + 1) + piece(2, q)
            turned = swap(jnp.where(first16, lower, upper))
            total = gm[q, x].astype(F32) + piece(1, q) + turned
            stage[q, pl.ds(x * 16, 16), :] = total

    @pl.loop(0, 16)
    def _(y):
        for q in range(8):
            out[y, :, pl.ds(q * LANES, LANES)] = stage[q, pl.ds(y, 8, stride=16), :].astype(BF)


def v_both(shear, beta_ref, w_ref, h_ref, cot, out, dvert, pay, beta, own, fv, taps, dps, sums, grads, outs, edges, blend, wt):
    shears = shear.shape[0]
    wide = 22
    plane = 10 * wide
    spread(beta_ref, beta)
    fill_weights(w_ref, wt)
    blend[...] = jnp.zeros(blend.shape, F32)
    first8 = low((8, LANES))

    for u in (0, 9):
        sheet = jnp.zeros((wide, 8, LANES), F32)
        for tap in (0, 1, 2) if u == 0 else (6, 7, 8):
            taps[pl.ds(tap * plane + u * wide, wide)] = sheet
        for jk in range(3 * shears):
            dps[pl.ds(jk * plane + u * wide, wide)] = sheet

    @pl.loop(1, 9)
    def _(u):
        rim = jnp.zeros((REACH, 8, LANES), F32)
        for side in (0, 16 + REACH):
            for tap in range(TAPS):
                taps[pl.ds(tap * plane + side + u * wide, REACH)] = rim
            for j in range(3):
                sums[pl.ds(j * plane + side + u * wide, REACH)] = rim
            for jk in range(3 * shears):
                dps[pl.ds(jk * plane + side + u * wide, REACH)] = rim

    @pl.loop(0, 8)
    def _(u):
        for x in range(8):
            own[u, pl.ds(x * 16, 16), :] = h_ref[u, x].astype(F32)
        for y in range(0, 16, 2):
            pair = [own[u, pl.ds(y + e, 8, stride=16), :] for e in range(2)]
            fv[pl.ds(pl.multiple_of(u * LANES + y * 8, 16), 16), :] = jnp.concatenate(pair, axis=0).astype(BF)
        for q in range(8):
            lanes = pl.ds(pl.multiple_of((u * 8 + q) * LANES, LANES), LANES)
            a, b = cot[0, :, lanes].astype(F32), cot[1, :, lanes].astype(F32)
            grads[u, 2 * q] = jnp.where(first8, a, swap(b))
            grads[u, 2 * q + 1] = jnp.where(first8, swap(a), b)

    @pl.loop(0, 2)
    def _(n):
        rows = pl.ds(pl.multiple_of(n * 512, 512), 512)
        for side in range(3):
            product = mm(fv[rows, :], wt[pl.ds(side * 384, 384), :], NT)
            for j in range(3):
                part = product[:, j * LANES : (j + 1) * LANES].reshape(4, 16, 8, LANES)
                for e in range(4):
                    taps[pl.ds((3 * side + j) * plane + (e + 1) * wide + REACH + n * 4 * wide, 16)] = part[e]

    def body(u, y):
        here = (u + 1) * wide + REACH + y
        g = grads[u, y]
        mid = taps[4 * plane + here]
        left = taps[3 * plane - 1 + here]
        right = taps[5 * plane + 1 + here]
        branch = jnp.zeros((8, LANES), F32)
        total = [jnp.zeros((8, LANES), F32) for _ in range(3)]
        shared = []
        for k in range(shears):
            d = shear[k]
            ys = y - d * (u - 4)
            keep = ((ys >= 0) & (ys < 16)).astype(F32)
            has_minus = (ys >= 1).astype(F32)
            has_plus = (ys <= 14).astype(F32)
            a, b = here - d, here + d
            main = mid + (taps[plane - wide + a] + taps[7 * plane + wide + b])
            minus = left + (taps[-wide - 1 + a] + taps[6 * plane + wide - 1 + b])
            plus = right + (taps[2 * plane - wide + 1 + a] + taps[8 * plane + wide + 1 + b])
            act, slope = gate(main + has_minus * minus + has_plus * plus)
            act = keep * act
            bk = beta[k]
            branch = branch + bk * act
            shared.append(g * act)
            dp = (bk * (keep * g) * slope).astype(BF).astype(F32)
            parts = (has_minus * dp, dp, has_plus * dp)
            for j in range(3):
                dps[(j * shears + k) * plane + here] = parts[j]
                total[j] = total[j] + parts[j]
        for j in range(3):
            sums[j * plane + here] = total[j]
        outs[u, y] = own[u, pl.ds(y, 8, stride=16), :] + branch
        return shared

    @pl.loop(0, 64)
    def _(n):
        u, y = n // 8, (n % 8) * 2
        first, second = body(u, y), body(u, y + 1)
        for k in range(shears):
            blend[k] += first[k] + second[k]

    @pl.loop(0, 64)
    def _(n):
        here = (n // 8 + 1) * wide + REACH + (n % 8) * 2
        at = pl.ds(pl.multiple_of(n * 16, 16), 16)
        below = [jnp.zeros((2, 8, LANES), F32) for _ in range(3)]
        above = [jnp.zeros((2, 8, LANES), F32) for _ in range(3)]
        for k in range(shears):
            d = shear[k]
            up, down = here + d, here - d
            for j in range(3):
                offset = (j * shears + k) * plane - (j - 1)
                below[j] = below[j] + dps[pl.ds(offset + wide + up, 2)]
                above[j] = above[j] + dps[pl.ds(offset - wide + down, 2)]
        for j in range(3):
            middle = sums[pl.ds(j * plane - (j - 1) + here, 2)]
            for side, value in enumerate((below[j], middle, above[j])):
                edges[at, pl.ds((3 * side + j) * LANES, LANES)] = value.reshape(16, LANES).astype(BF)

    pack_grads([mm(fv[...], edges[:, pl.ds(side * 384, 384)], TN) for side in range(3)], blend, pay)

    @pl.loop(0, 4)
    def _(n):
        rows = pl.ds(pl.multiple_of(n * 256, 256), 256)
        back = mm(edges[rows, :], wt[...], NN).reshape(2, LANES, LANES)
        for e in range(2):
            u = 2 * n + e
            own[u] = grads[u].reshape(LANES, LANES) + back[e]
            for x in range(8):
                dvert[u, x] = own[u, pl.ds(x, 16, stride=8), :].astype(BF)
            for q in range(8):
                lanes = pl.ds(pl.multiple_of((u * 8 + q) * LANES, LANES), LANES)
                a, b = outs[u, 2 * q], outs[u, 2 * q + 1]
                out[0, :, lanes] = jnp.where(first8, a, swap(b)).astype(BF)
                out[1, :, lanes] = jnp.where(first8, swap(a), b).astype(BF)


def call(body, operands, out_shapes, scratch, smem, cost):
    vmem = pl.BlockSpec(memory_space=pltpu.VMEM)
    specs = [pl.BlockSpec(memory_space=pltpu.SMEM)] * smem + [vmem] * (len(operands) - smem)
    return pl.pallas_call(
        body,
        out_shape=out_shapes,
        in_specs=specs,
        out_specs=[vmem] * len(out_shapes),
        scratch_shapes=scratch,
        compiler_params=pltpu.CompilerParams(vmem_limit_bytes=VMEM_BYTES),
        cost_estimate=pl.CostEstimate(flops=cost, bytes_accessed=4_000_000, transcendentals=1_000_000),
    )(*operands)


def reduce_all(pay):
    part = lax.all_to_all(pay.reshape(16, 40, LANES), "img", 0, 0, tiled=True).sum(0)
    part = lax.all_to_all(jnp.broadcast_to(part[None], (8, 40, LANES)), "vrow", 0, 0, tiled=True).sum(0)
    return lax.all_to_all(jnp.broadcast_to(part[None], (16, 40, LANES)), "img", 0, 0, tiled=True).reshape(640, LANES)


def per_device(features, weight_h, weight_v, beta_h, beta_v, shear_set, cotangent):
    shears = shear_set.shape[0]
    img = lax.axis_size("img")
    sds = jax.ShapeDtypeStruct
    own = features.reshape(16, 8, 1024)
    to_right = [(i, i + 1) for i in range(img - 1)]
    to_left = [(i + 1, i) for i in range(img - 1)]
    from_left = lax.ppermute(own, "img", to_right)
    from_right = lax.ppermute(own, "img", to_left)
    base = (lax.axis_index("img") * 8).astype(jnp.int32).reshape(1)
    w_h = jnp.transpose(weight_h, (2, 3, 0, 1)).reshape(TAPS, HALF, HALF)
    w_v = jnp.transpose(weight_v, (2, 3, 0, 1)).reshape(TAPS, HALF, HALF)

    hfeat, pre, f0, fmi, fpl = call(
        h_forward,
        (shear_set, base, beta_h, w_h, from_left, own, from_right),
        [sds((8, 8, 16, LANES), BF), sds((shears * 112, 2, 8, LANES), F32)] + [sds((1024, LANES), BF)] * 3,
        [pltpu.VMEM((shears, 8, LANES), F32), pltpu.VMEM((8, 384, LANES), F32)]
        + [pltpu.VMEM((20 * LANES, LANES), BF)] * 3
        + [pltpu.VMEM((TAPS * 160, 2, 8, LANES), F32), pltpu.VMEM((TAPS * LANES, LANES), BF)],
        2,
        2 * 2560 * LANES * TAPS * LANES,
    )
    moved = lax.all_to_all(hfeat, "vrow", 0, 0, tiled=True)
    output, dvert, pay_v = call(
        v_both,
        (shear_set, beta_v, w_v, moved, cotangent),
        [sds((2, 8, 8192), BF), sds((8, 8, 16, LANES), BF), sds((320, LANES), F32)],
        [
            pltpu.VMEM((shears, 8, LANES), F32),
            pltpu.VMEM((8, LANES, LANES), F32),
            pltpu.VMEM((1024, LANES), BF),
            pltpu.VMEM((TAPS * 220, 8, LANES), F32),
            pltpu.VMEM((3 * shears * 220, 8, LANES), F32),
            pltpu.VMEM((3 * 220, 8, LANES), F32),
            pltpu.VMEM((8, 16, 8, LANES), F32),
            pltpu.VMEM((8, 16, 8, LANES), F32),
            pltpu.VMEM((1024, TAPS * LANES), BF),
            pltpu.VMEM((shears, 8, LANES), F32),
            pltpu.VMEM((TAPS * LANES, LANES), BF),
        ],
        1,
        6 * 1024 * LANES * TAPS * LANES,
    )
    grad = lax.all_to_all(dvert, "vrow", 0, 0, tiled=True)
    grad_right = lax.ppermute(grad[:, :REACH], "img", to_left)
    grad_left = lax.ppermute(grad[:, 8 - REACH :], "img", to_right)
    grad_features, pay = call(
        h_backward,
        (shear_set, base, beta_h, w_h, pre, f0, fmi, fpl, grad, grad_left, grad_right, pay_v),
        [sds((16, 8, 1024), BF), sds((640, LANES), F32)],
        [
            pltpu.VMEM((shears, 8, LANES), F32),
            pltpu.VMEM((3 * shears * 112, 2, 8, LANES), F32),
            pltpu.VMEM((3 * 112, 2, 8, LANES), F32),
            pltpu.VMEM((3, 1024, 384), BF),
            pltpu.VMEM((3, 1024, LANES), F32),
            pltpu.VMEM((8, LANES, LANES), F32),
            pltpu.VMEM((shears, 8, LANES), F32),
            pltpu.VMEM((TAPS * LANES, LANES), BF),
        ],
        2,
        4 * 1024 * LANES * TAPS * LANES,
    )
    total = reduce_all(pay) * (262144.0**-0.5)

    def unpack(block):
        pairs = jnp.stack([block[:, :HALF].reshape(5, HALF, HALF), block[:, HALF:].reshape(5, HALF, HALF)], axis=1)
        weight = jnp.transpose(pairs.reshape(10, HALF, HALF)[:TAPS].reshape(3, 3, HALF, HALF), (2, 3, 0, 1))
        return weight, block[4 * HALF : 4 * HALF + shears, HALF:]

    weight_grad_h, beta_grad_h = unpack(total[:320])
    weight_grad_v, beta_grad_v = unpack(total[320:])
    return (
        output,
        grad_features.reshape(features.shape),
        weight_grad_h,
        weight_grad_v,
        beta_grad_h,
        beta_grad_v,
    )


def solution(mesh):
    placed = (P("vrow", None, "img", None), P(), P(), P(), P(), P(), P("vrow", "img", None))
    return jax.shard_map(
        per_device,
        mesh=mesh,
        in_specs=placed,
        out_specs=(P("vrow", "img", None), P("vrow", None, "img", None), P(), P(), P(), P()),
        check_vma=False,
    )
```

```python
import jax
import jax.numpy as jnp
from jax import lax
from jax.experimental import pallas as pl
from jax.experimental.pallas import tpu as pltpu
from jax.sharding import PartitionSpec as P

BF = jnp.bfloat16
F32 = jnp.float32
LANES = 128
HALF = 64
TAPS = 9
REACH = 3
MIB = 1024 * 1024
GRANT = (36, 36, 36)
NT = (((1,), (1,)), ((), ()))
NN = (((1,), (0,)), ((), ()))
TN = (((0,), (0,)), ((), ()))


def mm(lhs, rhs, dims):
    return lax.dot_general(lhs, rhs, dims, preferred_element_type=F32)


def lanes_of(shape):
    return lax.broadcasted_iota(jnp.int32, shape, len(shape) - 1)


def swap(value):
    return pltpu.roll(value, HALF, axis=value.ndim - 1)


def low(shape):
    return lanes_of(shape) < HALF


def fill_weights(w_ref, wt_ref):
    zero = jnp.zeros((HALF, HALF), BF)
    for tap in range(TAPS):
        w = w_ref[tap]
        wt_ref[pl.ds(tap * LANES, HALF), :] = jnp.concatenate([w, zero], axis=1)
        wt_ref[pl.ds(tap * LANES + HALF, HALF), :] = jnp.concatenate([zero, w], axis=1)


def spread(beta_ref, beta):
    for k in range(beta.shape[0]):
        line = beta_ref[pl.ds(k, 1), :]
        beta[k] = jnp.broadcast_to(jnp.concatenate([line, line], axis=1), (8, LANES))


def pack_grads(grads, blend_ref, pay_ref):
    first = low((HALF, LANES))
    rows = lax.broadcasted_iota(jnp.int32, (HALF, LANES), 0)
    blend = jnp.zeros((HALF, LANES), F32)
    for k in range(blend_ref.shape[0]):
        line = jnp.sum(blend_ref[k], axis=0, keepdims=True)
        blend = blend + jnp.where(rows == k, line + swap(line), 0.0)

    def tap_of(tap):
        block = grads[tap // 3][:, (tap % 3) * LANES : (tap % 3 + 1) * LANES]
        return block[:HALF] + swap(block[HALF:])

    for pair in range(5):
        even = tap_of(2 * pair)
        odd = tap_of(2 * pair + 1) if pair < 4 else even
        both = jnp.transpose(jnp.where(first, even, swap(odd)))
        value = jnp.concatenate([both[:HALF], both[HALF:]], axis=1)
        if pair == 4:
            value = jnp.where(first, value, blend)
        pay_ref[pl.ds(pair * HALF, HALF), :] = value


def gate(pre):
    s = 0.5 * jnp.tanh(0.5 * pre) + 0.5
    act = pre * s
    return act, s + act * (1.0 - s)


def halves():
    return (lanes_of((1, 8, LANES)) >= HALF).astype(jnp.int32)


def h_forward(ready, shear, beta_ref, w_ref, fm, base, fl, fr, hfeat, pre_ref, f0_out, fm_out, fp_out, beta, stage, f0, fmi, fpl, taps, wt):
    shears = shear.shape[0]
    ready()
    spread(beta_ref, beta)
    fill_weights(w_ref, wt)
    first16 = low((16, LANES))

    @pl.loop(0, 16)
    def _(y):
        for part, ref in enumerate((fl, fm, fr)):
            for q in range(8):
                stage[q, pl.ds(y * 24 + 8 * part, 8), :] = ref[y, :, pl.ds(q * LANES, LANES)].astype(F32)

    @pl.loop(0, 20)
    def _(x):
        own = [stage[q, pl.ds(x + 2, 16, stride=24), :] for q in range(8)]
        turned = [swap(a) for a in own]
        zero = jnp.zeros((16, LANES), F32)
        moved = [
            jnp.where(first16, turned[q - 1] if q > 0 else zero, turned[q] if q < 8 else zero).astype(BF)
            for q in range(9)
        ]
        for q in range(8):
            at = pl.ds(pl.multiple_of(x * LANES + q * 16, 16), 16)
            f0[at, :] = own[q].astype(BF)
            fmi[at, :] = moved[q]
            fpl[at, :] = moved[q + 1]

    @pl.loop(0, 5)
    def _(n):
        at = pl.ds(pl.multiple_of(n * 512, 512), 512)
        for side, ref in enumerate((fmi, f0, fpl)):
            product = mm(ref[at, :], wt[pl.ds(side * 384, 384), :], NT)
            for j in range(3):
                part = product[:, j * LANES : (j + 1) * LANES].reshape(32, 2, 8, LANES)
                taps[pl.ds((3 * side + j) * 160 + n * 32, 32)] = part

    f0_out[...] = f0[pl.ds(6 * LANES, 1024), :]
    fm_out[...] = fmi[pl.ds(6 * LANES, 1024), :]
    fp_out[...] = fpl[pl.ds(6 * LANES, 1024), :]

    half = halves()

    def body(xe, q, local):
        here = (xe + 3) * 8 + q
        vrel = half + (2 * q - 8)
        xg = base[0] + xe - REACH
        mid = taps[4 * 160 + here]
        left = taps[3 * 160 - 8 + here]
        right = taps[5 * 160 + 8 + here]
        branch = jnp.zeros((2, 8, LANES), F32)
        for k in range(shears):
            d = shear[k]
            xs = xg - d * vrel
            a, b = here - d * 8, here + d * 8
            main = mid + (taps[160 + a] + taps[7 * 160 + b])
            minus = left + (taps[a - 8] + taps[6 * 160 - 8 + b])
            plus = right + (taps[2 * 160 + 8 + a] + taps[8 * 160 + 8 + b])
            pre = main + jnp.where(xs >= 1, minus, 0.0) + jnp.where(xs <= LANES - 2, plus, 0.0)
            pre_ref[k * 112 + xe * 8 + q] = pre
            if local:
                keep = (xs >= 0) & (xs < LANES)
                branch = branch + jnp.where(keep, beta[k] * gate(pre)[0], 0.0)
        if local:
            own = f0[pl.ds(pl.multiple_of(here * 16, 16), 16), :].astype(F32)
            hfeat[q, xe - REACH] = (own + branch.reshape(16, LANES)).astype(BF)

    @pl.loop(0, 64)
    def _(n):
        body(n // 8 + REACH, n % 8, True)

    @pl.loop(0, 24)
    def _(n):
        body(n // 8, n % 8, False)
        body(n // 8 + 8 + REACH, n % 8, False)


def h_backward(ready, shear, beta_ref, w_ref, base, pre_ref, f0, fmi, fpl, gm, gl, gr, pay_v, out, pay, beta, dps, sums, edges, dfs, stage, blend, wt):
    shears = shear.shape[0]
    step = shears * 112
    ready()
    spread(beta_ref, beta)
    fill_weights(w_ref, wt)
    half = halves()
    blend[...] = jnp.zeros(blend.shape, F32)

    def body(xe, q, g, local):
        here = xe * 8 + q
        g = g.astype(F32).reshape(2, 8, LANES)
        vrel = half + (2 * q - 8)
        xg = base[0] + xe - REACH
        total = [jnp.zeros((2, 8, LANES), F32) for _ in range(3)]
        for k in range(shears):
            xs = xg - shear[k] * vrel
            act, slope = gate(pre_ref[k * 112 + here])
            gk = jnp.where((xs >= 0) & (xs < LANES), g, 0.0)
            dp = (beta[k] * gk * slope).astype(BF).astype(F32)
            parts = (jnp.where(xs >= 1, dp, 0.0), dp, jnp.where(xs <= LANES - 2, dp, 0.0))
            for j in range(3):
                dps[j * step + k * 112 + here] = parts[j]
                total[j] = total[j] + parts[j]
            if local:
                blend[k] += jnp.sum(gk * act, axis=0)
        for j in range(3):
            sums[j * 112 + here] = total[j]

    @pl.loop(0, 64)
    def _(n):
        x, q = n // 8, n % 8
        body(x + REACH, q, gm[q, x], True)

    @pl.loop(0, 24)
    def _(n):
        x, q = n // 8, n % 8
        body(x, q, gl[q, x], False)
        body(x + 8 + REACH, q, gr[q, x], False)

    @pl.loop(0, 64)
    def _(n):
        here = n + REACH * 8
        at = pl.ds(pl.multiple_of(n * 16, 16), 16)
        below = [jnp.zeros((2, 8, LANES), F32) for _ in range(3)]
        above = [jnp.zeros((2, 8, LANES), F32) for _ in range(3)]
        for k in range(shears):
            d = shear[k]
            up, down = here + d * 8, here - d * 8
            for j in range(3):
                below[j] = below[j] + dps[j * step + k * 112 - (j - 1) * 8 + up]
                above[j] = above[j] + dps[j * step + k * 112 - (j - 1) * 8 + down]
        for j in range(3):
            lanes = pl.ds(j * LANES, LANES)
            edges[0, at, lanes] = below[j].reshape(16, LANES).astype(BF)
            edges[1, at, lanes] = sums[j * 112 - (j - 1) * 8 + here].reshape(16, LANES).astype(BF)
            edges[2, at, lanes] = above[j].reshape(16, LANES).astype(BF)

    pack_grads([mm(ref[...], edges[side], TN) for side, ref in enumerate((fmi, f0, fpl))], blend, pay)
    pay[pl.ds(5 * HALF, 5 * HALF), :] = pay_v[...]

    @pl.loop(0, 4)
    def _(x):
        at = pl.ds(pl.multiple_of(x * 256, 256), 256)
        for side in range(3):
            dfs[side, at, :] = mm(edges[side, at, :], wt[pl.ds(side * 384, 384), :], NN)

    first16 = low((16, LANES))

    @pl.loop(0, 8)
    def _(x):
        def piece(side, q):
            if q < 0 or q > 7:
                return jnp.zeros((16, LANES), F32)
            return dfs[side, pl.ds(pl.multiple_of(x * LANES + q * 16, 16), 16), :]

        for q in range(8):
            upper = piece(0, q) + piece(2, q - 1)
            lower = piece(0, q + 1) + piece(2, q)
            turned = swap(jnp.where(first16, lower, upper))
            total = gm[q, x].astype(F32) + piece(1, q) + turned
            stage[q, pl.ds(x * 16, 16), :] = total

    @pl.loop(0, 16)
    def _(y):
        for q in range(8):
            out[y, :, pl.ds(q * LANES, LANES)] = stage[q, pl.ds(y, 8, stride=16), :].astype(BF)


def v_both(ready, shear, beta_ref, w_ref, cot, h_ref, out, dvert, pay, beta, own, fv, taps, dps, sums, grads, outs, edges, blend, wt):
    shears = shear.shape[0]
    wide = 22
    plane = 10 * wide
    blend[...] = jnp.zeros(blend.shape, F32)
    first8 = low((8, LANES))

    for u in (0, 9):
        sheet = jnp.zeros((wide, 8, LANES), F32)
        for tap in (0, 1, 2) if u == 0 else (6, 7, 8):
            taps[pl.ds(tap * plane + u * wide, wide)] = sheet
        for jk in range(3 * shears):
            dps[pl.ds(jk * plane + u * wide, wide)] = sheet

    @pl.loop(1, 9)
    def _(u):
        rim = jnp.zeros((REACH, 8, LANES), F32)
        for side in (0, 16 + REACH):
            for tap in range(TAPS):
                taps[pl.ds(tap * plane + side + u * wide, REACH)] = rim
            for j in range(3):
                sums[pl.ds(j * plane + side + u * wide, REACH)] = rim
            for jk in range(3 * shears):
                dps[pl.ds(jk * plane + side + u * wide, REACH)] = rim

    ready()
    spread(beta_ref, beta)
    fill_weights(w_ref, wt)

    @pl.loop(0, 8)
    def _(u):
        for x in range(8):
            own[u, pl.ds(x * 16, 16), :] = h_ref[u, x].astype(F32)
        for y in range(0, 16, 2):
            pair = [own[u, pl.ds(y + e, 8, stride=16), :] for e in range(2)]
            fv[pl.ds(pl.multiple_of(u * LANES + y * 8, 16), 16), :] = jnp.concatenate(pair, axis=0).astype(BF)
        for q in range(8):
            lanes = pl.ds(pl.multiple_of((u * 8 + q) * LANES, LANES), LANES)
            a, b = cot[0, :, lanes].astype(F32), cot[1, :, lanes].astype(F32)
            grads[u, 2 * q] = jnp.where(first8, a, swap(b))
            grads[u, 2 * q + 1] = jnp.where(first8, swap(a), b)

    @pl.loop(0, 2)
    def _(n):
        rows = pl.ds(pl.multiple_of(n * 512, 512), 512)
        for side in range(3):
            product = mm(fv[rows, :], wt[pl.ds(side * 384, 384), :], NT)
            for j in range(3):
                part = product[:, j * LANES : (j + 1) * LANES].reshape(4, 16, 8, LANES)
                for e in range(4):
                    taps[pl.ds((3 * side + j) * plane + (e + 1) * wide + REACH + n * 4 * wide, 16)] = part[e]

    def body(u, y):
        here = (u + 1) * wide + REACH + y
        g = grads[u, y]
        mid = taps[4 * plane + here]
        left = taps[3 * plane - 1 + here]
        right = taps[5 * plane + 1 + here]
        branch = jnp.zeros((8, LANES), F32)
        total = [jnp.zeros((8, LANES), F32) for _ in range(3)]
        shared = []
        for k in range(shears):
            d = shear[k]
            ys = y - d * (u - 4)
            keep = ((ys >= 0) & (ys < 16)).astype(F32)
            has_minus = (ys >= 1).astype(F32)
            has_plus = (ys <= 14).astype(F32)
            a, b = here - d, here + d
            main = mid + (taps[plane - wide + a] + taps[7 * plane + wide + b])
            minus = left + (taps[-wide - 1 + a] + taps[6 * plane + wide - 1 + b])
            plus = right + (taps[2 * plane - wide + 1 + a] + taps[8 * plane + wide + 1 + b])
            act, slope = gate(main + has_minus * minus + has_plus * plus)
            act = keep * act
            bk = beta[k]
            branch = branch + bk * act
            shared.append(g * act)
            dp = (bk * (keep * g) * slope).astype(BF).astype(F32)
            parts = (has_minus * dp, dp, has_plus * dp)
            for j in range(3):
                dps[(j * shears + k) * plane + here] = parts[j]
                total[j] = total[j] + parts[j]
        for j in range(3):
            sums[j * plane + here] = total[j]
        outs[u, y] = own[u, pl.ds(y, 8, stride=16), :] + branch
        return shared

    @pl.loop(0, 64)
    def _(n):
        u, y = n // 8, (n % 8) * 2
        first, second = body(u, y), body(u, y + 1)
        for k in range(shears):
            blend[k] += first[k] + second[k]

    @pl.loop(0, 64)
    def _(n):
        here = (n // 8 + 1) * wide + REACH + (n % 8) * 2
        at = pl.ds(pl.multiple_of(n * 16, 16), 16)
        below = [jnp.zeros((2, 8, LANES), F32) for _ in range(3)]
        above = [jnp.zeros((2, 8, LANES), F32) for _ in range(3)]
        for k in range(shears):
            d = shear[k]
            up, down = here + d, here - d
            for j in range(3):
                offset = (j * shears + k) * plane - (j - 1)
                below[j] = below[j] + dps[pl.ds(offset + wide + up, 2)]
                above[j] = above[j] + dps[pl.ds(offset - wide + down, 2)]
        for j in range(3):
            middle = sums[pl.ds(j * plane - (j - 1) + here, 2)]
            for side, value in enumerate((below[j], middle, above[j])):
                edges[at, pl.ds((3 * side + j) * LANES, LANES)] = value.reshape(16, LANES).astype(BF)

    pack_grads([mm(fv[...], edges[:, pl.ds(side * 384, 384)], TN) for side in range(3)], blend, pay)

    @pl.loop(0, 4)
    def _(n):
        rows = pl.ds(pl.multiple_of(n * 256, 256), 256)
        back = mm(edges[rows, :], wt[...], NN).reshape(2, LANES, LANES)
        for e in range(2):
            u = 2 * n + e
            own[u] = grads[u].reshape(LANES, LANES) + back[e]
            for x in range(8):
                dvert[u, x] = own[u, pl.ds(x, 16, stride=8), :].astype(BF)
            for q in range(8):
                lanes = pl.ds(pl.multiple_of((u * 8 + q) * LANES, LANES), LANES)
                a, b = outs[u, 2 * q], outs[u, 2 * q + 1]
                out[0, :, lanes] = jnp.where(first8, a, swap(b)).astype(BF)
                out[1, :, lanes] = jnp.where(first8, swap(a), b).astype(BF)


def call(body, fetched, operands, out_shapes, scratch, cost, vmem_mib):
    vmem = pl.BlockSpec(memory_space=pltpu.VMEM)
    specs = [pl.BlockSpec(memory_space=pltpu.HBM)] * len(fetched)
    specs += [pl.BlockSpec(memory_space=pltpu.SMEM if op.dtype == jnp.int32 else pltpu.VMEM) for op in operands]
    held = [pltpu.SMEM(fetched[0].shape, fetched[0].dtype)] + [pltpu.VMEM(op.shape, op.dtype) for op in fetched[1:]]
    count = len(fetched)

    def kernel(*refs):
        sources, others = refs[:count], refs[count : -count - 1]
        targets, sem = refs[-count - 1 : -1], refs[-1]
        copies = [pltpu.make_async_copy(sources[i], targets[i], sem.at[i]) for i in range(count)]
        for copy in copies:
            copy.start()

        def ready():
            for copy in copies:
                copy.wait()

        body(ready, *targets, *others)

    return pl.pallas_call(
        kernel,
        out_shape=out_shapes,
        in_specs=specs,
        out_specs=[vmem] * len(out_shapes),
        scratch_shapes=list(scratch) + held + [pltpu.SemaphoreType.DMA((count,))],
        compiler_params=pltpu.CompilerParams(vmem_limit_bytes=int(vmem_mib * MIB)),
        cost_estimate=pl.CostEstimate(flops=cost, bytes_accessed=4_000_000, transcendentals=1_000_000),
    )(*[pltpu.with_memory_space_constraint(op, pltpu.HBM) for op in fetched], *operands)


def unpack(total, w_h, w_v, b_h, b_v):
    scale = 262144.0**-0.5
    for at, weight, blend in ((0, w_h, b_h), (5 * HALF, w_v, b_v)):
        for pair in range(5):
            block = total[pl.ds(at + pair * HALF, HALF), :] * scale
            weight[2 * pair] = block[:, :HALF]
            other = swap(block)[:, :HALF]
            if pair < 4:
                weight[2 * pair + 1] = other
            else:
                blend[...] = other[: blend.shape[0]]


def reduce_all(pay):
    part = lax.all_to_all(pay.reshape(16, 40, LANES), "img", 0, 0, tiled=True).sum(0)
    part = lax.all_to_all(jnp.broadcast_to(part[None], (8, 40, LANES)), "vrow", 0, 0, tiled=True).sum(0)
    return lax.all_to_all(jnp.broadcast_to(part[None], (16, 40, LANES)), "img", 0, 0, tiled=True).reshape(640, LANES)


def per_device(features, weight_h, weight_v, beta_h, beta_v, shear_set, cotangent):
    shears = shear_set.shape[0]
    img = lax.axis_size("img")
    sds = jax.ShapeDtypeStruct
    own = features.reshape(16, 8, 1024)
    to_right = [(i, i + 1) for i in range(img - 1)]
    to_left = [(i + 1, i) for i in range(img - 1)]
    from_left = lax.ppermute(own, "img", to_right)
    from_right = lax.ppermute(own, "img", to_left)
    base = (lax.axis_index("img") * 8).astype(jnp.int32).reshape(1)
    w_h = jnp.transpose(weight_h, (2, 3, 0, 1)).reshape(TAPS, HALF, HALF)
    w_v = jnp.transpose(weight_v, (2, 3, 0, 1)).reshape(TAPS, HALF, HALF)

    hfeat, pre, f0, fmi, fpl = call(
        h_forward,
        (shear_set, beta_h, w_h, own),
        (base, from_left, from_right),
        [sds((8, 8, 16, LANES), BF), sds((shears * 112, 2, 8, LANES), F32)] + [sds((1024, LANES), BF)] * 3,
        [pltpu.VMEM((shears, 8, LANES), F32), pltpu.VMEM((8, 384, LANES), F32)]
        + [pltpu.VMEM((20 * LANES, LANES), BF)] * 3
        + [pltpu.VMEM((TAPS * 160, 2, 8, LANES), F32), pltpu.VMEM((TAPS * LANES, LANES), BF)],
        2 * 2560 * LANES * TAPS * LANES,
        GRANT[0],
    )
    moved = lax.all_to_all(hfeat, "vrow", 0, 0, tiled=True)
    output, dvert, pay_v = call(
        v_both,
        (shear_set, beta_v, w_v, cotangent),
        (moved,),
        [sds((2, 8, 8192), BF), sds((8, 8, 16, LANES), BF), sds((320, LANES), F32)],
        [
            pltpu.VMEM((shears, 8, LANES), F32),
            pltpu.VMEM((8, LANES, LANES), F32),
            pltpu.VMEM((1024, LANES), BF),
            pltpu.VMEM((TAPS * 220, 8, LANES), F32),
            pltpu.VMEM((3 * shears * 220, 8, LANES), F32),
            pltpu.VMEM((3 * 220, 8, LANES), F32),
            pltpu.VMEM((8, 16, 8, LANES), F32),
            pltpu.VMEM((8, 16, 8, LANES), F32),
            pltpu.VMEM((1024, TAPS * LANES), BF),
            pltpu.VMEM((shears, 8, LANES), F32),
            pltpu.VMEM((TAPS * LANES, LANES), BF),
        ],
        6 * 1024 * LANES * TAPS * LANES,
        GRANT[1],
    )
    grad = lax.all_to_all(dvert, "vrow", 0, 0, tiled=True)
    grad_right = lax.ppermute(grad[:, :REACH], "img", to_left)
    grad_left = lax.ppermute(grad[:, 8 - REACH :], "img", to_right)
    grad_features, pay = call(
        h_backward,
        (shear_set, beta_h, w_h),
        (base, pre, f0, fmi, fpl, grad, grad_left, grad_right, pay_v),
        [sds((16, 8, 1024), BF), sds((640, LANES), F32)],
        [
            pltpu.VMEM((shears, 8, LANES), F32),
            pltpu.VMEM((3 * shears * 112, 2, 8, LANES), F32),
            pltpu.VMEM((3 * 112, 2, 8, LANES), F32),
            pltpu.VMEM((3, 1024, 384), BF),
            pltpu.VMEM((3, 1024, LANES), F32),
            pltpu.VMEM((8, LANES, LANES), F32),
            pltpu.VMEM((shears, 8, LANES), F32),
            pltpu.VMEM((TAPS * LANES, LANES), BF),
        ],
        4 * 1024 * LANES * TAPS * LANES,
        GRANT[2],
    )
    vmem = pl.BlockSpec(memory_space=pltpu.VMEM)
    weights = sds((TAPS, HALF, HALF), F32)
    w_grad_h, w_grad_v, beta_grad_h, beta_grad_v = pl.pallas_call(
        unpack,
        out_shape=[weights, weights] + [sds((shears, HALF), F32)] * 2,
        in_specs=[vmem],
        out_specs=[vmem] * 4,
    )(reduce_all(pay))

    def placed(weight):
        return jnp.transpose(weight.reshape(3, 3, HALF, HALF), (2, 3, 0, 1))

    return output, grad_features.reshape(features.shape), placed(w_grad_h), placed(w_grad_v), beta_grad_h, beta_grad_v


def solution(mesh):
    placed = (P("vrow", None, "img", None), P(), P(), P(), P(), P(), P("vrow", "img", None))
    return jax.shard_map(
        per_device,
        mesh=mesh,
        in_specs=placed,
        out_specs=(P("vrow", "img", None), P("vrow", None, "img", None), P(), P(), P(), P()),
        check_vma=False,
    )
```

```python
import jax
import jax.numpy as jnp
from jax import lax
from jax.experimental import pallas as pl
from jax.experimental.pallas import tpu as pltpu
from jax.sharding import PartitionSpec as P

BF = jnp.bfloat16
F32 = jnp.float32
LANES = 128
HALF = 64
TAPS = 9
REACH = 3
MIB = 1024 * 1024
GRANT = (26, 36, 34, 26, 16)
NT = (((1,), (1,)), ((), ()))
NN = (((1,), (0,)), ((), ()))
TN = (((0,), (0,)), ((), ()))


def mm(lhs, rhs, dims):
    return lax.dot_general(lhs, rhs, dims, preferred_element_type=F32)


def lanes_of(shape):
    return lax.broadcasted_iota(jnp.int32, shape, len(shape) - 1)


def swap(value):
    return pltpu.roll(value, HALF, axis=value.ndim - 1)


def low(shape):
    return lanes_of(shape) < HALF


def fill_weights(w_ref, wt_ref):
    zero = jnp.zeros((HALF, HALF), BF)
    for tap in range(TAPS):
        w = w_ref[tap]
        wt_ref[pl.ds(tap * LANES, HALF), :] = jnp.concatenate([w, zero], axis=1)
        wt_ref[pl.ds(tap * LANES + HALF, HALF), :] = jnp.concatenate([zero, w], axis=1)


def spread(beta_ref, beta):
    for k in range(beta.shape[0]):
        line = beta_ref[pl.ds(k, 1), :]
        beta[k] = jnp.broadcast_to(jnp.concatenate([line, line], axis=1), (8, LANES))


def pack_grads(grads, blend_ref, pay_ref):
    first = low((HALF, LANES))
    rows = lax.broadcasted_iota(jnp.int32, (HALF, LANES), 0)
    blend = jnp.zeros((HALF, LANES), F32)
    for k in range(blend_ref.shape[0]):
        line = jnp.sum(blend_ref[k], axis=0, keepdims=True)
        blend = blend + jnp.where(rows == k, line + swap(line), 0.0)

    def tap_of(tap):
        block = grads[tap // 3][:, (tap % 3) * LANES : (tap % 3 + 1) * LANES]
        return block[:HALF] + swap(block[HALF:])

    for pair in range(5):
        even = tap_of(2 * pair)
        odd = tap_of(2 * pair + 1) if pair < 4 else even
        both = jnp.transpose(jnp.where(first, even, swap(odd)))
        value = jnp.concatenate([both[:HALF], both[HALF:]], axis=1)
        if pair == 4:
            value = jnp.where(first, value, blend)
        pay_ref[pl.ds(pair * HALF, HALF), :] = value


def gate(pre):
    s = 0.5 * jnp.tanh(0.5 * pre) + 0.5
    act = pre * s
    return act, s + act * (1.0 - s)


def halves():
    return (lanes_of((1, 8, LANES)) >= HALF).astype(jnp.int32)


def h_forward(ready, shear, beta_ref, w_ref, fm, base, fl, fr, hfeat, pre_ref, taps, f0_out, fm_out, fp_out, beta, stage, f0, fmi, fpl, wt):
    shears = shear.shape[0]
    ready()
    spread(beta_ref, beta)
    fill_weights(w_ref, wt)
    first16 = low((16, LANES))

    @pl.loop(0, 16)
    def _(y):
        for part, ref in enumerate((fl, fm, fr)):
            for q in range(8):
                stage[q, pl.ds(y * 24 + 8 * part, 8), :] = ref[y, :, pl.ds(q * LANES, LANES)].astype(F32)

    @pl.loop(0, 20)
    def _(x):
        own = [stage[q, pl.ds(x + 2, 16, stride=24), :] for q in range(8)]
        turned = [swap(a) for a in own]
        zero = jnp.zeros((16, LANES), F32)
        moved = [
            jnp.where(first16, turned[q - 1] if q > 0 else zero, turned[q] if q < 8 else zero).astype(BF)
            for q in range(9)
        ]
        for q in range(8):
            at = pl.ds(pl.multiple_of(x * LANES + q * 16, 16), 16)
            f0[at, :] = own[q].astype(BF)
            fmi[at, :] = moved[q]
            fpl[at, :] = moved[q + 1]

    @pl.loop(0, 5)
    def _(n):
        at = pl.ds(pl.multiple_of(n * 512, 512), 512)
        for side, ref in enumerate((fmi, f0, fpl)):
            product = mm(ref[at, :], wt[pl.ds(side * 384, 384), :], NT)
            for j in range(3):
                part = product[:, j * LANES : (j + 1) * LANES].reshape(32, 2, 8, LANES)
                taps[pl.ds((3 * side + j) * 160 + n * 32, 32)] = part

    f0_out[...] = f0[pl.ds(6 * LANES, 1024), :]
    fm_out[...] = fmi[pl.ds(6 * LANES, 1024), :]
    fp_out[...] = fpl[pl.ds(6 * LANES, 1024), :]

    half = halves()

    @pl.loop(0, 64)
    def _(n):
        q = n % 8
        branch = jnp.zeros((2, 8, LANES), F32)
        for k, (xs, pre) in enumerate(sheared_taps(shear, base, taps, half, n // 8 + REACH, q)):
            pre_ref[k * 64 + n] = pre
            keep = (xs >= 0) & (xs < LANES)
            branch = branch + jnp.where(keep, beta[k] * gate(pre)[0], 0.0)
        own = f0[pl.ds(pl.multiple_of(n * 16 + 6 * LANES, 16), 16), :].astype(F32)
        hfeat[q, n // 8] = (own + branch.reshape(16, LANES)).astype(BF)


def sheared_taps(shear, base, taps, half, xe, q):
    here = (xe + 3) * 8 + q
    vrel = half + (2 * q - 8)
    xg = base[0] + xe - REACH
    mid = taps[4 * 160 + here]
    left = taps[3 * 160 - 8 + here]
    right = taps[5 * 160 + 8 + here]
    found = []
    for k in range(shear.shape[0]):
        d = shear[k]
        xs = xg - d * vrel
        a, b = here - d * 8, here + d * 8
        main = mid + (taps[160 + a] + taps[7 * 160 + b])
        minus = left + (taps[a - 8] + taps[6 * 160 - 8 + b])
        plus = right + (taps[2 * 160 + 8 + a] + taps[8 * 160 + 8 + b])
        found.append((xs, main + jnp.where(xs >= 1, minus, 0.0) + jnp.where(xs <= LANES - 2, plus, 0.0)))
    return found


def h_slopes(ready, shear, beta_ref, base, pre_ref, taps, slopes, acts, beta):
    ready()
    spread(beta_ref, beta)
    half = halves()

    def save(k, at, xs, pre, local):
        act, slope = gate(pre)
        keep = (xs >= 0) & (xs < LANES)
        slopes[k * 112 + at] = jnp.where(keep, beta[k] * slope, 0.0)
        if local is not None:
            acts[k * 64 + local] = jnp.where(keep, act, 0.0)

    @pl.loop(0, 64)
    def _(n):
        vrel = half + (2 * (n % 8) - 8)
        xg = base[0] + n // 8
        for k in range(shear.shape[0]):
            save(k, n + REACH * 8, xg - shear[k] * vrel, pre_ref[k * 64 + n], n)

    @pl.loop(0, 24)
    def _(n):
        for xe in (n // 8, n // 8 + 8 + REACH):
            for k, (xs, pre) in enumerate(sheared_taps(shear, base, taps, half, xe, n % 8)):
                save(k, xe * 8 + n % 8, xs, pre, None)


def h_backward(ready, shear, base, slopes, acts, f0, fmi, fpl, gm, gl, gr, pay_v, pay, edges_out, dps, sums, edges, blend, edges_sem):
    shears = shear.shape[0]
    step = shears * 112
    ready()
    half = halves()
    blend[...] = jnp.zeros(blend.shape, F32)

    def body(xe, q, g, local):
        here = xe * 8 + q
        g = g.astype(F32).reshape(2, 8, LANES)
        vrel = half + (2 * q - 8)
        xg = base[0] + xe - REACH
        total = [jnp.zeros((2, 8, LANES), F32) for _ in range(3)]
        for k in range(shears):
            xs = xg - shear[k] * vrel
            dp = (slopes[k * 112 + here] * g).astype(BF).astype(F32)
            parts = (jnp.where(xs >= 1, dp, 0.0), dp, jnp.where(xs <= LANES - 2, dp, 0.0))
            for j in range(3):
                dps[j * step + k * 112 + here] = parts[j]
                total[j] = total[j] + parts[j]
            if local:
                blend[k] += jnp.sum(g * acts[k * 64 - REACH * 8 + here], axis=0)
        for j in range(3):
            sums[j * 112 + here] = total[j]

    @pl.loop(0, 64)
    def _(n):
        x, q = n // 8, n % 8
        body(x + REACH, q, gm[q, x], True)

    @pl.loop(0, 24)
    def _(n):
        x, q = n // 8, n % 8
        body(x, q, gl[q, x], False)
        body(x + 8 + REACH, q, gr[q, x], False)

    @pl.loop(0, 64)
    def _(n):
        here = n + REACH * 8
        at = pl.ds(pl.multiple_of(n * 16, 16), 16)
        below = [jnp.zeros((2, 8, LANES), F32) for _ in range(3)]
        above = [jnp.zeros((2, 8, LANES), F32) for _ in range(3)]
        for k in range(shears):
            d = shear[k]
            up, down = here + d * 8, here - d * 8
            for j in range(3):
                below[j] = below[j] + dps[j * step + k * 112 - (j - 1) * 8 + up]
                above[j] = above[j] + dps[j * step + k * 112 - (j - 1) * 8 + down]
        for j in range(3):
            lanes = pl.ds(j * LANES, LANES)
            edges[0, at, lanes] = below[j].reshape(16, LANES).astype(BF)
            edges[1, at, lanes] = sums[j * 112 - (j - 1) * 8 + here].reshape(16, LANES).astype(BF)
            edges[2, at, lanes] = above[j].reshape(16, LANES).astype(BF)

    copy = pltpu.make_async_copy(edges, edges_out, edges_sem)
    copy.start()
    pack_grads([mm(ref[...], edges[side], TN) for side, ref in enumerate((fmi, f0, fpl))], blend, pay)
    pay[pl.ds(5 * HALF, 5 * HALF), :] = pay_v[...]
    copy.wait()


def h_finish(ready, w_ref, edges, gm, out, token, dfs, stage, wt):
    token[...] = jnp.zeros(token.shape, F32)
    ready()
    fill_weights(w_ref, wt)

    @pl.loop(0, 4)
    def _(x):
        at = pl.ds(pl.multiple_of(x * 256, 256), 256)
        for side in range(3):
            dfs[side, at, :] = mm(edges[side, at, :], wt[pl.ds(side * 384, 384), :], NN)

    first16 = low((16, LANES))

    @pl.loop(0, 8)
    def _(x):
        def piece(side, q):
            if q < 0 or q > 7:
                return jnp.zeros((16, LANES), F32)
            return dfs[side, pl.ds(pl.multiple_of(x * LANES + q * 16, 16), 16), :]

        for q in range(8):
            upper = piece(0, q) + piece(2, q - 1)
            lower = piece(0, q + 1) + piece(2, q)
            turned = swap(jnp.where(first16, lower, upper))
            total = gm[q, x].astype(F32) + piece(1, q) + turned
            stage[q, pl.ds(x * 16, 16), :] = total

    @pl.loop(0, 16)
    def _(y):
        for q in range(8):
            out[y, :, pl.ds(q * LANES, LANES)] = stage[q, pl.ds(y, 8, stride=16), :].astype(BF)


def v_both(ready, shear, beta_ref, w_ref, cot, h_ref, out, dvert, pay, beta, own, fv, taps, dps, sums, grads, outs, edges, blend, wt):
    shears = shear.shape[0]
    wide = 22
    plane = 10 * wide
    blend[...] = jnp.zeros(blend.shape, F32)
    first8 = low((8, LANES))

    for u in (0, 9):
        sheet = jnp.zeros((wide, 8, LANES), F32)
        for tap in (0, 1, 2) if u == 0 else (6, 7, 8):
            taps[pl.ds(tap * plane + u * wide, wide)] = sheet
        for jk in range(3 * shears):
            dps[pl.ds(jk * plane + u * wide, wide)] = sheet

    @pl.loop(1, 9)
    def _(u):
        rim = jnp.zeros((REACH, 8, LANES), F32)
        for side in (0, 16 + REACH):
            for tap in range(TAPS):
                taps[pl.ds(tap * plane + side + u * wide, REACH)] = rim
            for j in range(3):
                sums[pl.ds(j * plane + side + u * wide, REACH)] = rim
            for jk in range(3 * shears):
                dps[pl.ds(jk * plane + side + u * wide, REACH)] = rim

    ready()
    spread(beta_ref, beta)
    fill_weights(w_ref, wt)

    @pl.loop(0, 8)
    def _(u):
        for x in range(8):
            own[u, pl.ds(x * 16, 16), :] = h_ref[u, x].astype(F32)
        for y in range(0, 16, 2):
            pair = [own[u, pl.ds(y + e, 8, stride=16), :] for e in range(2)]
            fv[pl.ds(pl.multiple_of(u * LANES + y * 8, 16), 16), :] = jnp.concatenate(pair, axis=0).astype(BF)
        for q in range(8):
            lanes = pl.ds(pl.multiple_of((u * 8 + q) * LANES, LANES), LANES)
            a, b = cot[0, :, lanes].astype(F32), cot[1, :, lanes].astype(F32)
            grads[u, 2 * q] = jnp.where(first8, a, swap(b))
            grads[u, 2 * q + 1] = jnp.where(first8, swap(a), b)

    @pl.loop(0, 2)
    def _(n):
        rows = pl.ds(pl.multiple_of(n * 512, 512), 512)
        for side in range(3):
            product = mm(fv[rows, :], wt[pl.ds(side * 384, 384), :], NT)
            for j in range(3):
                part = product[:, j * LANES : (j + 1) * LANES].reshape(4, 16, 8, LANES)
                for e in range(4):
                    taps[pl.ds((3 * side + j) * plane + (e + 1) * wide + REACH + n * 4 * wide, 16)] = part[e]

    def body(u, y):
        here = (u + 1) * wide + REACH + y
        g = grads[u, y]
        mid = taps[4 * plane + here]
        left = taps[3 * plane - 1 + here]
        right = taps[5 * plane + 1 + here]
        branch = jnp.zeros((8, LANES), F32)
        total = [jnp.zeros((8, LANES), F32) for _ in range(3)]
        shared = []
        for k in range(shears):
            d = shear[k]
            ys = jnp.full((8, LANES), y - d * (u - 4), jnp.int32)
            keep = (ys >= 0) & (ys < 16)
            has_minus, has_plus = ys >= 1, ys <= 14
            a, b = here - d, here + d
            main = mid + (taps[plane - wide + a] + taps[7 * plane + wide + b])
            minus = left + (taps[-wide - 1 + a] + taps[6 * plane + wide - 1 + b])
            plus = right + (taps[2 * plane - wide + 1 + a] + taps[8 * plane + wide + 1 + b])
            act, slope = gate(main + jnp.where(has_minus, minus, 0.0) + jnp.where(has_plus, plus, 0.0))
            act = jnp.where(keep, act, 0.0)
            bk = beta[k]
            branch = branch + bk * act
            shared.append(g * act)
            dp = jnp.where(keep, bk * g * slope, 0.0).astype(BF).astype(F32)
            parts = (jnp.where(has_minus, dp, 0.0), dp, jnp.where(has_plus, dp, 0.0))
            for j in range(3):
                dps[(j * shears + k) * plane + here] = parts[j]
                total[j] = total[j] + parts[j]
        for j in range(3):
            sums[j * plane + here] = total[j]
        outs[u, y] = own[u, pl.ds(y, 8, stride=16), :] + branch
        return shared

    @pl.loop(0, 64)
    def _(n):
        u, y = n // 8, (n % 8) * 2
        first, second = body(u, y), body(u, y + 1)
        for k in range(shears):
            blend[k] += first[k] + second[k]

    @pl.loop(0, 64)
    def _(n):
        here = (n // 8 + 1) * wide + REACH + (n % 8) * 2
        at = pl.ds(pl.multiple_of(n * 16, 16), 16)
        below = [jnp.zeros((2, 8, LANES), F32) for _ in range(3)]
        above = [jnp.zeros((2, 8, LANES), F32) for _ in range(3)]
        for k in range(shears):
            d = shear[k]
            up, down = here + d, here - d
            for j in range(3):
                offset = (j * shears + k) * plane - (j - 1)
                below[j] = below[j] + dps[pl.ds(offset + wide + up, 2)]
                above[j] = above[j] + dps[pl.ds(offset - wide + down, 2)]
        for j in range(3):
            middle = sums[pl.ds(j * plane - (j - 1) + here, 2)]
            for side, value in enumerate((below[j], middle, above[j])):
                edges[at, pl.ds((3 * side + j) * LANES, LANES)] = value.reshape(16, LANES).astype(BF)

    pack_grads([mm(fv[...], edges[:, pl.ds(side * 384, 384)], TN) for side in range(3)], blend, pay)

    @pl.loop(0, 4)
    def _(n):
        rows = pl.ds(pl.multiple_of(n * 256, 256), 256)
        back = mm(edges[rows, :], wt[...], NN).reshape(2, LANES, LANES)
        for e in range(2):
            u = 2 * n + e
            own[u] = grads[u].reshape(LANES, LANES) + back[e]
            for x in range(8):
                dvert[u, x] = own[u, pl.ds(x, 16, stride=8), :].astype(BF)
            for q in range(8):
                lanes = pl.ds(pl.multiple_of((u * 8 + q) * LANES, LANES), LANES)
                a, b = outs[u, 2 * q], outs[u, 2 * q + 1]
                out[0, :, lanes] = jnp.where(first8, a, swap(b)).astype(BF)
                out[1, :, lanes] = jnp.where(first8, swap(a), b).astype(BF)


def call(body, fetched, operands, out_shapes, scratch, cost, vmem_mib, far=()):
    vmem = pl.BlockSpec(memory_space=pltpu.VMEM)
    specs = [pl.BlockSpec(memory_space=pltpu.HBM)] * len(fetched)
    specs += [pl.BlockSpec(memory_space=pltpu.SMEM if op.dtype == jnp.int32 else pltpu.VMEM) for op in operands]
    held = [(pltpu.SMEM if op.dtype == jnp.int32 else pltpu.VMEM)(op.shape, op.dtype) for op in fetched]
    count = len(fetched)

    def kernel(*refs):
        sources, others = refs[:count], refs[count : -count - 1]
        targets, sem = refs[-count - 1 : -1], refs[-1]
        copies = [pltpu.make_async_copy(sources[i], targets[i], sem.at[i]) for i in range(count)]
        for copy in copies:
            copy.start()

        def ready():
            for copy in copies:
                copy.wait()

        body(ready, *targets, *others)

    return pl.pallas_call(
        kernel,
        out_shape=out_shapes,
        in_specs=specs,
        out_specs=[pl.BlockSpec(memory_space=pltpu.HBM) if i in far else vmem for i in range(len(out_shapes))],
        scratch_shapes=list(scratch) + held + [pltpu.SemaphoreType.DMA((count,))],
        compiler_params=pltpu.CompilerParams(vmem_limit_bytes=int(vmem_mib * MIB)),
        cost_estimate=pl.CostEstimate(flops=cost, bytes_accessed=4_000_000, transcendentals=1_000_000),
    )(*[pltpu.with_memory_space_constraint(op, pltpu.HBM) for op in fetched], *operands)


def unpack(total, w_h, w_v, b_h, b_v):
    scale = 262144.0**-0.5
    for at, weight, blend in ((0, w_h, b_h), (5 * HALF, w_v, b_v)):
        for pair in range(5):
            block = total[pl.ds(at + pair * HALF, HALF), :] * scale
            weight[2 * pair] = block[:, :HALF]
            other = swap(block)[:, :HALF]
            if pair < 4:
                weight[2 * pair + 1] = other
            else:
                blend[...] = other[: blend.shape[0]]


def reduce_all(pay, zero):
    part = lax.all_to_all(pay.reshape(16, 40, LANES), "img", 0, 0, tiled=True).sum(0) + zero
    part = lax.all_to_all(jnp.broadcast_to(part[None], (8, 40, LANES)), "vrow", 0, 0, tiled=True).sum(0)
    return lax.all_to_all(jnp.broadcast_to(part[None], (16, 40, LANES)), "img", 0, 0, tiled=True).reshape(640, LANES)


def per_device(features, weight_h, weight_v, beta_h, beta_v, shear_set, cotangent):
    shears = shear_set.shape[0]
    img = lax.axis_size("img")
    sds = jax.ShapeDtypeStruct
    own = features.reshape(16, 8, 1024)
    to_right = [(i, i + 1) for i in range(img - 1)]
    to_left = [(i + 1, i) for i in range(img - 1)]
    from_left = lax.ppermute(own, "img", to_right)
    from_right = lax.ppermute(own, "img", to_left)
    base = (lax.axis_index("img") * 8).astype(jnp.int32).reshape(1)
    w_h = jnp.transpose(weight_h, (2, 3, 0, 1)).reshape(TAPS, HALF, HALF)
    w_v = jnp.transpose(weight_v, (2, 3, 0, 1)).reshape(TAPS, HALF, HALF)

    hfeat, pre, taps, f0, fmi, fpl = call(
        h_forward,
        (shear_set, beta_h, w_h, own),
        (base, from_left, from_right),
        [sds((8, 8, 16, LANES), BF), sds((shears * 64, 2, 8, LANES), F32), sds((TAPS * 160, 2, 8, LANES), F32)]
        + [sds((1024, LANES), BF)] * 3,
        [pltpu.VMEM((shears, 8, LANES), F32), pltpu.VMEM((8, 384, LANES), F32)]
        + [pltpu.VMEM((20 * LANES, LANES), BF)] * 3
        + [pltpu.VMEM((TAPS * LANES, LANES), BF)],
        2 * 2560 * LANES * TAPS * LANES,
        GRANT[0],
    )
    moved = lax.all_to_all(hfeat, "vrow", 0, 0, tiled=True)
    slopes, acts = call(
        h_slopes,
        (shear_set, beta_h),
        (base, pre, taps),
        [sds((shears * 112, 2, 8, LANES), F32), sds((shears * 64, 2, 8, LANES), F32)],
        [pltpu.VMEM((shears, 8, LANES), F32)],
        1_000_000,
        GRANT[3],
    )
    output, dvert, pay_v = call(
        v_both,
        (shear_set, beta_v, w_v, cotangent),
        (moved,),
        [sds((2, 8, 8192), BF), sds((8, 8, 16, LANES), BF), sds((320, LANES), F32)],
        [
            pltpu.VMEM((shears, 8, LANES), F32),
            pltpu.VMEM((8, LANES, LANES), F32),
            pltpu.VMEM((1024, LANES), BF),
            pltpu.VMEM((TAPS * 220, 8, LANES), F32),
            pltpu.VMEM((3 * shears * 220, 8, LANES), F32),
            pltpu.VMEM((3 * 220, 8, LANES), F32),
            pltpu.VMEM((8, 16, 8, LANES), F32),
            pltpu.VMEM((8, 16, 8, LANES), F32),
            pltpu.VMEM((1024, TAPS * LANES), BF),
            pltpu.VMEM((shears, 8, LANES), F32),
            pltpu.VMEM((TAPS * LANES, LANES), BF),
        ],
        6 * 1024 * LANES * TAPS * LANES,
        GRANT[1],
    )
    grad = lax.all_to_all(dvert, "vrow", 0, 0, tiled=True)
    grad_right = lax.ppermute(grad[:, :REACH], "img", to_left)
    grad_left = lax.ppermute(grad[:, 8 - REACH :], "img", to_right)
    pay, edges_h = call(
        h_backward,
        (shear_set,),
        (base, slopes, acts, f0, fmi, fpl, grad, grad_left, grad_right, pay_v),
        [sds((640, LANES), F32), pltpu.HBM((3, 1024, 384), BF)],
        [
            pltpu.VMEM((3 * shears * 112, 2, 8, LANES), F32),
            pltpu.VMEM((3 * 112, 2, 8, LANES), F32),
            pltpu.VMEM((3, 1024, 384), BF),
            pltpu.VMEM((shears, 8, LANES), F32),
            pltpu.SemaphoreType.DMA,
        ],
        2 * 1024 * LANES * TAPS * LANES,
        GRANT[2],
        (1,),
    )
    grad_features, finished = call(
        h_finish,
        (w_h, edges_h, grad),
        (),
        [sds((16, 8, 1024), BF), sds((40, LANES), F32)],
        [
            pltpu.VMEM((3, 1024, LANES), F32),
            pltpu.VMEM((8, LANES, LANES), F32),
            pltpu.VMEM((TAPS * LANES, LANES), BF),
        ],
        2 * 1024 * LANES * TAPS * LANES,
        GRANT[4],
    )
    vmem = pl.BlockSpec(memory_space=pltpu.VMEM)
    weights = sds((TAPS, HALF, HALF), F32)
    w_grad_h, w_grad_v, beta_grad_h, beta_grad_v = pl.pallas_call(
        unpack,
        out_shape=[weights, weights] + [sds((shears, HALF), F32)] * 2,
        in_specs=[vmem],
        out_specs=[vmem] * 4,
    )(reduce_all(pay, finished))

    def placed(weight):
        return jnp.transpose(weight.reshape(3, 3, HALF, HALF), (2, 3, 0, 1))

    return output, grad_features.reshape(features.shape), placed(w_grad_h), placed(w_grad_v), beta_grad_h, beta_grad_v


def solution(mesh):
    placed = (P("vrow", None, "img", None), P(), P(), P(), P(), P(), P("vrow", "img", None))
    return jax.shard_map(
        per_device,
        mesh=mesh,
        in_specs=placed,
        out_specs=(P("vrow", "img", None), P("vrow", None, "img", None), P(), P(), P(), P()),
        check_vma=False,
    )
```

```python
import jax
import jax.numpy as jnp
from jax import lax
from jax.experimental import pallas as pl
from jax.experimental.pallas import tpu as pltpu
from jax.sharding import PartitionSpec as P

BF = jnp.bfloat16
F32 = jnp.float32
LANES = 128
HALF = 64
TAPS = 9
REACH = 3
MIB = 1024 * 1024
GRANT = (26, 36, 34, 26, 16)
NT = (((1,), (1,)), ((), ()))
NN = (((1,), (0,)), ((), ()))
TN = (((0,), (0,)), ((), ()))


def mm(lhs, rhs, dims):
    return lax.dot_general(lhs, rhs, dims, preferred_element_type=F32)


def lanes_of(shape):
    return lax.broadcasted_iota(jnp.int32, shape, len(shape) - 1)


def swap(value):
    return pltpu.roll(value, HALF, axis=value.ndim - 1)


def low(shape):
    return lanes_of(shape) < HALF


def fill_weights(w_ref, wt_ref, scale=1.0):
    zero = jnp.zeros((HALF, HALF), BF)
    for tap in range(TAPS):
        w = w_ref[tap]
        if scale != 1.0:
            w = (w.astype(F32) * scale).astype(BF)
        wt_ref[pl.ds(tap * LANES, HALF), :] = jnp.concatenate([w, zero], axis=1)
        wt_ref[pl.ds(tap * LANES + HALF, HALF), :] = jnp.concatenate([zero, w], axis=1)


def spread(beta_ref, beta):
    for k in range(beta.shape[0]):
        line = beta_ref[pl.ds(k, 1), :]
        beta[k] = jnp.broadcast_to(jnp.concatenate([line, line], axis=1), (8, LANES))


def pack_grads(grads, blend_ref, pay_ref):
    first = low((HALF, LANES))
    rows = lax.broadcasted_iota(jnp.int32, (HALF, LANES), 0)
    blend = jnp.zeros((HALF, LANES), F32)
    for k in range(blend_ref.shape[0]):
        line = jnp.sum(blend_ref[k], axis=0, keepdims=True)
        blend = blend + jnp.where(rows == k, line + swap(line), 0.0)

    def tap_of(tap):
        block = grads[tap // 3][:, (tap % 3) * LANES : (tap % 3 + 1) * LANES]
        return block[:HALF] + swap(block[HALF:])

    for pair in range(5):
        even = tap_of(2 * pair)
        odd = tap_of(2 * pair + 1) if pair < 4 else even
        both = jnp.transpose(jnp.where(first, even, swap(odd)))
        value = jnp.concatenate([both[:HALF], both[HALF:]], axis=1)
        if pair == 4:
            value = jnp.where(first, value, blend)
        pay_ref[pl.ds(pair * HALF, HALF), :] = value


def gate(h):
    t = jnp.tanh(h) + 1.0
    s = 0.5 * t
    act = h * t
    return act, s + act * (1.0 - s)


def halves():
    return (lanes_of((1, 8, LANES)) >= HALF).astype(jnp.int32)


def h_forward(ready, shear, beta_ref, w_ref, fm, base, fl, fr, hfeat, pre_ref, taps, f0_out, fm_out, fp_out, beta, stage, f0, fmi, fpl, wt):
    shears = shear.shape[0]
    ready()
    spread(beta_ref, beta)
    fill_weights(w_ref, wt, 0.5)
    first16 = low((16, LANES))

    @pl.loop(0, 16, unroll=2)
    def _(y):
        for part, ref in enumerate((fl, fm, fr)):
            for q in range(8):
                stage[q, pl.ds(y * 24 + 8 * part, 8), :] = ref[y, :, pl.ds(q * LANES, LANES)].astype(F32)

    @pl.loop(0, 20, unroll=4)
    def _(x):
        own = [stage[q, pl.ds(x + 2, 16, stride=24), :] for q in range(8)]
        turned = [swap(a) for a in own]
        zero = jnp.zeros((16, LANES), F32)
        moved = [
            jnp.where(first16, turned[q - 1] if q > 0 else zero, turned[q] if q < 8 else zero).astype(BF)
            for q in range(9)
        ]
        for q in range(8):
            at = pl.ds(pl.multiple_of(x * LANES + q * 16, 16), 16)
            f0[at, :] = own[q].astype(BF)
            fmi[at, :] = moved[q]
            fpl[at, :] = moved[q + 1]

    @pl.loop(0, 5)
    def _(n):
        at = pl.ds(pl.multiple_of(n * 512, 512), 512)
        for side, ref in enumerate((fmi, f0, fpl)):
            product = mm(ref[at, :], wt[pl.ds(side * 384, 384), :], NT)
            for j in range(3):
                part = product[:, j * LANES : (j + 1) * LANES].reshape(32, 2, 8, LANES)
                taps[pl.ds((3 * side + j) * 160 + n * 32, 32)] = part

    f0_out[...] = f0[pl.ds(6 * LANES, 1024), :]
    fm_out[...] = fmi[pl.ds(6 * LANES, 1024), :]
    fp_out[...] = fpl[pl.ds(6 * LANES, 1024), :]

    half = halves()

    @pl.loop(0, 64, unroll=8)
    def _(n):
        q = n % 8
        branch = jnp.zeros((2, 8, LANES), F32)
        for k, (xs, pre) in enumerate(sheared_taps(shear, base, taps, half, n // 8 + REACH, q)):
            pre_ref[k * 64 + n] = pre
            keep = xs.astype(jnp.uint32) < LANES
            branch = branch + jnp.where(keep, beta[k] * gate(pre)[0], 0.0)
        own = f0[pl.ds(pl.multiple_of(n * 16 + 6 * LANES, 16), 16), :].astype(F32)
        hfeat[q, n // 8] = (own + branch.reshape(16, LANES)).astype(BF)


def sheared_taps(shear, base, taps, half, xe, q):
    here = (xe + 3) * 8 + q
    vrel = half + (2 * q - 8)
    xg = base[0] + xe - REACH
    mid = taps[4 * 160 + here]
    left = taps[3 * 160 - 8 + here]
    right = taps[5 * 160 + 8 + here]
    found = []
    for k in range(shear.shape[0]):
        d = shear[k]
        xs = xg - d * vrel
        a, b = here - d * 8, here + d * 8
        main = mid + (taps[160 + a] + taps[7 * 160 + b])
        minus = left + (taps[a - 8] + taps[6 * 160 - 8 + b])
        plus = right + (taps[2 * 160 + 8 + a] + taps[8 * 160 + 8 + b])
        found.append((xs, main + jnp.where(xs >= 1, minus, 0.0) + jnp.where(xs <= LANES - 2, plus, 0.0)))
    return found


def h_slopes(ready, shear, beta_ref, base, pre_ref, taps, slopes, acts, beta):
    ready()
    spread(beta_ref, beta)
    half = halves()

    def save(k, at, xs, pre, local):
        act, slope = gate(pre)
        keep = xs.astype(jnp.uint32) < LANES
        slopes[k * 112 + at] = jnp.where(keep, beta[k] * slope, 0.0)
        if local is not None:
            acts[k * 64 + local] = jnp.where(keep, act, 0.0)

    @pl.loop(0, 64, unroll=8)
    def _(n):
        vrel = half + (2 * (n % 8) - 8)
        xg = base[0] + n // 8
        for k in range(shear.shape[0]):
            save(k, n + REACH * 8, xg - shear[k] * vrel, pre_ref[k * 64 + n], n)

    @pl.loop(0, 24)
    def _(n):
        for xe in (n // 8, n // 8 + 8 + REACH):
            for k, (xs, pre) in enumerate(sheared_taps(shear, base, taps, half, xe, n % 8)):
                save(k, xe * 8 + n % 8, xs, pre, None)


def h_backward(ready, shear, base, slopes, acts, f0, fmi, fpl, gm, gl, gr, pay_v, pay, edges_out, dps, sums, edges, blend, edges_sem):
    shears = shear.shape[0]
    step = shears * 112
    ready()
    half = halves()
    blend[...] = jnp.zeros(blend.shape, F32)

    def body(xe, q, g, local):
        here = xe * 8 + q
        g = g.astype(F32).reshape(2, 8, LANES)
        vrel = half + (2 * q - 8)
        xg = base[0] + xe - REACH
        total = [jnp.zeros((2, 8, LANES), F32) for _ in range(3)]
        for k in range(shears):
            xs = xg - shear[k] * vrel
            dp = (slopes[k * 112 + here] * g).astype(BF).astype(F32)
            parts = (jnp.where(xs >= 1, dp, 0.0), dp, jnp.where(xs <= LANES - 2, dp, 0.0))
            for j in range(3):
                dps[j * step + k * 112 + here] = parts[j]
                total[j] = total[j] + parts[j]
            if local:
                blend[k] += jnp.sum(g * acts[k * 64 - REACH * 8 + here], axis=0)
        for j in range(3):
            sums[j * 112 + here] = total[j]

    @pl.loop(0, 64, unroll=8)
    def _(n):
        x, q = n // 8, n % 8
        body(x + REACH, q, gm[q, x], True)

    @pl.loop(0, 24)
    def _(n):
        x, q = n // 8, n % 8
        body(x, q, gl[q, x], False)
        body(x + 8 + REACH, q, gr[q, x], False)

    @pl.loop(0, 64, unroll=8)
    def _(n):
        here = n + REACH * 8
        at = pl.ds(pl.multiple_of(n * 16, 16), 16)
        below = [jnp.zeros((2, 8, LANES), F32) for _ in range(3)]
        above = [jnp.zeros((2, 8, LANES), F32) for _ in range(3)]
        for k in range(shears):
            d = shear[k]
            up, down = here + d * 8, here - d * 8
            for j in range(3):
                below[j] = below[j] + dps[j * step + k * 112 - (j - 1) * 8 + up]
                above[j] = above[j] + dps[j * step + k * 112 - (j - 1) * 8 + down]
        for j in range(3):
            lanes = pl.ds(j * LANES, LANES)
            edges[0, at, lanes] = below[j].reshape(16, LANES).astype(BF)
            edges[1, at, lanes] = sums[j * 112 - (j - 1) * 8 + here].reshape(16, LANES).astype(BF)
            edges[2, at, lanes] = above[j].reshape(16, LANES).astype(BF)

    copy = pltpu.make_async_copy(edges, edges_out, edges_sem)
    copy.start()
    pack_grads([mm(ref[...], edges[side], TN) for side, ref in enumerate((fmi, f0, fpl))], blend, pay)
    pay[pl.ds(5 * HALF, 5 * HALF), :] = pay_v[...]
    copy.wait()


def h_finish(ready, w_ref, edges, gm, out, token, dfs, stage, wt):
    token[...] = jnp.zeros(token.shape, F32)
    ready()
    fill_weights(w_ref, wt)

    @pl.loop(0, 4)
    def _(x):
        at = pl.ds(pl.multiple_of(x * 256, 256), 256)
        for side in range(3):
            dfs[side, at, :] = mm(edges[side, at, :], wt[pl.ds(side * 384, 384), :], NN)

    first16 = low((16, LANES))

    @pl.loop(0, 8, unroll=2)
    def _(x):
        def piece(side, q):
            if q < 0 or q > 7:
                return jnp.zeros((16, LANES), F32)
            return dfs[side, pl.ds(pl.multiple_of(x * LANES + q * 16, 16), 16), :]

        for q in range(8):
            upper = piece(0, q) + piece(2, q - 1)
            lower = piece(0, q + 1) + piece(2, q)
            turned = swap(jnp.where(first16, lower, upper))
            total = gm[q, x].astype(F32) + piece(1, q) + turned
            stage[q, pl.ds(x * 16, 16), :] = total

    @pl.loop(0, 16, unroll=2)
    def _(y):
        for q in range(8):
            out[y, :, pl.ds(q * LANES, LANES)] = stage[q, pl.ds(y, 8, stride=16), :].astype(BF)


def v_both(ready, shear, beta_ref, w_ref, cot, h_ref, out, dvert, pay, beta, own, fv, taps, dps, sums, grads, outs, edges, blend, wt):
    shears = shear.shape[0]
    wide = 22
    plane = 10 * wide
    blend[...] = jnp.zeros(blend.shape, F32)
    first8 = low((8, LANES))

    for u in (0, 9):
        sheet = jnp.zeros((wide, 8, LANES), F32)
        for tap in (0, 1, 2) if u == 0 else (6, 7, 8):
            taps[pl.ds(tap * plane + u * wide, wide)] = sheet
        for jk in range(3 * shears):
            dps[pl.ds(jk * plane + u * wide, wide)] = sheet

    @pl.loop(1, 9)
    def _(u):
        rim = jnp.zeros((REACH, 8, LANES), F32)
        for side in (0, 16 + REACH):
            for tap in range(TAPS):
                taps[pl.ds(tap * plane + side + u * wide, REACH)] = rim
            for j in range(3):
                sums[pl.ds(j * plane + side + u * wide, REACH)] = rim
            for jk in range(3 * shears):
                dps[pl.ds(jk * plane + side + u * wide, REACH)] = rim

    ready()
    spread(beta_ref, beta)
    fill_weights(w_ref, wt, 0.5)

    @pl.loop(0, 8, unroll=2)
    def _(u):
        for x in range(8):
            own[u, pl.ds(x * 16, 16), :] = h_ref[u, x].astype(F32)
        for y in range(0, 16, 2):
            pair = [own[u, pl.ds(y + e, 8, stride=16), :] for e in range(2)]
            fv[pl.ds(pl.multiple_of(u * LANES + y * 8, 16), 16), :] = jnp.concatenate(pair, axis=0).astype(BF)
        for q in range(8):
            lanes = pl.ds(pl.multiple_of((u * 8 + q) * LANES, LANES), LANES)
            a, b = cot[0, :, lanes].astype(F32), cot[1, :, lanes].astype(F32)
            grads[u, 2 * q] = jnp.where(first8, a, swap(b))
            grads[u, 2 * q + 1] = jnp.where(first8, swap(a), b)

    @pl.loop(0, 2)
    def _(n):
        rows = pl.ds(pl.multiple_of(n * 512, 512), 512)
        for side in range(3):
            product = mm(fv[rows, :], wt[pl.ds(side * 384, 384), :], NT)
            for j in range(3):
                part = product[:, j * LANES : (j + 1) * LANES].reshape(4, 16, 8, LANES)
                for e in range(4):
                    taps[pl.ds((3 * side + j) * plane + (e + 1) * wide + REACH + n * 4 * wide, 16)] = part[e]

    def body(u, y):
        here = (u + 1) * wide + REACH + y
        g = grads[u, y]
        mid = taps[4 * plane + here]
        left = taps[3 * plane - 1 + here]
        right = taps[5 * plane + 1 + here]
        branch = jnp.zeros((8, LANES), F32)
        total = [jnp.zeros((8, LANES), F32) for _ in range(3)]
        shared = []
        for k in range(shears):
            d = shear[k]
            ys = jnp.full((8, LANES), y - d * (u - 4), jnp.int32)
            keep = ys.astype(jnp.uint32) < 16
            has_minus, has_plus = ys >= 1, ys <= 14
            a, b = here - d, here + d
            main = mid + (taps[plane - wide + a] + taps[7 * plane + wide + b])
            minus = left + (taps[-wide - 1 + a] + taps[6 * plane + wide - 1 + b])
            plus = right + (taps[2 * plane - wide + 1 + a] + taps[8 * plane + wide + 1 + b])
            act, slope = gate(main + jnp.where(has_minus, minus, 0.0) + jnp.where(has_plus, plus, 0.0))
            act = jnp.where(keep, act, 0.0)
            bk = beta[k]
            branch = branch + bk * act
            shared.append(g * act)
            dp = jnp.where(keep, bk * g * slope, 0.0).astype(BF).astype(F32)
            parts = (jnp.where(has_minus, dp, 0.0), dp, jnp.where(has_plus, dp, 0.0))
            for j in range(3):
                dps[(j * shears + k) * plane + here] = parts[j]
                total[j] = total[j] + parts[j]
        for j in range(3):
            sums[j * plane + here] = total[j]
        outs[u, y] = own[u, pl.ds(y, 8, stride=16), :] + branch
        return shared

    @pl.loop(0, 64, unroll=8)
    def _(n):
        u, y = n // 8, (n % 8) * 2
        first, second = body(u, y), body(u, y + 1)
        for k in range(shears):
            blend[k] += first[k] + second[k]

    @pl.loop(0, 64, unroll=4)
    def _(n):
        here = (n // 8 + 1) * wide + REACH + (n % 8) * 2
        at = pl.ds(pl.multiple_of(n * 16, 16), 16)
        below = [jnp.zeros((2, 8, LANES), F32) for _ in range(3)]
        above = [jnp.zeros((2, 8, LANES), F32) for _ in range(3)]
        for k in range(shears):
            d = shear[k]
            up, down = here + d, here - d
            for j in range(3):
                offset = (j * shears + k) * plane - (j - 1)
                below[j] = below[j] + dps[pl.ds(offset + wide + up, 2)]
                above[j] = above[j] + dps[pl.ds(offset - wide + down, 2)]
        for j in range(3):
            middle = sums[pl.ds(j * plane - (j - 1) + here, 2)]
            for side, value in enumerate((below[j], middle, above[j])):
                edges[at, pl.ds((3 * side + j) * LANES, LANES)] = value.reshape(16, LANES).astype(BF)

    pack_grads([mm(fv[...], edges[:, pl.ds(side * 384, 384)], TN) for side in range(3)], blend, pay)

    @pl.loop(0, 2)
    def _(n):
        rows = pl.ds(pl.multiple_of(n * 512, 512), 512)
        back = 2.0 * mm(edges[rows, :], wt[...], NN).reshape(4, LANES, LANES)
        for e in range(4):
            u = 4 * n + e
            own[u] = grads[u].reshape(LANES, LANES) + back[e]
            for x in range(8):
                dvert[u, x] = own[u, pl.ds(x, 16, stride=8), :].astype(BF)
            for q in range(8):
                lanes = pl.ds(pl.multiple_of((u * 8 + q) * LANES, LANES), LANES)
                a, b = outs[u, 2 * q], outs[u, 2 * q + 1]
                out[0, :, lanes] = jnp.where(first8, a, swap(b)).astype(BF)
                out[1, :, lanes] = jnp.where(first8, swap(a), b).astype(BF)


def call(body, fetched, operands, out_shapes, scratch, cost, vmem_mib, far=()):
    vmem = pl.BlockSpec(memory_space=pltpu.VMEM)
    specs = [pl.BlockSpec(memory_space=pltpu.HBM)] * len(fetched)
    specs += [pl.BlockSpec(memory_space=pltpu.SMEM if op.dtype == jnp.int32 else pltpu.VMEM) for op in operands]
    held = [(pltpu.SMEM if op.dtype == jnp.int32 else pltpu.VMEM)(op.shape, op.dtype) for op in fetched]
    count = len(fetched)

    def kernel(*refs):
        sources, others = refs[:count], refs[count : -count - 1]
        targets, sem = refs[-count - 1 : -1], refs[-1]
        copies = [pltpu.make_async_copy(sources[i], targets[i], sem.at[i]) for i in range(count)]
        for copy in copies:
            copy.start()

        def ready():
            for copy in copies:
                copy.wait()

        body(ready, *targets, *others)

    return pl.pallas_call(
        kernel,
        out_shape=out_shapes,
        in_specs=specs,
        out_specs=[pl.BlockSpec(memory_space=pltpu.HBM) if i in far else vmem for i in range(len(out_shapes))],
        scratch_shapes=list(scratch) + held + [pltpu.SemaphoreType.DMA((count,))],
        compiler_params=pltpu.CompilerParams(vmem_limit_bytes=int(vmem_mib * MIB)),
        cost_estimate=pl.CostEstimate(flops=cost, bytes_accessed=4_000_000, transcendentals=1_000_000),
    )(*[pltpu.with_memory_space_constraint(op, pltpu.HBM) for op in fetched], *operands)


def unpack(total, w_h, w_v, b_h, b_v):
    scale = 262144.0**-0.5
    for at, weight, blend in ((0, w_h, b_h), (5 * HALF, w_v, b_v)):
        for pair in range(5):
            block = total[pl.ds(at + pair * HALF, HALF), :] * scale
            weight[2 * pair] = block[:, :HALF]
            other = swap(block)[:, :HALF]
            if pair < 4:
                weight[2 * pair + 1] = other
            else:
                blend[...] = other[: blend.shape[0]]


def reduce_all(pay, zero):
    part = lax.all_to_all(pay.reshape(16, 40, LANES), "img", 0, 0, tiled=True).sum(0) + zero
    part = lax.all_to_all(jnp.broadcast_to(part[None], (8, 40, LANES)), "vrow", 0, 0, tiled=True).sum(0)
    return lax.all_to_all(jnp.broadcast_to(part[None], (16, 40, LANES)), "img", 0, 0, tiled=True).reshape(640, LANES)


def per_device(features, weight_h, weight_v, beta_h, beta_v, shear_set, cotangent):
    shears = shear_set.shape[0]
    img = lax.axis_size("img")
    sds = jax.ShapeDtypeStruct
    own = features.reshape(16, 8, 1024)
    to_right = [(i, i + 1) for i in range(img - 1)]
    to_left = [(i + 1, i) for i in range(img - 1)]
    from_left = lax.ppermute(own, "img", to_right)
    from_right = lax.ppermute(own, "img", to_left)
    base = (lax.axis_index("img") * 8).astype(jnp.int32).reshape(1)
    w_h = jnp.transpose(weight_h, (2, 3, 0, 1)).reshape(TAPS, HALF, HALF)
    w_v = jnp.transpose(weight_v, (2, 3, 0, 1)).reshape(TAPS, HALF, HALF)

    hfeat, pre, taps, f0, fmi, fpl = call(
        h_forward,
        (shear_set, beta_h, w_h, own),
        (base, from_left, from_right),
        [sds((8, 8, 16, LANES), BF), sds((shears * 64, 2, 8, LANES), F32), sds((TAPS * 160, 2, 8, LANES), F32)]
        + [sds((1024, LANES), BF)] * 3,
        [pltpu.VMEM((shears, 8, LANES), F32), pltpu.VMEM((8, 384, LANES), F32)]
        + [pltpu.VMEM((20 * LANES, LANES), BF)] * 3
        + [pltpu.VMEM((TAPS * LANES, LANES), BF)],
        2 * 2560 * LANES * TAPS * LANES,
        GRANT[0],
    )
    moved = lax.all_to_all(hfeat, "vrow", 0, 0, tiled=True)
    slopes, acts = call(
        h_slopes,
        (shear_set, beta_h),
        (base, pre, taps),
        [sds((shears * 112, 2, 8, LANES), F32), sds((shears * 64, 2, 8, LANES), F32)],
        [pltpu.VMEM((shears, 8, LANES), F32)],
        1_000_000,
        GRANT[3],
    )
    output, dvert, pay_v = call(
        v_both,
        (shear_set, beta_v, w_v, cotangent),
        (moved,),
        [sds((2, 8, 8192), BF), sds((8, 8, 16, LANES), BF), sds((320, LANES), F32)],
        [
            pltpu.VMEM((shears, 8, LANES), F32),
            pltpu.VMEM((8, LANES, LANES), F32),
            pltpu.VMEM((1024, LANES), BF),
            pltpu.VMEM((TAPS * 220, 8, LANES), F32),
            pltpu.VMEM((3 * shears * 220, 8, LANES), F32),
            pltpu.VMEM((3 * 220, 8, LANES), F32),
            pltpu.VMEM((8, 16, 8, LANES), F32),
            pltpu.VMEM((8, 16, 8, LANES), F32),
            pltpu.VMEM((1024, TAPS * LANES), BF),
            pltpu.VMEM((shears, 8, LANES), F32),
            pltpu.VMEM((TAPS * LANES, LANES), BF),
        ],
        6 * 1024 * LANES * TAPS * LANES,
        GRANT[1],
    )
    grad = lax.all_to_all(dvert, "vrow", 0, 0, tiled=True)
    grad_right = lax.ppermute(grad[:, :REACH], "img", to_left)
    grad_left = lax.ppermute(grad[:, 8 - REACH :], "img", to_right)
    pay, edges_h = call(
        h_backward,
        (shear_set,),
        (base, slopes, acts, f0, fmi, fpl, grad, grad_left, grad_right, pay_v),
        [sds((640, LANES), F32), pltpu.HBM((3, 1024, 384), BF)],
        [
            pltpu.VMEM((3 * shears * 112, 2, 8, LANES), F32),
            pltpu.VMEM((3 * 112, 2, 8, LANES), F32),
            pltpu.VMEM((3, 1024, 384), BF),
            pltpu.VMEM((shears, 8, LANES), F32),
            pltpu.SemaphoreType.DMA,
        ],
        2 * 1024 * LANES * TAPS * LANES,
        GRANT[2],
        (1,),
    )
    grad_features, finished = call(
        h_finish,
        (w_h, edges_h, grad),
        (),
        [sds((16, 8, 1024), BF), sds((40, LANES), F32)],
        [
            pltpu.VMEM((3, 1024, LANES), F32),
            pltpu.VMEM((8, LANES, LANES), F32),
            pltpu.VMEM((TAPS * LANES, LANES), BF),
        ],
        2 * 1024 * LANES * TAPS * LANES,
        GRANT[4],
    )
    vmem = pl.BlockSpec(memory_space=pltpu.VMEM)
    weights = sds((TAPS, HALF, HALF), F32)
    w_grad_h, w_grad_v, beta_grad_h, beta_grad_v = pl.pallas_call(
        unpack,
        out_shape=[weights, weights] + [sds((shears, HALF), F32)] * 2,
        in_specs=[vmem],
        out_specs=[vmem] * 4,
    )(reduce_all(pay, finished))

    def placed(weight):
        return jnp.transpose(weight.reshape(3, 3, HALF, HALF), (2, 3, 0, 1))

    return output, grad_features.reshape(features.shape), placed(w_grad_h), placed(w_grad_v), beta_grad_h, beta_grad_v


def solution(mesh):
    placed = (P("vrow", None, "img", None), P(), P(), P(), P(), P(), P("vrow", "img", None))
    return jax.shard_map(
        per_device,
        mesh=mesh,
        in_specs=placed,
        out_specs=(P("vrow", "img", None), P("vrow", None, "img", None), P(), P(), P(), P()),
        check_vma=False,
    )
```

```python
import jax
import jax.numpy as jnp
from jax import lax
from jax.experimental import pallas as pl
from jax.experimental.pallas import tpu as pltpu
from jax.sharding import PartitionSpec as P


BF = jnp.bfloat16
F32 = jnp.float32
LANES = 128
HALF = 64
TAPS = 9
REACH = 3
WIDE = 8 + 2 * REACH
PLANE = WIDE * 8
MIB = 1024 * 1024
GRANT = (26, 36, 34, 20, 12)
NT = (((1,), (1,)), ((), ()))
NN = (((1,), (0,)), ((), ()))
TN = (((0,), (0,)), ((), ()))


def mm(lhs, rhs, dims):
    return lax.dot_general(lhs, rhs, dims, preferred_element_type=F32)


def lanes_of(shape):
    return lax.broadcasted_iota(jnp.int32, shape, len(shape) - 1)


def swap(value):
    return pltpu.roll(value, HALF, axis=value.ndim - 1)


def low(shape):
    return lanes_of(shape) < HALF


def fill_weights(w_ref, wt_ref, scale=1.0):
    zero = jnp.zeros((HALF, HALF), BF)
    for tap in range(TAPS):
        w = w_ref[tap]
        if scale != 1.0:
            w = (w.astype(F32) * scale).astype(BF)
        wt_ref[pl.ds(tap * LANES, HALF), :] = jnp.concatenate([w, zero], axis=1)
        wt_ref[pl.ds(tap * LANES + HALF, HALF), :] = jnp.concatenate([zero, w], axis=1)


def spread(beta_ref, beta):
    for k in range(beta.shape[0]):
        line = beta_ref[pl.ds(k, 1), :]
        beta[k] = jnp.broadcast_to(jnp.concatenate([line, line], axis=1), (8, LANES))


def pack_grads(grads, blend_ref, pay_ref):
    first = low((HALF, LANES))
    rows = lax.broadcasted_iota(jnp.int32, (HALF, LANES), 0)
    blend = jnp.zeros((HALF, LANES), F32)
    for k in range(blend_ref.shape[0]):
        line = jnp.sum(blend_ref[k], axis=0, keepdims=True)
        blend = blend + jnp.where(rows == k, line + swap(line), 0.0)

    def tap_of(tap):
        block = grads[tap // 3][:, (tap % 3) * LANES : (tap % 3 + 1) * LANES]
        return block[:HALF] + swap(block[HALF:])

    for pair in range(5):
        even = tap_of(2 * pair)
        odd = tap_of(2 * pair + 1) if pair < 4 else even
        both = jnp.transpose(jnp.where(first, even, swap(odd)))
        value = jnp.concatenate([both[:HALF], both[HALF:]], axis=1)
        if pair == 4:
            value = jnp.where(first, value, blend)
        pay_ref[pl.ds(pair * HALF, HALF), :] = value


def gate(h):
    t = jnp.tanh(h) + 1.0
    s = 0.5 * t
    act = h * t
    return act, s + act * (1.0 - s)


def halves():
    return (lanes_of((1, 8, LANES)) >= HALF).astype(jnp.int32)


def h_forward(ready, shear, beta_ref, w_ref, fm, base, fl, fr, hfeat, pre_ref, f0, fmi, fpl, beta, stage, taps, wt):
    shears = shear.shape[0]
    ready()
    spread(beta_ref, beta)
    fill_weights(w_ref, wt, 0.5)
    first16 = low((16, LANES))

    @pl.loop(0, 16, unroll=2)
    def _(y):
        for part, ref in enumerate((fl, fm, fr)):
            for q in range(8):
                stage[q, pl.ds(y * 24 + 8 * part, 8), :] = ref[y, :, pl.ds(q * LANES, LANES)].astype(F32)

    @pl.loop(0, WIDE, unroll=2)
    def _(x):
        own = [stage[q, pl.ds(x + 8 - REACH, 16, stride=24), :] for q in range(8)]
        turned = [swap(a) for a in own]
        zero = jnp.zeros((16, LANES), F32)
        moved = [
            jnp.where(first16, turned[q - 1] if q > 0 else zero, turned[q] if q < 8 else zero).astype(BF)
            for q in range(9)
        ]
        for q in range(8):
            at = pl.ds(pl.multiple_of(x * LANES + q * 16, 16), 16)
            f0[at, :] = own[q].astype(BF)
            fmi[at, :] = moved[q]
            fpl[at, :] = moved[q + 1]

    @pl.loop(0, 4)
    def _(n):
        at = pl.ds(pl.multiple_of(n * 448, 448), 448)
        for side, ref in enumerate((fmi, f0, fpl)):
            product = mm(ref[at, :], wt[pl.ds(side * 384, 384), :], NT)
            for j in range(3):
                part = product[:, j * LANES : (j + 1) * LANES].reshape(28, 2, 8, LANES)
                taps[pl.ds((3 * side + j) * PLANE + n * 28, 28)] = part

    half = halves()

    @pl.loop(0, 64, unroll=8)
    def _(n):
        q = n % 8
        here = n + REACH * 8
        vrel = half + (2 * q - 8)
        xg = base[0] + n // 8
        mid = taps[4 * PLANE + here]
        left = taps[3 * PLANE - 8 + here]
        right = taps[5 * PLANE + 8 + here]
        branch = jnp.zeros((2, 8, LANES), F32)
        for k in range(shears):
            d = shear[k]
            xs = xg - d * vrel
            a, b = here - d * 8, here + d * 8
            main = mid + (taps[PLANE + a] + taps[7 * PLANE + b])
            minus = left + (taps[a - 8] + taps[6 * PLANE - 8 + b])
            plus = right + (taps[2 * PLANE + 8 + a] + taps[8 * PLANE + 8 + b])
            pre = main + jnp.where(xs >= 1, minus, 0.0) + jnp.where(xs <= LANES - 2, plus, 0.0)
            pre_ref[k * 64 + n] = pre
            keep = xs.astype(jnp.uint32) < LANES
            branch = branch + jnp.where(keep, beta[k] * gate(pre)[0], 0.0)
        own = f0[pl.ds(pl.multiple_of(here * 16, 16), 16), :].astype(F32)
        hfeat[q, n // 8] = (own + branch.reshape(16, LANES)).astype(BF)


def h_backward(ready, shear, beta_ref, base, pre_ref, f0, fmi, fpl, gm, pay_v, pay, out0, out1, out2, beta, dps, sums, edges, blend, edges_sem):
    shears = shear.shape[0]
    ready()
    spread(beta_ref, beta)
    half = halves()
    blend[...] = jnp.zeros(blend.shape, F32)
    for gap in range(3 * shears + 1):
        dps[pl.ds(gap * PLANE, 48)] = jnp.zeros((48, 2, 8, LANES), F32)
    for gap in range(4):
        sums[pl.ds(gap * 96, 32)] = jnp.zeros((32, 2, 8, LANES), F32)

    @pl.loop(0, 64, unroll=8)
    def _(n):
        x, q = n // 8, n % 8
        g = gm[q, x].astype(F32).reshape(2, 8, LANES)
        vrel = half + (2 * q - 8)
        xg = base[0] + x
        total = [jnp.zeros((2, 8, LANES), F32) for _ in range(3)]
        for k in range(shears):
            xs = xg - shear[k] * vrel
            act, slope = gate(pre_ref[k * 64 + n])
            gk = jnp.where(xs.astype(jnp.uint32) < LANES, g, 0.0)
            dp = (beta[k] * gk * slope).astype(BF).astype(F32)
            parts = (jnp.where(xs >= 1, dp, 0.0), dp, jnp.where(xs <= LANES - 2, dp, 0.0))
            for j in range(3):
                dps[(j * shears + k) * PLANE + 48 + n] = parts[j]
                total[j] = total[j] + parts[j]
            blend[k] += jnp.sum(gk * act, axis=0)
        for j in range(3):
            sums[j * 96 + 32 + n] = total[j]

    @pl.loop(0, WIDE * 8, unroll=8)
    def _(n):
        at = pl.ds(pl.multiple_of(n * 16, 16), 16)
        below = [jnp.zeros((2, 8, LANES), F32) for _ in range(3)]
        above = [jnp.zeros((2, 8, LANES), F32) for _ in range(3)]
        for k in range(shears):
            d = shear[k]
            up, down = n + d * 8, n - d * 8
            for j in range(3):
                offset = (j * shears + k) * PLANE + 48 - REACH * 8 - (j - 1) * 8
                below[j] = below[j] + dps[offset + up]
                above[j] = above[j] + dps[offset + down]
        for j in range(3):
            lanes = pl.ds(j * LANES, LANES)
            middle = sums[j * 96 + 32 - REACH * 8 - (j - 1) * 8 + n]
            for side, value in enumerate((below[j], middle, above[j])):
                edges[side, at, lanes] = value.reshape(16, LANES).astype(BF)

    copies = [pltpu.make_async_copy(edges.at[i], out, edges_sem.at[i]) for i, out in enumerate((out0, out1, out2))]
    for copy in copies:
        copy.start()
    pack_grads([mm(ref[...], edges[side], TN) for side, ref in enumerate((fmi, f0, fpl))], blend, pay)
    pay[pl.ds(5 * HALF, 5 * HALF), :] = pay_v[...]
    for copy in copies:
        copy.wait()


def h_inputs(ready, w_ref, edges0, edges1, edges2, own, to_left, to_right, token, dfs, wt):
    token[...] = jnp.zeros(token.shape, F32)
    ready(0)
    fill_weights(w_ref, wt)
    for side, edges in enumerate((edges0, edges1, edges2)):
        ready(side + 1)

        @pl.loop(0, 4)
        def _(n):
            at = pl.ds(pl.multiple_of(n * 448, 448), 448)
            dfs[side, at, :] = mm(edges[at, :], wt[pl.ds(side * 384, 384), :], NN)

    first16 = low((16, LANES))

    def column(x, out, at):
        def piece(side, q):
            if q < 0 or q > 7:
                return jnp.zeros((16, LANES), F32)
            return dfs[side, pl.ds(pl.multiple_of(x * LANES + q * 16, 16), 16), :]

        for q in range(8):
            upper = piece(0, q) + piece(2, q - 1)
            lower = piece(0, q + 1) + piece(2, q)
            out[at, q] = piece(1, q) + swap(jnp.where(first16, lower, upper))

    for x in range(REACH):
        column(x, to_left, x)
        column(x + 8 + REACH, to_right, x)

    @pl.loop(0, 8)
    def _(x):
        column(x + REACH, own, x)


def h_finish(ready, own, gm, from_left, from_right, out, stage):
    ready()
    for x in range(8):
        for q in range(8):
            total = gm[q, x].astype(F32) + own[x, q]
            if x < REACH:
                total = total + from_left[x, q]
            if x >= 8 - REACH:
                total = total + from_right[x - 8 + REACH, q]
            stage[q, pl.ds(x * 16, 16), :] = total

    @pl.loop(0, 16, unroll=2)
    def _(y):
        for q in range(8):
            out[y, :, pl.ds(q * LANES, LANES)] = stage[q, pl.ds(y, 8, stride=16), :].astype(BF)


def v_both(ready, shear, beta_ref, w_ref, cot, h_ref, out, dvert, pay, beta, own, fv, taps, dps, sums, grads, outs, edges, blend, wt):
    shears = shear.shape[0]
    wide = 22
    plane = 10 * wide
    blend[...] = jnp.zeros(blend.shape, F32)
    first8 = low((8, LANES))

    for u in (0, 9):
        sheet = jnp.zeros((wide, 8, LANES), F32)
        for tap in (0, 1, 2) if u == 0 else (6, 7, 8):
            taps[pl.ds(tap * plane + u * wide, wide)] = sheet
        for jk in range(3 * shears):
            dps[pl.ds(jk * plane + u * wide, wide)] = sheet

    @pl.loop(1, 9)
    def _(u):
        rim = jnp.zeros((REACH, 8, LANES), F32)
        for side in (0, 16 + REACH):
            for tap in range(TAPS):
                taps[pl.ds(tap * plane + side + u * wide, REACH)] = rim
            for j in range(3):
                sums[pl.ds(j * plane + side + u * wide, REACH)] = rim
            for jk in range(3 * shears):
                dps[pl.ds(jk * plane + side + u * wide, REACH)] = rim

    ready()
    spread(beta_ref, beta)
    fill_weights(w_ref, wt, 0.5)

    @pl.loop(0, 8, unroll=2)
    def _(u):
        for x in range(8):
            own[u, pl.ds(x * 16, 16), :] = h_ref[u, x].astype(F32)
        for y in range(0, 16, 2):
            pair = [own[u, pl.ds(y + e, 8, stride=16), :] for e in range(2)]
            fv[pl.ds(pl.multiple_of(u * LANES + y * 8, 16), 16), :] = jnp.concatenate(pair, axis=0).astype(BF)
        for q in range(8):
            lanes = pl.ds(pl.multiple_of((u * 8 + q) * LANES, LANES), LANES)
            a, b = cot[0, :, lanes].astype(F32), cot[1, :, lanes].astype(F32)
            grads[u, 2 * q] = jnp.where(first8, a, swap(b))
            grads[u, 2 * q + 1] = jnp.where(first8, swap(a), b)

    @pl.loop(0, 2)
    def _(n):
        rows = pl.ds(pl.multiple_of(n * 512, 512), 512)
        for side in range(3):
            product = mm(fv[rows, :], wt[pl.ds(side * 384, 384), :], NT)
            for j in range(3):
                part = product[:, j * LANES : (j + 1) * LANES].reshape(4, 16, 8, LANES)
                for e in range(4):
                    taps[pl.ds((3 * side + j) * plane + (e + 1) * wide + REACH + n * 4 * wide, 16)] = part[e]

    def body(u, y):
        here = (u + 1) * wide + REACH + y
        g = grads[u, y]
        mid = taps[4 * plane + here]
        left = taps[3 * plane - 1 + here]
        right = taps[5 * plane + 1 + here]
        branch = jnp.zeros((8, LANES), F32)
        total = [jnp.zeros((8, LANES), F32) for _ in range(3)]
        shared = []
        for k in range(shears):
            d = shear[k]
            ys = jnp.full((8, LANES), y - d * (u - 4), jnp.int32)
            keep = ys.astype(jnp.uint32) < 16
            has_minus, has_plus = ys >= 1, ys <= 14
            a, b = here - d, here + d
            main = mid + (taps[plane - wide + a] + taps[7 * plane + wide + b])
            minus = left + (taps[-wide - 1 + a] + taps[6 * plane + wide - 1 + b])
            plus = right + (taps[2 * plane - wide + 1 + a] + taps[8 * plane + wide + 1 + b])
            act, slope = gate(main + jnp.where(has_minus, minus, 0.0) + jnp.where(has_plus, plus, 0.0))
            act = jnp.where(keep, act, 0.0)
            bk = beta[k]
            branch = branch + bk * act
            shared.append(g * act)
            dp = jnp.where(keep, bk * g * slope, 0.0).astype(BF).astype(F32)
            parts = (jnp.where(has_minus, dp, 0.0), dp, jnp.where(has_plus, dp, 0.0))
            for j in range(3):
                dps[(j * shears + k) * plane + here] = parts[j]
                total[j] = total[j] + parts[j]
        for j in range(3):
            sums[j * plane + here] = total[j]
        outs[u, y] = own[u, pl.ds(y, 8, stride=16), :] + branch
        return shared

    @pl.loop(0, 64, unroll=8)
    def _(n):
        u, y = n // 8, (n % 8) * 2
        first, second = body(u, y), body(u, y + 1)
        for k in range(shears):
            blend[k] += first[k] + second[k]

    @pl.loop(0, 64, unroll=4)
    def _(n):
        here = (n // 8 + 1) * wide + REACH + (n % 8) * 2
        at = pl.ds(pl.multiple_of(n * 16, 16), 16)
        below = [jnp.zeros((2, 8, LANES), F32) for _ in range(3)]
        above = [jnp.zeros((2, 8, LANES), F32) for _ in range(3)]
        for k in range(shears):
            d = shear[k]
            up, down = here + d, here - d
            for j in range(3):
                offset = (j * shears + k) * plane - (j - 1)
                below[j] = below[j] + dps[pl.ds(offset + wide + up, 2)]
                above[j] = above[j] + dps[pl.ds(offset - wide + down, 2)]
        for j in range(3):
            middle = sums[pl.ds(j * plane - (j - 1) + here, 2)]
            for side, value in enumerate((below[j], middle, above[j])):
                edges[at, pl.ds((3 * side + j) * LANES, LANES)] = value.reshape(16, LANES).astype(BF)

    pack_grads([mm(fv[...], edges[:, pl.ds(side * 384, 384)], TN) for side in range(3)], blend, pay)

    @pl.loop(0, 2)
    def _(n):
        rows = pl.ds(pl.multiple_of(n * 512, 512), 512)
        back = 2.0 * mm(edges[rows, :], wt[...], NN).reshape(4, LANES, LANES)
        for e in range(4):
            u = 4 * n + e
            own[u] = grads[u].reshape(LANES, LANES) + back[e]
            for x in range(8):
                dvert[u, x] = own[u, pl.ds(x, 16, stride=8), :].astype(BF)
            for q in range(8):
                lanes = pl.ds(pl.multiple_of((u * 8 + q) * LANES, LANES), LANES)
                a, b = outs[u, 2 * q], outs[u, 2 * q + 1]
                out[0, :, lanes] = jnp.where(first8, a, swap(b)).astype(BF)
                out[1, :, lanes] = jnp.where(first8, swap(a), b).astype(BF)


def call(body, fetched, operands, out_shapes, scratch, cost, vmem_mib, far=()):
    vmem = pl.BlockSpec(memory_space=pltpu.VMEM)
    specs = [pl.BlockSpec(memory_space=pltpu.HBM)] * len(fetched)
    specs += [pl.BlockSpec(memory_space=pltpu.SMEM if op.dtype == jnp.int32 else pltpu.VMEM) for op in operands]
    held = [(pltpu.SMEM if op.dtype == jnp.int32 else pltpu.VMEM)(op.shape, op.dtype) for op in fetched]
    count = len(fetched)

    def kernel(*refs):
        sources, others = refs[:count], refs[count : -count - 1]
        targets, sem = refs[-count - 1 : -1], refs[-1]
        copies = [pltpu.make_async_copy(sources[i], targets[i], sem.at[i]) for i in range(count)]
        for copy in copies:
            copy.start()

        def ready(*which):
            for i in which or range(count):
                copies[i].wait()

        body(ready, *targets, *others)

    return pl.pallas_call(
        kernel,
        out_shape=out_shapes,
        in_specs=specs,
        out_specs=[pl.BlockSpec(memory_space=pltpu.HBM) if i in far else vmem for i in range(len(out_shapes))],
        scratch_shapes=list(scratch) + held + [pltpu.SemaphoreType.DMA((count,))],
        compiler_params=pltpu.CompilerParams(vmem_limit_bytes=int(vmem_mib * MIB)),
        cost_estimate=pl.CostEstimate(flops=cost, bytes_accessed=4_000_000, transcendentals=1_000_000),
    )(*[pltpu.with_memory_space_constraint(op, pltpu.HBM) for op in fetched], *operands)


def unpack(total, w_h, w_v, b_h, b_v):
    scale = 262144.0**-0.5
    for at, weight, blend in ((0, w_h, b_h), (5 * HALF, w_v, b_v)):
        for pair in range(5):
            block = total[pl.ds(at + pair * HALF, HALF), :] * scale
            weight[2 * pair] = block[:, :HALF]
            other = swap(block)[:, :HALF]
            if pair < 4:
                weight[2 * pair + 1] = other
            else:
                blend[...] = other[: blend.shape[0]]


def reduce_all(pay, zero):
    part = lax.all_to_all(pay.reshape(16, 40, LANES), "img", 0, 0, tiled=True)
    part = jnp.broadcast_to((part.sum(0) + zero)[None], (8, 40, LANES))
    part = lax.all_to_all(part, "vrow", 0, 0, tiled=True)
    part = jnp.broadcast_to(part.sum(0)[None], (16, 40, LANES))
    return lax.all_to_all(part, "img", 0, 0, tiled=True).reshape(640, LANES)


def whole_step(features, weight_h, weight_v, beta_h, beta_v, shear_set, cotangent):
    shears = shear_set.shape[0]
    img = lax.axis_size("img")
    sds = jax.ShapeDtypeStruct
    own = features.reshape(16, 8, 1024)
    to_right = [(i, i + 1) for i in range(img - 1)]
    to_left = [(i + 1, i) for i in range(img - 1)]
    from_left = lax.ppermute(own, "img", to_right)
    from_right = lax.ppermute(own, "img", to_left)
    base = (lax.axis_index("img") * 8).astype(jnp.int32).reshape(1)
    w_h = jnp.transpose(weight_h, (2, 3, 0, 1)).reshape(TAPS, HALF, HALF)
    w_v = jnp.transpose(weight_v, (2, 3, 0, 1)).reshape(TAPS, HALF, HALF)

    hfeat, pre, f0, fmi, fpl = call(
        h_forward,
        (shear_set, beta_h, w_h, own),
        (base, from_left, from_right),
        [sds((8, 8, 16, LANES), BF), sds((shears * 64, 2, 8, LANES), F32)] + [sds((WIDE * LANES, LANES), BF)] * 3,
        [
            pltpu.VMEM((shears, 8, LANES), F32),
            pltpu.VMEM((8, 384, LANES), F32),
            pltpu.VMEM((TAPS * PLANE, 2, 8, LANES), F32),
            pltpu.VMEM((TAPS * LANES, LANES), BF),
        ],
        2 * WIDE * LANES * LANES * TAPS * LANES,
        GRANT[0],
    )
    moved = lax.all_to_all(hfeat, "vrow", 0, 0, tiled=True)
    output, dvert, pay_v = call(
        v_both,
        (shear_set, beta_v, w_v, cotangent),
        (moved,),
        [sds((2, 8, 8192), BF), sds((8, 8, 16, LANES), BF), sds((320, LANES), F32)],
        [
            pltpu.VMEM((shears, 8, LANES), F32),
            pltpu.VMEM((8, LANES, LANES), F32),
            pltpu.VMEM((1024, LANES), BF),
            pltpu.VMEM((TAPS * 220, 8, LANES), F32),
            pltpu.VMEM((3 * shears * 220, 8, LANES), F32),
            pltpu.VMEM((3 * 220, 8, LANES), F32),
            pltpu.VMEM((8, 16, 8, LANES), F32),
            pltpu.VMEM((8, 16, 8, LANES), F32),
            pltpu.VMEM((1024, TAPS * LANES), BF),
            pltpu.VMEM((shears, 8, LANES), F32),
            pltpu.VMEM((TAPS * LANES, LANES), BF),
        ],
        6 * 1024 * LANES * TAPS * LANES,
        GRANT[1],
    )
    grad = lax.all_to_all(dvert, "vrow", 0, 0, tiled=True)
    pay, *edges_h = call(
        h_backward,
        (shear_set, beta_h),
        (base, pre, f0, fmi, fpl, grad, pay_v),
        [sds((640, LANES), F32)] + [pltpu.HBM((WIDE * LANES, 384), BF)] * 3,
        [
            pltpu.VMEM((shears, 8, LANES), F32),
            pltpu.VMEM((3 * shears * PLANE + 48, 2, 8, LANES), F32),
            pltpu.VMEM((3 * 96 + 32, 2, 8, LANES), F32),
            pltpu.VMEM((3, WIDE * LANES, 384), BF),
            pltpu.VMEM((shears, 8, LANES), F32),
            pltpu.SemaphoreType.DMA((3,)),
        ],
        2 * WIDE * LANES * LANES * TAPS * LANES,
        GRANT[2],
        (1, 2, 3),
    )
    back, halo_left, halo_right, inputs_done = call(
        h_inputs,
        (w_h, *edges_h),
        (),
        [pltpu.HBM((8, 8, 16, LANES), F32)] + [pltpu.HBM((REACH, 8, 16, LANES), F32)] * 2 + [sds((40, LANES), F32)],
        [pltpu.VMEM((3, WIDE * LANES, LANES), F32), pltpu.VMEM((TAPS * LANES, LANES), BF)],
        2 * WIDE * LANES * LANES * TAPS * LANES,
        GRANT[3],
    )
    halo_from_right = lax.ppermute(halo_left, "img", to_left)
    halo_from_left = lax.ppermute(halo_right, "img", to_right)
    (grad_features,) = call(
        h_finish,
        (back, grad),
        (halo_from_left, halo_from_right),
        [sds((16, 8, 1024), BF)],
        [pltpu.VMEM((8, LANES, LANES), F32)],
        1_000_000,
        GRANT[4],
    )
    vmem = pl.BlockSpec(memory_space=pltpu.VMEM)
    weights = sds((TAPS, HALF, HALF), F32)
    w_grad_h, w_grad_v, beta_grad_h, beta_grad_v = pl.pallas_call(
        unpack,
        out_shape=[weights, weights] + [sds((shears, HALF), F32)] * 2,
        in_specs=[vmem],
        out_specs=[vmem] * 4,
        compiler_params=pltpu.CompilerParams(vmem_limit_bytes=6 * MIB),
    )(reduce_all(pay, inputs_done))

    def placed(weight):
        return jnp.transpose(weight.reshape(3, 3, HALF, HALF), (2, 3, 0, 1))

    return output, grad_features.reshape(features.shape), placed(w_grad_h), placed(w_grad_v), beta_grad_h, beta_grad_v


def solution(mesh):
    placed = (P("vrow", None, "img", None), P(), P(), P(), P(), P(), P("vrow", "img", None))
    return jax.shard_map(
        whole_step,
        mesh=mesh,
        in_specs=placed,
        out_specs=(P("vrow", "img", None), P("vrow", None, "img", None), P(), P(), P(), P()),
        check_vma=False,
    )
```

```python
import jax
import jax.numpy as jnp
from jax import lax
from jax.experimental import pallas as pl
from jax.experimental.pallas import tpu as pltpu
from jax.sharding import PartitionSpec as P


BF = jnp.bfloat16
F32 = jnp.float32
LANES = 128
HALF = 64
TAPS = 9
REACH = 3
WIDE = 8 + 2 * REACH
PLANE = WIDE * 8
MIB = 1024 * 1024
GRANT = (26, 36, 34, 20, 12)
NT = (((1,), (1,)), ((), ()))
NN = (((1,), (0,)), ((), ()))
TN = (((0,), (0,)), ((), ()))


def mm(lhs, rhs, dims):
    return lax.dot_general(lhs, rhs, dims, preferred_element_type=F32)


def lanes_of(shape):
    return lax.broadcasted_iota(jnp.int32, shape, len(shape) - 1)


def swap(value):
    return pltpu.roll(value, HALF, axis=value.ndim - 1)


def low(shape):
    return lanes_of(shape) < HALF


def fill_weights(w_ref, wt_ref, scale=1.0):
    zero = jnp.zeros((HALF, HALF), BF)
    for tap in range(TAPS):
        w = w_ref[tap]
        if scale != 1.0:
            w = (w.astype(F32) * scale).astype(BF)
        wt_ref[pl.ds(tap * LANES, HALF), :] = jnp.concatenate([w, zero], axis=1)
        wt_ref[pl.ds(tap * LANES + HALF, HALF), :] = jnp.concatenate([zero, w], axis=1)


def spread(beta_ref, beta):
    for k in range(beta.shape[0]):
        line = beta_ref[pl.ds(k, 1), :]
        beta[k] = jnp.broadcast_to(jnp.concatenate([line, line], axis=1), (8, LANES))


def pack_grads(grads, blend_ref, pay_ref):
    first = low((HALF, LANES))
    rows = lax.broadcasted_iota(jnp.int32, (HALF, LANES), 0)
    blend = jnp.zeros((HALF, LANES), F32)
    for k in range(blend_ref.shape[0]):
        line = jnp.sum(blend_ref[k], axis=0, keepdims=True)
        blend = blend + jnp.where(rows == k, line + swap(line), 0.0)

    def tap_of(tap):
        block = grads[tap // 3][:, (tap % 3) * LANES : (tap % 3 + 1) * LANES]
        return block[:HALF] + swap(block[HALF:])

    for pair in range(5):
        even = tap_of(2 * pair)
        odd = tap_of(2 * pair + 1) if pair < 4 else even
        both = jnp.transpose(jnp.where(first, even, swap(odd)))
        value = jnp.concatenate([both[:HALF], both[HALF:]], axis=1)
        if pair == 4:
            value = jnp.where(first, value, blend)
        pay_ref[pl.ds(pair * HALF, HALF), :] = value


def gate(h):
    t = jnp.tanh(h) + 1.0
    s = 0.5 * t
    act = h * t
    return act, s + act * (1.0 - s)


def halves():
    return (lanes_of((1, 8, LANES)) >= HALF).astype(jnp.int32)


def h_forward(ready, shear, beta_ref, w_ref, fm, base, fl, fr, hfeat, pre_ref, f0, fmi, fpl, beta, stage, taps, wt):
    shears = shear.shape[0]
    ready()
    spread(beta_ref, beta)
    fill_weights(w_ref, wt, 0.5)
    first16 = low((16, LANES))

    @pl.loop(0, 16, unroll=2)
    def _(y):
        for start, rows, ref in ((4, 4, fl), (8, 8, fm), (16, 4, fr)):
            for q in range(8):
                stage[q, pl.ds(y * 24 + start, rows), :] = ref[y, :, pl.ds(q * LANES, LANES)].astype(F32)

    @pl.loop(0, WIDE, unroll=2)
    def _(x):
        own = [stage[q, pl.ds(x + 8 - REACH, 16, stride=24), :] for q in range(8)]
        turned = [swap(a) for a in own]
        zero = jnp.zeros((16, LANES), F32)
        moved = [
            jnp.where(first16, turned[q - 1] if q > 0 else zero, turned[q] if q < 8 else zero).astype(BF)
            for q in range(9)
        ]
        for q in range(8):
            at = pl.ds(pl.multiple_of(x * LANES + q * 16, 16), 16)
            f0[at, :] = own[q].astype(BF)
            fmi[at, :] = moved[q]
            fpl[at, :] = moved[q + 1]

    @pl.loop(0, 4)
    def _(n):
        at = pl.ds(pl.multiple_of(n * 448, 448), 448)
        for side, ref in enumerate((fmi, f0, fpl)):
            product = mm(ref[at, :], wt[pl.ds(side * 384, 384), :], NT)
            for j in range(3):
                part = product[:, j * LANES : (j + 1) * LANES].reshape(28, 2, 8, LANES)
                taps[pl.ds((3 * side + j) * PLANE + n * 28, 28)] = part

    half = halves()

    @pl.loop(0, 64, unroll=8)
    def _(n):
        q = n % 8
        here = n + REACH * 8
        vrel = half + (2 * q - 8)
        xg = base[0] + n // 8
        mid = taps[4 * PLANE + here]
        left = taps[3 * PLANE - 8 + here]
        right = taps[5 * PLANE + 8 + here]
        branch = jnp.zeros((2, 8, LANES), F32)
        for k in range(shears):
            d = shear[k]
            xs = xg - d * vrel
            a, b = here - d * 8, here + d * 8
            main = mid + (taps[PLANE + a] + taps[7 * PLANE + b])
            minus = left + (taps[a - 8] + taps[6 * PLANE - 8 + b])
            plus = right + (taps[2 * PLANE + 8 + a] + taps[8 * PLANE + 8 + b])
            pre = main + jnp.where(xs >= 1, minus, 0.0) + jnp.where(xs <= LANES - 2, plus, 0.0)
            pre_ref[k * 64 + n] = pre
            keep = xs.astype(jnp.uint32) < LANES
            branch = branch + jnp.where(keep, beta[k] * gate(pre)[0], 0.0)
        own = f0[pl.ds(pl.multiple_of(here * 16, 16), 16), :].astype(F32)
        hfeat[q, n // 8] = (own + branch.reshape(16, LANES)).astype(BF)


def h_backward(ready, shear, beta_ref, base, pre_ref, f0, fmi, fpl, gm, pay_v, pay, out0, out1, out2, beta, dps, sums, edges, blend, edges_sem):
    shears = shear.shape[0]
    ready()
    spread(beta_ref, beta)
    half = halves()
    blend[...] = jnp.zeros(blend.shape, F32)

    @pl.loop(0, 64, unroll=8)
    def _(n):
        dps[pl.ds((n // 4) * PLANE + (n % 4) * 12, 12)] = jnp.zeros((12, 2, 8, LANES), F32)
        sums[pl.ds((n // 16) * 96 + (n % 16) * 2, 2)] = jnp.zeros((2, 2, 8, LANES), F32)
        x, q = n // 8, n % 8
        g = gm[q, x].astype(F32).reshape(2, 8, LANES)
        vrel = half + (2 * q - 8)
        xg = base[0] + x
        total = [jnp.zeros((2, 8, LANES), F32) for _ in range(3)]
        for k in range(shears):
            xs = xg - shear[k] * vrel
            act, slope = gate(pre_ref[k * 64 + n])
            gk = jnp.where(xs.astype(jnp.uint32) < LANES, g, 0.0)
            dp = (beta[k] * gk * slope).astype(BF).astype(F32)
            parts = (jnp.where(xs >= 1, dp, 0.0), dp, jnp.where(xs <= LANES - 2, dp, 0.0))
            for j in range(3):
                dps[(j * shears + k) * PLANE + 48 + n] = parts[j]
                total[j] = total[j] + parts[j]
            blend[k] += jnp.sum(gk * act, axis=0)
        for j in range(3):
            sums[j * 96 + 32 + n] = total[j]

    @pl.loop(0, WIDE * 8, unroll=8)
    def _(n):
        at = pl.ds(pl.multiple_of(n * 16, 16), 16)
        below = [jnp.zeros((2, 8, LANES), F32) for _ in range(3)]
        above = [jnp.zeros((2, 8, LANES), F32) for _ in range(3)]
        for k in range(shears):
            d = shear[k]
            up, down = n + d * 8, n - d * 8
            for j in range(3):
                offset = (j * shears + k) * PLANE + 48 - REACH * 8 - (j - 1) * 8
                below[j] = below[j] + dps[offset + up]
                above[j] = above[j] + dps[offset + down]
        for j in range(3):
            lanes = pl.ds(j * LANES, LANES)
            middle = sums[j * 96 + 32 - REACH * 8 - (j - 1) * 8 + n]
            for side, value in enumerate((below[j], middle, above[j])):
                edges[side, at, lanes] = value.reshape(16, LANES).astype(BF)

    copies = [pltpu.make_async_copy(edges.at[i], out, edges_sem.at[i]) for i, out in enumerate((out0, out1, out2))]
    for copy in copies:
        copy.start()
    pack_grads([mm(ref[...], edges[side], TN) for side, ref in enumerate((fmi, f0, fpl))], blend, pay)
    pay[pl.ds(5 * HALF, 5 * HALF), :] = pay_v[...]
    for copy in copies:
        copy.wait()


def h_inputs(ready, w_ref, edges0, edges1, edges2, own, to_left, to_right, token, dfs, wt):
    token[...] = jnp.zeros(token.shape, F32)
    ready(0)
    fill_weights(w_ref, wt)
    for side, edges in enumerate((edges0, edges1, edges2)):
        ready(side + 1)

        @pl.loop(0, 4)
        def _(n):
            at = pl.ds(pl.multiple_of(n * 448, 448), 448)
            dfs[side, at, :] = mm(edges[at, :], wt[pl.ds(side * 384, 384), :], NN)

    first16 = low((16, LANES))

    def column(x, out, at):
        def piece(side, q):
            if q < 0 or q > 7:
                return jnp.zeros((16, LANES), F32)
            return dfs[side, pl.ds(pl.multiple_of(x * LANES + q * 16, 16), 16), :]

        for q in range(8):
            upper = piece(0, q) + piece(2, q - 1)
            lower = piece(0, q + 1) + piece(2, q)
            out[at, q] = piece(1, q) + swap(jnp.where(first16, lower, upper))

    for x in range(REACH):
        column(x, to_left, x)
        column(x + 8 + REACH, to_right, x)

    @pl.loop(0, 8)
    def _(x):
        column(x + REACH, own, x)


def h_finish(ready, own, gm, from_left, from_right, out, stage):
    ready()
    for x in range(8):
        for q in range(8):
            total = gm[q, x].astype(F32) + own[x, q]
            if x < REACH:
                total = total + from_left[x, q]
            if x >= 8 - REACH:
                total = total + from_right[x - 8 + REACH, q]
            stage[q, pl.ds(x * 16, 16), :] = total

    @pl.loop(0, 16, unroll=2)
    def _(y):
        for q in range(8):
            out[y, :, pl.ds(q * LANES, LANES)] = stage[q, pl.ds(y, 8, stride=16), :].astype(BF)


def v_both(ready, shear, beta_ref, w_ref, cot, h_ref, out, dvert, pay, beta, own, fv, taps, dps, sums, grads, outs, edges, blend, wt):
    shears = shear.shape[0]
    wide = 22
    plane = 10 * wide
    blend[...] = jnp.zeros(blend.shape, F32)
    first8 = low((8, LANES))

    for u in (0, 9):
        sheet = jnp.zeros((wide, 8, LANES), F32)
        for tap in (0, 1, 2) if u == 0 else (6, 7, 8):
            taps[pl.ds(tap * plane + u * wide, wide)] = sheet
        for jk in range(3 * shears):
            dps[pl.ds(jk * plane + u * wide, wide)] = sheet

    @pl.loop(1, 9)
    def _(u):
        rim = jnp.zeros((REACH, 8, LANES), F32)
        for side in (0, 16 + REACH):
            for tap in range(TAPS):
                taps[pl.ds(tap * plane + side + u * wide, REACH)] = rim
            for j in range(3):
                sums[pl.ds(j * plane + side + u * wide, REACH)] = rim
            for jk in range(3 * shears):
                dps[pl.ds(jk * plane + side + u * wide, REACH)] = rim

    ready()
    spread(beta_ref, beta)
    fill_weights(w_ref, wt, 0.5)

    @pl.loop(0, 8, unroll=2)
    def _(u):
        for x in range(8):
            own[u, pl.ds(x * 16, 16), :] = h_ref[u, x].astype(F32)
        for y in range(0, 16, 2):
            pair = [own[u, pl.ds(y + e, 8, stride=16), :] for e in range(2)]
            fv[pl.ds(pl.multiple_of(u * LANES + y * 8, 16), 16), :] = jnp.concatenate(pair, axis=0).astype(BF)
        for q in range(8):
            lanes = pl.ds(pl.multiple_of((u * 8 + q) * LANES, LANES), LANES)
            a, b = cot[0, :, lanes].astype(F32), cot[1, :, lanes].astype(F32)
            grads[u, 2 * q] = jnp.where(first8, a, swap(b))
            grads[u, 2 * q + 1] = jnp.where(first8, swap(a), b)

    @pl.loop(0, 2)
    def _(n):
        rows = pl.ds(pl.multiple_of(n * 512, 512), 512)
        for side in range(3):
            product = mm(fv[rows, :], wt[pl.ds(side * 384, 384), :], NT)
            for j in range(3):
                part = product[:, j * LANES : (j + 1) * LANES].reshape(4, 16, 8, LANES)
                for e in range(4):
                    taps[pl.ds((3 * side + j) * plane + (e + 1) * wide + REACH + n * 4 * wide, 16)] = part[e]

    def body(u, y):
        here = (u + 1) * wide + REACH + y
        g = grads[u, y]
        mid = taps[4 * plane + here]
        left = taps[3 * plane - 1 + here]
        right = taps[5 * plane + 1 + here]
        branch = jnp.zeros((8, LANES), F32)
        total = [jnp.zeros((8, LANES), F32) for _ in range(3)]
        shared = []
        for k in range(shears):
            d = shear[k]
            ys = jnp.full((8, LANES), y - d * (u - 4), jnp.int32)
            keep = ys.astype(jnp.uint32) < 16
            has_minus, has_plus = ys >= 1, ys <= 14
            a, b = here - d, here + d
            main = mid + (taps[plane - wide + a] + taps[7 * plane + wide + b])
            minus = left + (taps[-wide - 1 + a] + taps[6 * plane + wide - 1 + b])
            plus = right + (taps[2 * plane - wide + 1 + a] + taps[8 * plane + wide + 1 + b])
            act, slope = gate(main + jnp.where(has_minus, minus, 0.0) + jnp.where(has_plus, plus, 0.0))
            act = jnp.where(keep, act, 0.0)
            bk = beta[k]
            branch = branch + bk * act
            shared.append(g * act)
            dp = jnp.where(keep, bk * g * slope, 0.0).astype(BF).astype(F32)
            parts = (jnp.where(has_minus, dp, 0.0), dp, jnp.where(has_plus, dp, 0.0))
            for j in range(3):
                dps[(j * shears + k) * plane + here] = parts[j]
                total[j] = total[j] + parts[j]
        for j in range(3):
            sums[j * plane + here] = total[j]
        outs[u, y] = own[u, pl.ds(y, 8, stride=16), :] + branch
        return shared

    @pl.loop(0, 64, unroll=8)
    def _(n):
        u, y = n // 8, (n % 8) * 2
        first, second = body(u, y), body(u, y + 1)
        for k in range(shears):
            blend[k] += first[k] + second[k]

    @pl.loop(0, 64, unroll=4)
    def _(n):
        here = (n // 8 + 1) * wide + REACH + (n % 8) * 2
        at = pl.ds(pl.multiple_of(n * 16, 16), 16)
        below = [jnp.zeros((2, 8, LANES), F32) for _ in range(3)]
        above = [jnp.zeros((2, 8, LANES), F32) for _ in range(3)]
        for k in range(shears):
            d = shear[k]
            up, down = here + d, here - d
            for j in range(3):
                offset = (j * shears + k) * plane - (j - 1)
                below[j] = below[j] + dps[pl.ds(offset + wide + up, 2)]
                above[j] = above[j] + dps[pl.ds(offset - wide + down, 2)]
        for j in range(3):
            middle = sums[pl.ds(j * plane - (j - 1) + here, 2)]
            for side, value in enumerate((below[j], middle, above[j])):
                edges[at, pl.ds((3 * side + j) * LANES, LANES)] = value.reshape(16, LANES).astype(BF)

    pack_grads([mm(fv[...], edges[:, pl.ds(side * 384, 384)], TN) for side in range(3)], blend, pay)

    @pl.loop(0, 2)
    def _(n):
        rows = pl.ds(pl.multiple_of(n * 512, 512), 512)
        back = 2.0 * mm(edges[rows, :], wt[...], NN).reshape(4, LANES, LANES)
        for e in range(4):
            u = 4 * n + e
            own[u] = grads[u].reshape(LANES, LANES) + back[e]
            for x in range(8):
                dvert[u, x] = own[u, pl.ds(x, 16, stride=8), :].astype(BF)
            for q in range(8):
                lanes = pl.ds(pl.multiple_of((u * 8 + q) * LANES, LANES), LANES)
                a, b = outs[u, 2 * q], outs[u, 2 * q + 1]
                out[0, :, lanes] = jnp.where(first8, a, swap(b)).astype(BF)
                out[1, :, lanes] = jnp.where(first8, swap(a), b).astype(BF)


def call(body, fetched, operands, out_shapes, scratch, cost, vmem_mib, far=()):
    vmem = pl.BlockSpec(memory_space=pltpu.VMEM)
    specs = [pl.BlockSpec(memory_space=pltpu.HBM)] * len(fetched)
    specs += [pl.BlockSpec(memory_space=pltpu.SMEM if op.dtype == jnp.int32 else pltpu.VMEM) for op in operands]
    held = [(pltpu.SMEM if op.dtype == jnp.int32 else pltpu.VMEM)(op.shape, op.dtype) for op in fetched]
    count = len(fetched)

    def kernel(*refs):
        sources, others = refs[:count], refs[count : -count - 1]
        targets, sem = refs[-count - 1 : -1], refs[-1]
        copies = [pltpu.make_async_copy(sources[i], targets[i], sem.at[i]) for i in range(count)]
        for copy in copies:
            copy.start()

        def ready(*which):
            for i in which or range(count):
                copies[i].wait()

        body(ready, *targets, *others)

    return pl.pallas_call(
        kernel,
        out_shape=out_shapes,
        in_specs=specs,
        out_specs=[pl.BlockSpec(memory_space=pltpu.HBM) if i in far else vmem for i in range(len(out_shapes))],
        scratch_shapes=list(scratch) + held + [pltpu.SemaphoreType.DMA((count,))],
        compiler_params=pltpu.CompilerParams(vmem_limit_bytes=int(vmem_mib * MIB)),
        cost_estimate=pl.CostEstimate(flops=cost, bytes_accessed=4_000_000, transcendentals=1_000_000),
    )(*[pltpu.with_memory_space_constraint(op, pltpu.HBM) for op in fetched], *operands)


def unpack(total, w_h, w_v, b_h, b_v):
    scale = 262144.0**-0.5
    for at, weight, blend in ((0, w_h, b_h), (5 * HALF, w_v, b_v)):
        for pair in range(5):
            block = total[pl.ds(at + pair * HALF, HALF), :] * scale
            weight[2 * pair] = block[:, :HALF]
            other = swap(block)[:, :HALF]
            if pair < 4:
                weight[2 * pair + 1] = other
            else:
                blend[...] = other[: blend.shape[0]]


def added(parts):
    total = parts[0]
    for i in range(1, parts.shape[0]):
        total = total + parts[i]
    return total


def reduce_all(pay, zero):
    part = lax.all_to_all(pay.reshape(16, 40, LANES), "img", 0, 0, tiled=True)
    part = jnp.broadcast_to((added(part) + zero)[None], (8, 40, LANES))
    part = lax.all_to_all(part, "vrow", 0, 0, tiled=True)
    part = jnp.broadcast_to(added(part)[None], (16, 40, LANES))
    return lax.all_to_all(part, "img", 0, 0, tiled=True).reshape(640, LANES)


def whole_step(features, weight_h, weight_v, beta_h, beta_v, shear_set, cotangent):
    shears = shear_set.shape[0]
    img = lax.axis_size("img")
    sds = jax.ShapeDtypeStruct
    own = features.reshape(16, 8, 1024)
    to_right = [(i, i + 1) for i in range(img - 1)]
    to_left = [(i + 1, i) for i in range(img - 1)]
    from_left = lax.ppermute(own[:, 4:], "img", to_right)
    from_right = lax.ppermute(own[:, :4], "img", to_left)
    base = (lax.axis_index("img") * 8).astype(jnp.int32).reshape(1)
    w_h = jnp.transpose(weight_h, (2, 3, 0, 1)).reshape(TAPS, HALF, HALF)
    w_v = jnp.transpose(weight_v, (2, 3, 0, 1)).reshape(TAPS, HALF, HALF)

    hfeat, pre, f0, fmi, fpl = call(
        h_forward,
        (shear_set, beta_h, w_h, own),
        (base, from_left, from_right),
        [sds((8, 8, 16, LANES), BF), sds((shears * 64, 2, 8, LANES), F32)] + [sds((WIDE * LANES, LANES), BF)] * 3,
        [
            pltpu.VMEM((shears, 8, LANES), F32),
            pltpu.VMEM((8, 384, LANES), F32),
            pltpu.VMEM((TAPS * PLANE, 2, 8, LANES), F32),
            pltpu.VMEM((TAPS * LANES, LANES), BF),
        ],
        2 * WIDE * LANES * LANES * TAPS * LANES,
        GRANT[0],
    )
    moved = lax.all_to_all(hfeat, "vrow", 0, 0, tiled=True)
    output, dvert, pay_v = call(
        v_both,
        (shear_set, beta_v, w_v, cotangent),
        (moved,),
        [sds((2, 8, 8192), BF), sds((8, 8, 16, LANES), BF), sds((320, LANES), F32)],
        [
            pltpu.VMEM((shears, 8, LANES), F32),
            pltpu.VMEM((8, LANES, LANES), F32),
            pltpu.VMEM((1024, LANES), BF),
            pltpu.VMEM((TAPS * 220, 8, LANES), F32),
            pltpu.VMEM((3 * shears * 220, 8, LANES), F32),
            pltpu.VMEM((3 * 220, 8, LANES), F32),
            pltpu.VMEM((8, 16, 8, LANES), F32),
            pltpu.VMEM((8, 16, 8, LANES), F32),
            pltpu.VMEM((1024, TAPS * LANES), BF),
            pltpu.VMEM((shears, 8, LANES), F32),
            pltpu.VMEM((TAPS * LANES, LANES), BF),
        ],
        6 * 1024 * LANES * TAPS * LANES,
        GRANT[1],
    )
    grad = lax.all_to_all(dvert, "vrow", 0, 0, tiled=True)
    pay, *edges_h = call(
        h_backward,
        (shear_set, beta_h),
        (base, pre, f0, fmi, fpl, grad, pay_v),
        [sds((640, LANES), F32)] + [pltpu.HBM((WIDE * LANES, 384), BF)] * 3,
        [
            pltpu.VMEM((shears, 8, LANES), F32),
            pltpu.VMEM((3 * shears * PLANE + 48, 2, 8, LANES), F32),
            pltpu.VMEM((3 * 96 + 32, 2, 8, LANES), F32),
            pltpu.VMEM((3, WIDE * LANES, 384), BF),
            pltpu.VMEM((shears, 8, LANES), F32),
            pltpu.SemaphoreType.DMA((3,)),
        ],
        2 * WIDE * LANES * LANES * TAPS * LANES,
        GRANT[2],
        (1, 2, 3),
    )
    back, halo_left, halo_right, inputs_done = call(
        h_inputs,
        (w_h, *edges_h),
        (),
        [pltpu.HBM((8, 8, 16, LANES), F32)] + [pltpu.HBM((REACH, 8, 16, LANES), F32)] * 2 + [sds((40, LANES), F32)],
        [pltpu.VMEM((3, WIDE * LANES, LANES), F32), pltpu.VMEM((TAPS * LANES, LANES), BF)],
        2 * WIDE * LANES * LANES * TAPS * LANES,
        GRANT[3],
    )
    halo_from_right = lax.ppermute(halo_left, "img", to_left)
    halo_from_left = lax.ppermute(halo_right, "img", to_right)
    (grad_features,) = call(
        h_finish,
        (back, grad),
        (halo_from_left, halo_from_right),
        [sds((16, 8, 1024), BF)],
        [pltpu.VMEM((8, LANES, LANES), F32)],
        1_000_000,
        GRANT[4],
    )
    vmem = pl.BlockSpec(memory_space=pltpu.VMEM)
    weights = sds((TAPS, HALF, HALF), F32)
    w_grad_h, w_grad_v, beta_grad_h, beta_grad_v = pl.pallas_call(
        unpack,
        out_shape=[weights, weights] + [sds((shears, HALF), F32)] * 2,
        in_specs=[vmem],
        out_specs=[vmem] * 4,
        compiler_params=pltpu.CompilerParams(vmem_limit_bytes=6 * MIB),
    )(reduce_all(pay, inputs_done))

    def placed(weight):
        return jnp.transpose(weight.reshape(3, 3, HALF, HALF), (2, 3, 0, 1))

    return output, grad_features.reshape(features.shape), placed(w_grad_h), placed(w_grad_v), beta_grad_h, beta_grad_v


def solution(mesh):
    placed = (P("vrow", None, "img", None), P(), P(), P(), P(), P(), P("vrow", "img", None))
    return jax.shard_map(
        whole_step,
        mesh=mesh,
        in_specs=placed,
        out_specs=(P("vrow", "img", None), P("vrow", None, "img", None), P(), P(), P(), P()),
        check_vma=False,
    )
```

```python
import jax
import jax.numpy as jnp
from jax import lax
from jax.experimental import pallas as pl
from jax.experimental.pallas import tpu as pltpu
from jax.sharding import PartitionSpec as P


BF = jnp.bfloat16
F32 = jnp.float32
LANES = 128
HALF = 64
TAPS = 9
REACH = 3
WIDE = 8 + 2 * REACH
PLANE = WIDE * 8
MIB = 1024 * 1024
GRANT = (26, 36, 34, 20, 12)
NT = (((1,), (1,)), ((), ()))
NN = (((1,), (0,)), ((), ()))
TN = (((0,), (0,)), ((), ()))


def mm(lhs, rhs, dims):
    return lax.dot_general(lhs, rhs, dims, preferred_element_type=F32)


def lanes_of(shape):
    return lax.broadcasted_iota(jnp.int32, shape, len(shape) - 1)


def swap(value):
    return pltpu.roll(value, HALF, axis=value.ndim - 1)


def low(shape):
    return lanes_of(shape) < HALF


def fill_weights(w_ref, wt_ref, scale=1.0):
    zero = jnp.zeros((HALF, HALF), BF)
    for tap in range(TAPS):
        w = w_ref[tap]
        if scale != 1.0:
            w = (w.astype(F32) * scale).astype(BF)
        wt_ref[pl.ds(tap * LANES, HALF), :] = jnp.concatenate([w, zero], axis=1)
        wt_ref[pl.ds(tap * LANES + HALF, HALF), :] = jnp.concatenate([zero, w], axis=1)


def spread(beta_ref, beta):
    for k in range(beta.shape[0]):
        line = beta_ref[pl.ds(k, 1), :]
        beta[k] = jnp.broadcast_to(jnp.concatenate([line, line], axis=1), (8, LANES))


def pack_grads(grads, blend_ref, pay_ref):
    first = low((HALF, LANES))
    rows = lax.broadcasted_iota(jnp.int32, (HALF, LANES), 0)
    blend = jnp.zeros((HALF, LANES), F32)
    for k in range(blend_ref.shape[0]):
        line = jnp.sum(blend_ref[k], axis=0, keepdims=True)
        blend = blend + jnp.where(rows == k, line + swap(line), 0.0)

    def tap_of(tap):
        block = grads[tap // 3][:, (tap % 3) * LANES : (tap % 3 + 1) * LANES]
        return block[:HALF] + swap(block[HALF:])

    for pair in range(5):
        even = tap_of(2 * pair)
        odd = tap_of(2 * pair + 1) if pair < 4 else even
        both = jnp.transpose(jnp.where(first, even, swap(odd)))
        value = jnp.concatenate([both[:HALF], both[HALF:]], axis=1)
        if pair == 4:
            value = jnp.where(first, value, blend)
        pay_ref[pl.ds(pair * HALF, HALF), :] = value.astype(pay_ref.dtype)


def gate(h):
    t = jnp.tanh(h) + 1.0
    s = 0.5 * t
    act = h * t
    return act, s + act * (1.0 - s)


def halves():
    return (lanes_of((1, 8, LANES)) >= HALF).astype(jnp.int32)


def h_forward(ready, shear, beta_ref, w_ref, fm, base, fl, fr, hfeat, pre_ref, f0, fmi, fpl, beta, stage, taps, wt):
    shears = shear.shape[0]
    ready()
    spread(beta_ref, beta)
    fill_weights(w_ref, wt, 0.5)
    first16 = low((16, LANES))

    @pl.loop(0, 16, unroll=2)
    def _(y):
        for start, rows, ref in ((4, 4, fl), (8, 8, fm), (16, 4, fr)):
            for q in range(8):
                stage[q, pl.ds(y * 24 + start, rows), :] = ref[y, :, pl.ds(q * LANES, LANES)].astype(F32)

    @pl.loop(0, WIDE, unroll=2)
    def _(x):
        own = [stage[q, pl.ds(x + 8 - REACH, 16, stride=24), :] for q in range(8)]
        turned = [swap(a) for a in own]
        zero = jnp.zeros((16, LANES), F32)
        moved = [
            jnp.where(first16, turned[q - 1] if q > 0 else zero, turned[q] if q < 8 else zero).astype(BF)
            for q in range(9)
        ]
        for q in range(8):
            at = pl.ds(pl.multiple_of(x * LANES + q * 16, 16), 16)
            f0[at, :] = own[q].astype(BF)
            fmi[at, :] = moved[q]
            fpl[at, :] = moved[q + 1]

    @pl.loop(0, 4)
    def _(n):
        at = pl.ds(pl.multiple_of(n * 448, 448), 448)
        for side, ref in enumerate((fmi, f0, fpl)):
            product = mm(ref[at, :], wt[pl.ds(side * 384, 384), :], NT)
            for j in range(3):
                part = product[:, j * LANES : (j + 1) * LANES].reshape(28, 2, 8, LANES)
                taps[pl.ds((3 * side + j) * PLANE + n * 28, 28)] = part

    half = halves()

    @pl.loop(0, 64, unroll=8)
    def _(n):
        q = n % 8
        here = n + REACH * 8
        vrel = half + (2 * q - 8)
        xg = base[0] + n // 8
        mid = taps[4 * PLANE + here]
        left = taps[3 * PLANE - 8 + here]
        right = taps[5 * PLANE + 8 + here]
        branch = jnp.zeros((2, 8, LANES), F32)
        for k in range(shears):
            d = shear[k]
            xs = xg - d * vrel
            a, b = here - d * 8, here + d * 8
            main = mid + (taps[PLANE + a] + taps[7 * PLANE + b])
            minus = left + (taps[a - 8] + taps[6 * PLANE - 8 + b])
            plus = right + (taps[2 * PLANE + 8 + a] + taps[8 * PLANE + 8 + b])
            pre = main + jnp.where(xs >= 1, minus, 0.0) + jnp.where(xs <= LANES - 2, plus, 0.0)
            pre_ref[k * 64 + n] = pre
            keep = xs.astype(jnp.uint32) < LANES
            branch = branch + jnp.where(keep, beta[k] * gate(pre)[0], 0.0)
        own = f0[pl.ds(pl.multiple_of(here * 16, 16), 16), :].astype(F32)
        hfeat[q, n // 8] = (own + branch.reshape(16, LANES)).astype(BF)


def h_backward(ready, shear, beta_ref, base, pre_ref, f0, fmi, fpl, gm, pay_v, pay, rim0, rim1, rim2, out0, out1, out2, beta, dps, sums, edges, blend, edges_sem):
    shears = shear.shape[0]
    ready()
    spread(beta_ref, beta)
    half = halves()
    blend[...] = jnp.zeros(blend.shape, F32)

    @pl.loop(0, 64, unroll=8)
    def _(n):
        dps[pl.ds((n // 4) * PLANE + (n % 4) * 12, 12)] = jnp.zeros((12, 2, 8, LANES), F32)
        sums[pl.ds((n // 16) * 96 + (n % 16) * 2, 2)] = jnp.zeros((2, 2, 8, LANES), F32)
        x, q = n // 8, n % 8
        g = gm[q, x].astype(F32).reshape(2, 8, LANES)
        vrel = half + (2 * q - 8)
        xg = base[0] + x
        total = [jnp.zeros((2, 8, LANES), F32) for _ in range(3)]
        for k in range(shears):
            xs = xg - shear[k] * vrel
            act, slope = gate(pre_ref[k * 64 + n])
            gk = jnp.where(xs.astype(jnp.uint32) < LANES, g, 0.0)
            dp = (beta[k] * gk * slope).astype(BF).astype(F32)
            parts = (jnp.where(xs >= 1, dp, 0.0), dp, jnp.where(xs <= LANES - 2, dp, 0.0))
            for j in range(3):
                dps[(j * shears + k) * PLANE + 48 + n] = parts[j]
                total[j] = total[j] + parts[j]
            blend[k] += jnp.sum(gk * act, axis=0)
        for j in range(3):
            sums[j * 96 + 32 + n] = total[j]

    @pl.loop(0, WIDE * 8, unroll=8)
    def _(n):
        at = pl.ds(pl.multiple_of(n * 16, 16), 16)
        below = [jnp.zeros((2, 8, LANES), F32) for _ in range(3)]
        above = [jnp.zeros((2, 8, LANES), F32) for _ in range(3)]
        for k in range(shears):
            d = shear[k]
            up, down = n + d * 8, n - d * 8
            for j in range(3):
                offset = (j * shears + k) * PLANE + 48 - REACH * 8 - (j - 1) * 8
                below[j] = below[j] + dps[offset + up]
                above[j] = above[j] + dps[offset + down]
        for j in range(3):
            lanes = pl.ds(j * LANES, LANES)
            middle = sums[j * 96 + 32 - REACH * 8 - (j - 1) * 8 + n]
            for side, value in enumerate((below[j], middle, above[j])):
                edges[side, at, lanes] = value.reshape(16, LANES).astype(BF)

    side = REACH * LANES
    copies = []
    for i, (rim, out) in enumerate(((rim0, out0), (rim1, out1), (rim2, out2))):
        pieces = ((0, side, rim.at[pl.ds(0, side)]), (side + 1024, side, rim.at[pl.ds(side, side)]), (side, 1024, out))
        for e, (start, rows, target) in enumerate(pieces):
            copies.append(pltpu.make_async_copy(edges.at[i, pl.ds(start, rows)], target, edges_sem.at[3 * i + e]))
    for copy in copies:
        copy.start()
    pack_grads([mm(ref[...], edges[side], TN) for side, ref in enumerate((fmi, f0, fpl))], blend, pay)
    pay[pl.ds(5 * HALF, 5 * HALF), :] = pay_v[...]
    for copy in copies:
        copy.wait()


def back_through(ready, w_ref, edges, dfs, wt, chunk):
    ready(0)
    fill_weights(w_ref, wt)
    for side in range(3):
        ready(side + 1)
        for start in range(0, dfs.shape[1], chunk):
            rows = pl.ds(start, chunk)
            dfs[side, rows, :] = mm(edges[side][rows, :], wt[pl.ds(side * 384, 384), :], NN)


def column(dfs, x):
    first16 = low((16, LANES))

    def piece(side, q):
        if q < 0 or q > 7:
            return jnp.zeros((16, LANES), F32)
        return dfs[side, pl.ds(pl.multiple_of(x * LANES + q * 16, 16), 16), :]

    found = []
    for q in range(8):
        upper = piece(0, q) + piece(2, q - 1)
        lower = piece(0, q + 1) + piece(2, q)
        found.append(piece(1, q) + swap(jnp.where(first16, lower, upper)))
    return found


def h_rims(ready, w_ref, edges0, edges1, edges2, to_left, to_right, token, dfs, wt):
    token[...] = jnp.zeros(token.shape, F32)
    back_through(ready, w_ref, (edges0, edges1, edges2), dfs, wt, 768)
    for x in range(REACH):
        for q, value in enumerate(column(dfs, x)):
            to_left[x, q] = value
        for q, value in enumerate(column(dfs, x + REACH)):
            to_right[x, q] = value


def h_finish(ready, w_ref, edges0, edges1, edges2, gm, from_left, from_right, out, dfs, stage, wt):
    back_through(ready, w_ref, (edges0, edges1, edges2), dfs, wt, 512)
    ready(4)
    for x in range(8):
        for q, value in enumerate(column(dfs, x)):
            total = gm[q, x].astype(F32) + value
            if x < REACH:
                total = total + from_left[x, q]
            if x >= 8 - REACH:
                total = total + from_right[x - 8 + REACH, q]
            stage[q, pl.ds(x * 16, 16), :] = total

    @pl.loop(0, 16, unroll=2)
    def _(y):
        for q in range(8):
            out[y, :, pl.ds(q * LANES, LANES)] = stage[q, pl.ds(y, 8, stride=16), :].astype(BF)


def v_both(ready, shear, beta_ref, w_ref, cot, h_ref, out, dvert, pay, beta, own, fv, taps, dps, sums, grads, outs, edges, blend, wt):
    shears = shear.shape[0]
    wide = 22
    plane = 10 * wide
    blend[...] = jnp.zeros(blend.shape, F32)
    first8 = low((8, LANES))

    for u in (0, 9):
        sheet = jnp.zeros((wide, 8, LANES), F32)
        for tap in (0, 1, 2) if u == 0 else (6, 7, 8):
            taps[pl.ds(tap * plane + u * wide, wide)] = sheet
        for jk in range(3 * shears):
            dps[pl.ds(jk * plane + u * wide, wide)] = sheet

    @pl.loop(1, 9)
    def _(u):
        rim = jnp.zeros((REACH, 8, LANES), F32)
        for side in (0, 16 + REACH):
            for tap in range(TAPS):
                taps[pl.ds(tap * plane + side + u * wide, REACH)] = rim
            for j in range(3):
                sums[pl.ds(j * plane + side + u * wide, REACH)] = rim
            for jk in range(3 * shears):
                dps[pl.ds(jk * plane + side + u * wide, REACH)] = rim

    ready()
    spread(beta_ref, beta)
    fill_weights(w_ref, wt, 0.5)

    @pl.loop(0, 8, unroll=2)
    def _(u):
        for x in range(8):
            own[u, pl.ds(x * 16, 16), :] = h_ref[u, x].astype(F32)
        for y in range(0, 16, 2):
            pair = [own[u, pl.ds(y + e, 8, stride=16), :] for e in range(2)]
            fv[pl.ds(pl.multiple_of(u * LANES + y * 8, 16), 16), :] = jnp.concatenate(pair, axis=0).astype(BF)
        for q in range(8):
            lanes = pl.ds(pl.multiple_of((u * 8 + q) * LANES, LANES), LANES)
            a, b = cot[0, :, lanes].astype(F32), cot[1, :, lanes].astype(F32)
            grads[u, 2 * q] = jnp.where(first8, a, swap(b))
            grads[u, 2 * q + 1] = jnp.where(first8, swap(a), b)

    @pl.loop(0, 2)
    def _(n):
        rows = pl.ds(pl.multiple_of(n * 512, 512), 512)
        for side in range(3):
            product = mm(fv[rows, :], wt[pl.ds(side * 384, 384), :], NT)
            for j in range(3):
                part = product[:, j * LANES : (j + 1) * LANES].reshape(4, 16, 8, LANES)
                for e in range(4):
                    taps[pl.ds((3 * side + j) * plane + (e + 1) * wide + REACH + n * 4 * wide, 16)] = part[e]

    def body(u, y):
        here = (u + 1) * wide + REACH + y
        g = grads[u, y]
        mid = taps[4 * plane + here]
        left = taps[3 * plane - 1 + here]
        right = taps[5 * plane + 1 + here]
        branch = jnp.zeros((8, LANES), F32)
        total = [jnp.zeros((8, LANES), F32) for _ in range(3)]
        shared = []
        for k in range(shears):
            d = shear[k]
            ys = jnp.full((8, LANES), y - d * (u - 4), jnp.int32)
            keep = ys.astype(jnp.uint32) < 16
            has_minus, has_plus = ys >= 1, ys <= 14
            a, b = here - d, here + d
            main = mid + (taps[plane - wide + a] + taps[7 * plane + wide + b])
            minus = left + (taps[-wide - 1 + a] + taps[6 * plane + wide - 1 + b])
            plus = right + (taps[2 * plane - wide + 1 + a] + taps[8 * plane + wide + 1 + b])
            act, slope = gate(main + jnp.where(has_minus, minus, 0.0) + jnp.where(has_plus, plus, 0.0))
            act = jnp.where(keep, act, 0.0)
            bk = beta[k]
            branch = branch + bk * act
            shared.append(g * act)
            dp = jnp.where(keep, bk * g * slope, 0.0).astype(BF).astype(F32)
            parts = (jnp.where(has_minus, dp, 0.0), dp, jnp.where(has_plus, dp, 0.0))
            for j in range(3):
                dps[(j * shears + k) * plane + here] = parts[j]
                total[j] = total[j] + parts[j]
        for j in range(3):
            sums[j * plane + here] = total[j]
        outs[u, y] = own[u, pl.ds(y, 8, stride=16), :] + branch
        return shared

    @pl.loop(0, 64, unroll=8)
    def _(n):
        u, y = n // 8, (n % 8) * 2
        first, second = body(u, y), body(u, y + 1)
        for k in range(shears):
            blend[k] += first[k] + second[k]

    @pl.loop(0, 64, unroll=4)
    def _(n):
        here = (n // 8 + 1) * wide + REACH + (n % 8) * 2
        at = pl.ds(pl.multiple_of(n * 16, 16), 16)
        below = [jnp.zeros((2, 8, LANES), F32) for _ in range(3)]
        above = [jnp.zeros((2, 8, LANES), F32) for _ in range(3)]
        for k in range(shears):
            d = shear[k]
            up, down = here + d, here - d
            for j in range(3):
                offset = (j * shears + k) * plane - (j - 1)
                below[j] = below[j] + dps[pl.ds(offset + wide + up, 2)]
                above[j] = above[j] + dps[pl.ds(offset - wide + down, 2)]
        for j in range(3):
            middle = sums[pl.ds(j * plane - (j - 1) + here, 2)]
            for side, value in enumerate((below[j], middle, above[j])):
                edges[at, pl.ds((3 * side + j) * LANES, LANES)] = value.reshape(16, LANES).astype(BF)

    pack_grads([mm(fv[...], edges[:, pl.ds(side * 384, 384)], TN) for side in range(3)], blend, pay)

    @pl.loop(0, 2)
    def _(n):
        rows = pl.ds(pl.multiple_of(n * 512, 512), 512)
        back = 2.0 * mm(edges[rows, :], wt[...], NN).reshape(4, LANES, LANES)
        for e in range(4):
            u = 4 * n + e
            own[u] = grads[u].reshape(LANES, LANES) + back[e]
            for x in range(8):
                dvert[u, x] = own[u, pl.ds(x, 16, stride=8), :].astype(BF)
            for q in range(8):
                lanes = pl.ds(pl.multiple_of((u * 8 + q) * LANES, LANES), LANES)
                a, b = outs[u, 2 * q], outs[u, 2 * q + 1]
                out[0, :, lanes] = jnp.where(first8, a, swap(b)).astype(BF)
                out[1, :, lanes] = jnp.where(first8, swap(a), b).astype(BF)


def call(body, fetched, operands, out_shapes, scratch, cost, vmem_mib, far=()):
    vmem = pl.BlockSpec(memory_space=pltpu.VMEM)
    specs = [pl.BlockSpec(memory_space=pltpu.HBM)] * len(fetched)
    specs += [pl.BlockSpec(memory_space=pltpu.SMEM if op.dtype == jnp.int32 else pltpu.VMEM) for op in operands]
    held = [(pltpu.SMEM if op.dtype == jnp.int32 else pltpu.VMEM)(op.shape, op.dtype) for op in fetched]
    count = len(fetched)

    def kernel(*refs):
        sources, others = refs[:count], refs[count : -count - 1]
        targets, sem = refs[-count - 1 : -1], refs[-1]
        copies = [pltpu.make_async_copy(sources[i], targets[i], sem.at[i]) for i in range(count)]
        for copy in copies:
            copy.start()

        def ready(*which):
            for i in which or range(count):
                copies[i].wait()

        body(ready, *targets, *others)

    return pl.pallas_call(
        kernel,
        out_shape=out_shapes,
        in_specs=specs,
        out_specs=[pl.BlockSpec(memory_space=pltpu.HBM) if i in far else vmem for i in range(len(out_shapes))],
        scratch_shapes=list(scratch) + held + [pltpu.SemaphoreType.DMA((count,))],
        compiler_params=pltpu.CompilerParams(vmem_limit_bytes=int(vmem_mib * MIB)),
        cost_estimate=pl.CostEstimate(flops=cost, bytes_accessed=4_000_000, transcendentals=1_000_000),
    )(*[pltpu.with_memory_space_constraint(op, pltpu.HBM) for op in fetched], *operands)


def unpack(total, w_h, w_v, b_h, b_v):
    scale = 262144.0**-0.5
    for at, weight, blend in ((0, w_h, b_h), (5 * HALF, w_v, b_v)):
        for pair in range(5):
            block = total[pl.ds(at + pair * HALF, HALF), :] * scale
            weight[2 * pair] = block[:, :HALF]
            other = swap(block)[:, :HALF]
            if pair < 4:
                weight[2 * pair + 1] = other
            else:
                blend[...] = other[: blend.shape[0]]


def added(parts):
    total = parts[0]
    for i in range(1, parts.shape[0]):
        total = total + parts[i]
    return total


def reduce_all(pay, zero):
    part = lax.all_to_all(pay.reshape(16, 40, LANES), "img", 0, 0, tiled=True)
    part = jnp.broadcast_to((added(part.astype(F32)) + zero)[None], (8, 40, LANES))
    part = lax.all_to_all(part, "vrow", 0, 0, tiled=True)
    part = jnp.broadcast_to(added(part)[None], (16, 40, LANES))
    return lax.all_to_all(part, "img", 0, 0, tiled=True).reshape(640, LANES)


def whole_step(features, weight_h, weight_v, beta_h, beta_v, shear_set, cotangent):
    shears = shear_set.shape[0]
    img = lax.axis_size("img")
    sds = jax.ShapeDtypeStruct
    own = features.reshape(16, 8, 1024)
    to_right = [(i, i + 1) for i in range(img - 1)]
    to_left = [(i + 1, i) for i in range(img - 1)]
    from_left = lax.ppermute(own[:, 4:], "img", to_right)
    from_right = lax.ppermute(own[:, :4], "img", to_left)
    base = (lax.axis_index("img") * 8).astype(jnp.int32).reshape(1)
    w_h = jnp.transpose(weight_h, (2, 3, 0, 1)).reshape(TAPS, HALF, HALF)
    w_v = jnp.transpose(weight_v, (2, 3, 0, 1)).reshape(TAPS, HALF, HALF)

    hfeat, pre, f0, fmi, fpl = call(
        h_forward,
        (shear_set, beta_h, w_h, own),
        (base, from_left, from_right),
        [sds((8, 8, 16, LANES), BF), sds((shears * 64, 2, 8, LANES), F32)] + [sds((WIDE * LANES, LANES), BF)] * 3,
        [
            pltpu.VMEM((shears, 8, LANES), F32),
            pltpu.VMEM((8, 384, LANES), F32),
            pltpu.VMEM((TAPS * PLANE, 2, 8, LANES), F32),
            pltpu.VMEM((TAPS * LANES, LANES), BF),
        ],
        2 * WIDE * LANES * LANES * TAPS * LANES,
        GRANT[0],
    )
    moved = lax.all_to_all(hfeat, "vrow", 0, 0, tiled=True)
    output, dvert, pay_v = call(
        v_both,
        (shear_set, beta_v, w_v, cotangent),
        (moved,),
        [sds((2, 8, 8192), BF), sds((8, 8, 16, LANES), BF), sds((320, LANES), BF)],
        [
            pltpu.VMEM((shears, 8, LANES), F32),
            pltpu.VMEM((8, LANES, LANES), F32),
            pltpu.VMEM((1024, LANES), BF),
            pltpu.VMEM((TAPS * 220, 8, LANES), F32),
            pltpu.VMEM((3 * shears * 220, 8, LANES), F32),
            pltpu.VMEM((3 * 220, 8, LANES), F32),
            pltpu.VMEM((8, 16, 8, LANES), F32),
            pltpu.VMEM((8, 16, 8, LANES), F32),
            pltpu.VMEM((1024, TAPS * LANES), BF),
            pltpu.VMEM((shears, 8, LANES), F32),
            pltpu.VMEM((TAPS * LANES, LANES), BF),
        ],
        6 * 1024 * LANES * TAPS * LANES,
        GRANT[1],
    )
    grad = lax.all_to_all(dvert, "vrow", 0, 0, tiled=True)
    pay, rim0, rim1, rim2, *edges_h = call(
        h_backward,
        (shear_set, beta_h),
        (base, pre, f0, fmi, fpl, grad, pay_v),
        [sds((640, LANES), BF)] + [pltpu.HBM((2 * REACH * LANES, 384), BF)] * 3 + [pltpu.HBM((1024, 384), BF)] * 3,
        [
            pltpu.VMEM((shears, 8, LANES), F32),
            pltpu.VMEM((3 * shears * PLANE + 48, 2, 8, LANES), F32),
            pltpu.VMEM((3 * 96 + 32, 2, 8, LANES), F32),
            pltpu.VMEM((3, WIDE * LANES, 384), BF),
            pltpu.VMEM((shears, 8, LANES), F32),
            pltpu.SemaphoreType.DMA((9,)),
        ],
        2 * WIDE * LANES * LANES * TAPS * LANES,
        GRANT[2],
        (1, 2, 3, 4, 5, 6),
    )
    halo_left, halo_right, rims_done = call(
        h_rims,
        (w_h, rim0, rim1, rim2),
        (),
        [pltpu.HBM((REACH, 8, 16, LANES), F32)] * 2 + [sds((40, LANES), F32)],
        [pltpu.VMEM((3, 2 * REACH * LANES, LANES), F32), pltpu.VMEM((TAPS * LANES, LANES), BF)],
        2 * 2 * REACH * LANES * LANES * TAPS * LANES,
        GRANT[3],
    )
    halo_from_right = lax.ppermute(halo_left, "img", to_left)
    halo_from_left = lax.ppermute(halo_right, "img", to_right)
    (grad_features,) = call(
        h_finish,
        (w_h, *edges_h, grad),
        (halo_from_left, halo_from_right),
        [sds((16, 8, 1024), BF)],
        [pltpu.VMEM((3, 1024, LANES), F32), pltpu.VMEM((8, LANES, LANES), F32), pltpu.VMEM((TAPS * LANES, LANES), BF)],
        2 * 1024 * LANES * TAPS * LANES,
        GRANT[4],
    )
    vmem = pl.BlockSpec(memory_space=pltpu.VMEM)
    weights = sds((TAPS, HALF, HALF), F32)
    w_grad_h, w_grad_v, beta_grad_h, beta_grad_v = pl.pallas_call(
        unpack,
        out_shape=[weights, weights] + [sds((shears, HALF), F32)] * 2,
        in_specs=[vmem],
        out_specs=[vmem] * 4,
        compiler_params=pltpu.CompilerParams(vmem_limit_bytes=6 * MIB),
    )(reduce_all(pay, rims_done))

    def placed(weight):
        return jnp.transpose(weight.reshape(3, 3, HALF, HALF), (2, 3, 0, 1))

    return output, grad_features.reshape(features.shape), placed(w_grad_h), placed(w_grad_v), beta_grad_h, beta_grad_v


def solution(mesh):
    placed = (P("vrow", None, "img", None), P(), P(), P(), P(), P(), P("vrow", "img", None))
    return jax.shard_map(
        whole_step,
        mesh=mesh,
        in_specs=placed,
        out_specs=(P("vrow", "img", None), P("vrow", None, "img", None), P(), P(), P(), P()),
        check_vma=False,
    )
```

```python
import jax
import jax.numpy as jnp
from jax import lax
from jax.experimental import pallas as pl
from jax.experimental.pallas import tpu as pltpu
from jax.sharding import PartitionSpec as P


BF = jnp.bfloat16
F32 = jnp.float32
LANES = 128
HALF = 64
TAPS = 9
REACH = 3
WIDE = 8 + 2 * REACH
PLANE = WIDE * 8
MIB = 1024 * 1024
GRANT = (26, 36, 34, 20, 12)
NT = (((1,), (1,)), ((), ()))
NN = (((1,), (0,)), ((), ()))
TN = (((0,), (0,)), ((), ()))


def mm(lhs, rhs, dims):
    return lax.dot_general(lhs, rhs, dims, preferred_element_type=F32)


def lanes_of(shape):
    return lax.broadcasted_iota(jnp.int32, shape, len(shape) - 1)


def swap(value):
    return pltpu.roll(value, HALF, axis=value.ndim - 1)


def low(shape):
    return lanes_of(shape) < HALF


def fill_weights(w_ref, wt_ref, scale=1.0):
    zero = jnp.zeros((HALF, HALF), BF)
    for tap in range(TAPS):
        w = w_ref[tap]
        if scale != 1.0:
            w = (w.astype(F32) * scale).astype(BF)
        wt_ref[pl.ds(tap * LANES, HALF), :] = jnp.concatenate([w, zero], axis=1)
        wt_ref[pl.ds(tap * LANES + HALF, HALF), :] = jnp.concatenate([zero, w], axis=1)


def spread(beta_ref, beta):
    for k in range(beta.shape[0]):
        line = beta_ref[pl.ds(k, 1), :]
        beta[k] = jnp.broadcast_to(jnp.concatenate([line, line], axis=1), (8, LANES))


def pack_grads(grads, blend_ref, pay_ref):
    first = low((HALF, LANES))
    rows = lax.broadcasted_iota(jnp.int32, (HALF, LANES), 0)
    blend = jnp.zeros((HALF, LANES), F32)
    for k in range(blend_ref.shape[0]):
        line = jnp.sum(blend_ref[k], axis=0, keepdims=True)
        blend = blend + jnp.where(rows == k, line + swap(line), 0.0)

    def tap_of(tap):
        block = grads[tap // 3][:, (tap % 3) * LANES : (tap % 3 + 1) * LANES]
        return block[:HALF] + swap(block[HALF:])

    for pair in range(5):
        even = tap_of(2 * pair)
        odd = tap_of(2 * pair + 1) if pair < 4 else even
        both = jnp.transpose(jnp.where(first, even, swap(odd)))
        value = jnp.concatenate([both[:HALF], both[HALF:]], axis=1)
        if pair == 4:
            value = jnp.where(first, value, blend)
        pay_ref[pl.ds(pair * HALF, HALF), :] = value.astype(pay_ref.dtype)


def gate(h):
    t = jnp.tanh(h) + 1.0
    s = 0.5 * t
    act = h * t
    return act, s + act * (1.0 - s)


def halves():
    return (lanes_of((1, 8, LANES)) >= HALF).astype(jnp.int32)


def h_forward(ready, shear, beta_ref, w_ref, fm, base, fl, fr, hfeat, pre_ref, f0, fmi, fpl, beta, stage, taps, wt):
    shears = shear.shape[0]
    ready()
    spread(beta_ref, beta)
    fill_weights(w_ref, wt, 0.5)
    first16 = low((16, LANES))

    @pl.loop(0, 16, unroll=2)
    def _(y):
        for start, rows, ref in ((4, 4, fl), (8, 8, fm), (16, 4, fr)):
            for q in range(8):
                stage[q, pl.ds(y * 24 + start, rows), :] = ref[y, :, pl.ds(q * LANES, LANES)].astype(F32)

    @pl.loop(0, WIDE, unroll=2)
    def _(x):
        own = [stage[q, pl.ds(x + 8 - REACH, 16, stride=24), :] for q in range(8)]
        turned = [swap(a) for a in own]
        zero = jnp.zeros((16, LANES), F32)
        moved = [
            jnp.where(first16, turned[q - 1] if q > 0 else zero, turned[q] if q < 8 else zero).astype(BF)
            for q in range(9)
        ]
        for q in range(8):
            at = pl.ds(pl.multiple_of(x * LANES + q * 16, 16), 16)
            f0[at, :] = own[q].astype(BF)
            fmi[at, :] = moved[q]
            fpl[at, :] = moved[q + 1]

    @pl.loop(0, 4)
    def _(n):
        at = pl.ds(pl.multiple_of(n * 448, 448), 448)
        for side, ref in enumerate((fmi, f0, fpl)):
            product = mm(ref[at, :], wt[pl.ds(side * 384, 384), :], NT)
            for j in range(3):
                part = product[:, j * LANES : (j + 1) * LANES].reshape(28, 2, 8, LANES)
                taps[pl.ds((3 * side + j) * PLANE + n * 28, 28)] = part

    half = halves()

    @pl.loop(0, 64, unroll=8)
    def _(n):
        q = n % 8
        here = n + REACH * 8
        vrel = half + (2 * q - 8)
        xg = base[0] + n // 8
        mid = taps[4 * PLANE + here]
        left = taps[3 * PLANE - 8 + here]
        right = taps[5 * PLANE + 8 + here]
        branch = jnp.zeros((2, 8, LANES), F32)
        for k in range(shears):
            d = shear[k]
            xs = xg - d * vrel
            a, b = here - d * 8, here + d * 8
            main = mid + (taps[PLANE + a] + taps[7 * PLANE + b])
            minus = left + (taps[a - 8] + taps[6 * PLANE - 8 + b])
            plus = right + (taps[2 * PLANE + 8 + a] + taps[8 * PLANE + 8 + b])
            pre = main + jnp.where(xs >= 1, minus, 0.0) + jnp.where(xs <= LANES - 2, plus, 0.0)
            pre_ref[k * 64 + n] = pre
            keep = xs.astype(jnp.uint32) < LANES
            branch = branch + jnp.where(keep, beta[k] * gate(pre)[0], 0.0)
        own = f0[pl.ds(pl.multiple_of(here * 16, 16), 16), :].astype(F32)
        hfeat[q, n // 8] = (own + branch.reshape(16, LANES)).astype(BF)


def h_backward(ready, shear, beta_ref, base, pre_ref, f0, fmi, fpl, gm, pay_v, pay, rim0, rim1, rim2, out0, out1, out2, beta, dps, sums, edges, blend, edges_sem):
    shears = shear.shape[0]
    ready()
    spread(beta_ref, beta)
    half = halves()
    blend[...] = jnp.zeros(blend.shape, F32)

    @pl.loop(0, 64, unroll=8)
    def _(n):
        dps[pl.ds((n // 4) * PLANE + (n % 4) * 12, 12)] = jnp.zeros((12, 2, 8, LANES), F32)
        sums[pl.ds((n // 16) * 96 + (n % 16) * 2, 2)] = jnp.zeros((2, 2, 8, LANES), F32)
        x, q = n // 8, n % 8
        g = gm[q, x].astype(F32).reshape(2, 8, LANES)
        vrel = half + (2 * q - 8)
        xg = base[0] + x
        total = [jnp.zeros((2, 8, LANES), F32) for _ in range(3)]
        for k in range(shears):
            xs = xg - shear[k] * vrel
            act, slope = gate(pre_ref[k * 64 + n])
            gk = jnp.where(xs.astype(jnp.uint32) < LANES, g, 0.0)
            dp = (beta[k] * gk * slope).astype(BF).astype(F32)
            parts = (jnp.where(xs >= 1, dp, 0.0), dp, jnp.where(xs <= LANES - 2, dp, 0.0))
            for j in range(3):
                dps[(j * shears + k) * PLANE + 48 + n] = parts[j]
                total[j] = total[j] + parts[j]
            blend[k] += jnp.sum(gk * act, axis=0)
        for j in range(3):
            sums[j * 96 + 32 + n] = total[j]

    @pl.loop(0, WIDE * 8, unroll=8)
    def _(n):
        at = pl.ds(pl.multiple_of(n * 16, 16), 16)
        below = [jnp.zeros((2, 8, LANES), F32) for _ in range(3)]
        above = [jnp.zeros((2, 8, LANES), F32) for _ in range(3)]
        for k in range(shears):
            d = shear[k]
            up, down = n + d * 8, n - d * 8
            for j in range(3):
                offset = (j * shears + k) * PLANE + 48 - REACH * 8 - (j - 1) * 8
                below[j] = below[j] + dps[offset + up]
                above[j] = above[j] + dps[offset + down]
        for j in range(3):
            lanes = pl.ds(j * LANES, LANES)
            middle = sums[j * 96 + 32 - REACH * 8 - (j - 1) * 8 + n]
            for side, value in enumerate((below[j], middle, above[j])):
                edges[side, at, lanes] = value.reshape(16, LANES).astype(BF)

    side = REACH * LANES
    copies = []
    for i, (rim, out) in enumerate(((rim0, out0), (rim1, out1), (rim2, out2))):
        pieces = ((0, side, rim.at[pl.ds(0, side)]), (side + 1024, side, rim.at[pl.ds(side, side)]), (side, 1024, out))
        for e, (start, rows, target) in enumerate(pieces):
            copies.append(pltpu.make_async_copy(edges.at[i, pl.ds(start, rows)], target, edges_sem.at[3 * i + e]))
    for copy in copies:
        copy.start()
    pack_grads([mm(ref[...], edges[side], TN) for side, ref in enumerate((fmi, f0, fpl))], blend, pay)
    pay[pl.ds(5 * HALF, 5 * HALF), :] = pay_v[...]
    for copy in copies:
        copy.wait()


def back_through(ready, w_ref, edges, dfs, wt, chunk):
    ready(0)
    fill_weights(w_ref, wt)
    for side in range(3):
        ready(side + 1)
        for start in range(0, dfs.shape[1], chunk):
            rows = pl.ds(start, chunk)
            dfs[side, rows, :] = mm(edges[side][rows, :], wt[pl.ds(side * 384, 384), :], NN)


def column(dfs, x):
    first16 = low((16, LANES))

    def piece(side, q):
        if q < 0 or q > 7:
            return jnp.zeros((16, LANES), F32)
        return dfs[side, pl.ds(pl.multiple_of(x * LANES + q * 16, 16), 16), :]

    found = []
    for q in range(8):
        upper = piece(0, q) + piece(2, q - 1)
        lower = piece(0, q + 1) + piece(2, q)
        found.append(piece(1, q) + swap(jnp.where(first16, lower, upper)))
    return found


def h_rims(ready, w_ref, edges0, edges1, edges2, to_left, to_right, token, dfs, wt):
    token[...] = jnp.zeros(token.shape, F32)
    back_through(ready, w_ref, (edges0, edges1, edges2), dfs, wt, 768)
    for x in range(REACH):
        for q, value in enumerate(column(dfs, x)):
            to_left[x, q] = value
        for q, value in enumerate(column(dfs, x + REACH)):
            to_right[x, q] = value


def h_finish(ready, w_ref, edges0, edges1, edges2, gm, from_left, from_right, out, dfs, stage, wt):
    back_through(ready, w_ref, (edges0, edges1, edges2), dfs, wt, 512)
    ready(4)
    for x in range(8):
        for q, value in enumerate(column(dfs, x)):
            total = gm[q, x].astype(F32) + value
            if x < REACH:
                total = total + from_left[x, q]
            if x >= 8 - REACH:
                total = total + from_right[x - 8 + REACH, q]
            stage[q, pl.ds(x * 16, 16), :] = total

    @pl.loop(0, 16, unroll=2)
    def _(y):
        for q in range(8):
            out[y, :, pl.ds(q * LANES, LANES)] = stage[q, pl.ds(y, 8, stride=16), :].astype(BF)


def v_both(ready, shear, beta_ref, w_ref, cot, h_ref, out, dvert, pay, beta, own, fv, taps, dps, sums, grads, outs, edges, blend, wt):
    shears = shear.shape[0]
    wide = 22
    plane = 10 * wide
    blend[...] = jnp.zeros(blend.shape, F32)
    first8 = low((8, LANES))

    for u in (0, 9):
        sheet = jnp.zeros((wide, 8, LANES), F32)
        for tap in (0, 1, 2) if u == 0 else (6, 7, 8):
            taps[pl.ds(tap * plane + u * wide, wide)] = sheet
        for jk in range(3 * shears):
            dps[pl.ds(jk * plane + u * wide, wide)] = sheet

    @pl.loop(1, 9)
    def _(u):
        rim = jnp.zeros((REACH, 8, LANES), F32)
        for side in (0, 16 + REACH):
            for tap in range(TAPS):
                taps[pl.ds(tap * plane + side + u * wide, REACH)] = rim
            for j in range(3):
                sums[pl.ds(j * plane + side + u * wide, REACH)] = rim
            for jk in range(3 * shears):
                dps[pl.ds(jk * plane + side + u * wide, REACH)] = rim

    ready()
    spread(beta_ref, beta)
    fill_weights(w_ref, wt, 0.5)

    @pl.loop(0, 8, unroll=2)
    def _(u):
        for x in range(8):
            own[u, pl.ds(x * 16, 16), :] = h_ref[u, x].astype(F32)
        for y in range(0, 16, 2):
            pair = [own[u, pl.ds(y + e, 8, stride=16), :] for e in range(2)]
            fv[pl.ds(pl.multiple_of(u * LANES + y * 8, 16), 16), :] = jnp.concatenate(pair, axis=0).astype(BF)
        for q in range(8):
            lanes = pl.ds(pl.multiple_of((u * 8 + q) * LANES, LANES), LANES)
            a, b = cot[0, :, lanes].astype(F32), cot[1, :, lanes].astype(F32)
            grads[u, 2 * q] = jnp.where(first8, a, swap(b))
            grads[u, 2 * q + 1] = jnp.where(first8, swap(a), b)

    @pl.loop(0, 2)
    def _(n):
        rows = pl.ds(pl.multiple_of(n * 512, 512), 512)
        for side in range(3):
            product = mm(fv[rows, :], wt[pl.ds(side * 384, 384), :], NT)
            for j in range(3):
                part = product[:, j * LANES : (j + 1) * LANES].reshape(4, 16, 8, LANES)
                for e in range(4):
                    taps[pl.ds((3 * side + j) * plane + (e + 1) * wide + REACH + n * 4 * wide, 16)] = part[e]

    def body(u, y):
        here = (u + 1) * wide + REACH + y
        g = grads[u, y]
        mid = taps[4 * plane + here]
        left = taps[3 * plane - 1 + here]
        right = taps[5 * plane + 1 + here]
        branch = jnp.zeros((8, LANES), F32)
        total = [jnp.zeros((8, LANES), F32) for _ in range(3)]
        shared = []
        for k in range(shears):
            d = shear[k]
            ys = jnp.full((8, LANES), y - d * (u - 4), jnp.int32)
            keep = ys.astype(jnp.uint32) < 16
            has_minus, has_plus = ys >= 1, ys <= 14
            a, b = here - d, here + d
            main = mid + (taps[plane - wide + a] + taps[7 * plane + wide + b])
            minus = left + (taps[-wide - 1 + a] + taps[6 * plane + wide - 1 + b])
            plus = right + (taps[2 * plane - wide + 1 + a] + taps[8 * plane + wide + 1 + b])
            act, slope = gate(main + jnp.where(has_minus, minus, 0.0) + jnp.where(has_plus, plus, 0.0))
            act = jnp.where(keep, act, 0.0)
            bk = beta[k]
            branch = branch + bk * act
            shared.append(g * act)
            dp = jnp.where(keep, bk * g * slope, 0.0).astype(BF).astype(F32)
            parts = (jnp.where(has_minus, dp, 0.0), dp, jnp.where(has_plus, dp, 0.0))
            for j in range(3):
                dps[(j * shears + k) * plane + here] = parts[j]
                total[j] = total[j] + parts[j]
        for j in range(3):
            sums[j * plane + here] = total[j]
        outs[u, y] = own[u, pl.ds(y, 8, stride=16), :] + branch
        return shared

    @pl.loop(0, 64, unroll=8)
    def _(n):
        u, y = n // 8, (n % 8) * 2
        first, second = body(u, y), body(u, y + 1)
        for k in range(shears):
            blend[k] += first[k] + second[k]

    @pl.loop(0, 8)
    def _(u):
        for step in range(8):
            here = (u + 1) * wide + (REACH + 2 * step)
            at = pl.ds(pl.multiple_of(u * LANES + step * 16, 16), 16)
            below = [jnp.zeros((2, 8, LANES), F32) for _ in range(3)]
            above = [jnp.zeros((2, 8, LANES), F32) for _ in range(3)]
            for k in range(shears):
                d = shear[k]
                up, down = here + d, here - d
                for j in range(3):
                    offset = (j * shears + k) * plane - (j - 1)
                    below[j] = below[j] + dps[pl.ds(offset + wide + up, 2)]
                    above[j] = above[j] + dps[pl.ds(offset - wide + down, 2)]
            for j in range(3):
                middle = sums[pl.ds(j * plane - (j - 1) + here, 2)]
                for side, value in enumerate((below[j], middle, above[j])):
                    edges[at, pl.ds((3 * side + j) * LANES, LANES)] = value.reshape(16, LANES).astype(BF)

    pack_grads([mm(fv[...], edges[:, pl.ds(side * 384, 384)], TN) for side in range(3)], blend, pay)

    @pl.loop(0, 2)
    def _(n):
        rows = pl.ds(pl.multiple_of(n * 512, 512), 512)
        back = 2.0 * mm(edges[rows, :], wt[...], NN).reshape(4, LANES, LANES)
        for e in range(4):
            u = 4 * n + e
            own[u] = grads[u].reshape(LANES, LANES) + back[e]
            for x in range(8):
                dvert[u, x] = own[u, pl.ds(x, 16, stride=8), :].astype(BF)
            for q in range(8):
                lanes = pl.ds(pl.multiple_of((u * 8 + q) * LANES, LANES), LANES)
                a, b = outs[u, 2 * q], outs[u, 2 * q + 1]
                out[0, :, lanes] = jnp.where(first8, a, swap(b)).astype(BF)
                out[1, :, lanes] = jnp.where(first8, swap(a), b).astype(BF)


def call(body, fetched, operands, out_shapes, scratch, cost, vmem_mib, far=()):
    vmem = pl.BlockSpec(memory_space=pltpu.VMEM)
    specs = [pl.BlockSpec(memory_space=pltpu.HBM)] * len(fetched)
    specs += [pl.BlockSpec(memory_space=pltpu.SMEM if op.dtype == jnp.int32 else pltpu.VMEM) for op in operands]
    held = [(pltpu.SMEM if op.dtype == jnp.int32 else pltpu.VMEM)(op.shape, op.dtype) for op in fetched]
    count = len(fetched)

    def kernel(*refs):
        sources, others = refs[:count], refs[count : -count - 1]
        targets, sem = refs[-count - 1 : -1], refs[-1]
        copies = [pltpu.make_async_copy(sources[i], targets[i], sem.at[i]) for i in range(count)]
        for copy in copies:
            copy.start()

        def ready(*which):
            for i in which or range(count):
                copies[i].wait()

        body(ready, *targets, *others)

    return pl.pallas_call(
        kernel,
        out_shape=out_shapes,
        in_specs=specs,
        out_specs=[pl.BlockSpec(memory_space=pltpu.HBM) if i in far else vmem for i in range(len(out_shapes))],
        scratch_shapes=list(scratch) + held + [pltpu.SemaphoreType.DMA((count,))],
        compiler_params=pltpu.CompilerParams(vmem_limit_bytes=int(vmem_mib * MIB)),
        cost_estimate=pl.CostEstimate(flops=cost, bytes_accessed=4_000_000, transcendentals=1_000_000),
    )(*[pltpu.with_memory_space_constraint(op, pltpu.HBM) for op in fetched], *operands)


def unpack(total, w_h, w_v, b_h, b_v):
    scale = 262144.0**-0.5
    for at, weight, blend in ((0, w_h, b_h), (5 * HALF, w_v, b_v)):
        for pair in range(5):
            block = total[pl.ds(at + pair * HALF, HALF), :] * scale
            weight[2 * pair] = block[:, :HALF]
            other = swap(block)[:, :HALF]
            if pair < 4:
                weight[2 * pair + 1] = other
            else:
                blend[...] = other[: blend.shape[0]]


def added(parts):
    total = parts[0]
    for i in range(1, parts.shape[0]):
        total = total + parts[i]
    return total


def reduce_all(pay, zero):
    part = lax.all_to_all(pay.reshape(16, 40, LANES), "img", 0, 0, tiled=True)
    part = jnp.broadcast_to((added(part.astype(F32)) + zero)[None], (8, 40, LANES))
    part = lax.all_to_all(part, "vrow", 0, 0, tiled=True)
    part = jnp.broadcast_to(added(part)[None], (16, 40, LANES))
    return lax.all_to_all(part, "img", 0, 0, tiled=True).reshape(640, LANES)


def whole_step(features, weight_h, weight_v, beta_h, beta_v, shear_set, cotangent):
    shears = shear_set.shape[0]
    img = lax.axis_size("img")
    sds = jax.ShapeDtypeStruct
    own = features.reshape(16, 8, 1024)
    to_right = [(i, i + 1) for i in range(img - 1)]
    to_left = [(i + 1, i) for i in range(img - 1)]
    from_left = lax.ppermute(own[:, 4:], "img", to_right)
    from_right = lax.ppermute(own[:, :4], "img", to_left)
    base = (lax.axis_index("img") * 8).astype(jnp.int32).reshape(1)
    w_h = jnp.transpose(weight_h, (2, 3, 0, 1)).reshape(TAPS, HALF, HALF)
    w_v = jnp.transpose(weight_v, (2, 3, 0, 1)).reshape(TAPS, HALF, HALF)

    hfeat, pre, f0, fmi, fpl = call(
        h_forward,
        (shear_set, beta_h, w_h, own),
        (base, from_left, from_right),
        [sds((8, 8, 16, LANES), BF), sds((shears * 64, 2, 8, LANES), F32)] + [sds((WIDE * LANES, LANES), BF)] * 3,
        [
            pltpu.VMEM((shears, 8, LANES), F32),
            pltpu.VMEM((8, 384, LANES), F32),
            pltpu.VMEM((TAPS * PLANE, 2, 8, LANES), F32),
            pltpu.VMEM((TAPS * LANES, LANES), BF),
        ],
        2 * WIDE * LANES * LANES * TAPS * LANES,
        GRANT[0],
    )
    moved = lax.all_to_all(hfeat, "vrow", 0, 0, tiled=True)
    output, dvert, pay_v = call(
        v_both,
        (shear_set, beta_v, w_v, cotangent),
        (moved,),
        [sds((2, 8, 8192), BF), sds((8, 8, 16, LANES), BF), sds((320, LANES), BF)],
        [
            pltpu.VMEM((shears, 8, LANES), F32),
            pltpu.VMEM((8, LANES, LANES), F32),
            pltpu.VMEM((1024, LANES), BF),
            pltpu.VMEM((TAPS * 220, 8, LANES), F32),
            pltpu.VMEM((3 * shears * 220, 8, LANES), F32),
            pltpu.VMEM((3 * 220, 8, LANES), F32),
            pltpu.VMEM((8, 16, 8, LANES), F32),
            pltpu.VMEM((8, 16, 8, LANES), F32),
            pltpu.VMEM((1024, TAPS * LANES), BF),
            pltpu.VMEM((shears, 8, LANES), F32),
            pltpu.VMEM((TAPS * LANES, LANES), BF),
        ],
        6 * 1024 * LANES * TAPS * LANES,
        GRANT[1],
    )
    grad = lax.all_to_all(dvert, "vrow", 0, 0, tiled=True)
    pay, rim0, rim1, rim2, *edges_h = call(
        h_backward,
        (shear_set, beta_h),
        (base, pre, f0, fmi, fpl, grad, pay_v),
        [sds((640, LANES), BF)] + [pltpu.HBM((2 * REACH * LANES, 384), BF)] * 3 + [pltpu.HBM((1024, 384), BF)] * 3,
        [
            pltpu.VMEM((shears, 8, LANES), F32),
            pltpu.VMEM((3 * shears * PLANE + 48, 2, 8, LANES), F32),
            pltpu.VMEM((3 * 96 + 32, 2, 8, LANES), F32),
            pltpu.VMEM((3, WIDE * LANES, 384), BF),
            pltpu.VMEM((shears, 8, LANES), F32),
            pltpu.SemaphoreType.DMA((9,)),
        ],
        2 * WIDE * LANES * LANES * TAPS * LANES,
        GRANT[2],
        (1, 2, 3, 4, 5, 6),
    )
    halo_left, halo_right, rims_done = call(
        h_rims,
        (w_h, rim0, rim1, rim2),
        (),
        [pltpu.HBM((REACH, 8, 16, LANES), F32)] * 2 + [sds((40, LANES), F32)],
        [pltpu.VMEM((3, 2 * REACH * LANES, LANES), F32), pltpu.VMEM((TAPS * LANES, LANES), BF)],
        2 * 2 * REACH * LANES * LANES * TAPS * LANES,
        GRANT[3],
    )
    halo_from_right = lax.ppermute(halo_left, "img", to_left)
    halo_from_left = lax.ppermute(halo_right, "img", to_right)
    (grad_features,) = call(
        h_finish,
        (w_h, *edges_h, grad),
        (halo_from_left, halo_from_right),
        [sds((16, 8, 1024), BF)],
        [pltpu.VMEM((3, 1024, LANES), F32), pltpu.VMEM((8, LANES, LANES), F32), pltpu.VMEM((TAPS * LANES, LANES), BF)],
        2 * 1024 * LANES * TAPS * LANES,
        GRANT[4],
    )
    vmem = pl.BlockSpec(memory_space=pltpu.VMEM)
    weights = sds((TAPS, HALF, HALF), F32)
    w_grad_h, w_grad_v, beta_grad_h, beta_grad_v = pl.pallas_call(
        unpack,
        out_shape=[weights, weights] + [sds((shears, HALF), F32)] * 2,
        in_specs=[vmem],
        out_specs=[vmem] * 4,
        compiler_params=pltpu.CompilerParams(vmem_limit_bytes=6 * MIB),
    )(reduce_all(pay, rims_done))

    def placed(weight):
        return jnp.transpose(weight.reshape(3, 3, HALF, HALF), (2, 3, 0, 1))

    return output, grad_features.reshape(features.shape), placed(w_grad_h), placed(w_grad_v), beta_grad_h, beta_grad_v


def solution(mesh):
    placed = (P("vrow", None, "img", None), P(), P(), P(), P(), P(), P("vrow", "img", None))
    return jax.shard_map(
        whole_step,
        mesh=mesh,
        in_specs=placed,
        out_specs=(P("vrow", "img", None), P("vrow", None, "img", None), P(), P(), P(), P()),
        check_vma=False,
    )
```

```python
import jax
import jax.numpy as jnp
from jax import lax
from jax.experimental import pallas as pl
from jax.experimental.pallas import tpu as pltpu
from jax.sharding import PartitionSpec as P


BF = jnp.bfloat16
F32 = jnp.float32
LANES = 128
HALF = 64
TAPS = 9
REACH = 3
WIDE = 8 + 2 * REACH
PLANE = WIDE * 8
MIB = 1024 * 1024
GRANT = (26, 36, 34, 20, 12)
NT = (((1,), (1,)), ((), ()))
NN = (((1,), (0,)), ((), ()))
TN = (((0,), (0,)), ((), ()))


def mm(lhs, rhs, dims):
    return lax.dot_general(lhs, rhs, dims, preferred_element_type=F32)


def lanes_of(shape):
    return lax.broadcasted_iota(jnp.int32, shape, len(shape) - 1)


def swap(value):
    return pltpu.roll(value, HALF, axis=value.ndim - 1)


def low(shape):
    return lanes_of(shape) < HALF


def fill_weights(w_ref, wt_ref, scale=1.0):
    zero = jnp.zeros((HALF, HALF), BF)
    for tap in range(TAPS):
        w = w_ref[tap]
        if scale != 1.0:
            w = (w.astype(F32) * scale).astype(BF)
        wt_ref[pl.ds(tap * LANES, HALF), :] = jnp.concatenate([w, zero], axis=1)
        wt_ref[pl.ds(tap * LANES + HALF, HALF), :] = jnp.concatenate([zero, w], axis=1)


def spread(beta_ref, beta):
    for k in range(beta.shape[0]):
        line = beta_ref[pl.ds(k, 1), :]
        beta[k] = jnp.broadcast_to(jnp.concatenate([line, line], axis=1), (8, LANES))


def pack_grads(grads, blend_ref, pay_ref):
    first = low((HALF, LANES))
    rows = lax.broadcasted_iota(jnp.int32, (HALF, LANES), 0)
    blend = jnp.zeros((HALF, LANES), F32)
    for k in range(blend_ref.shape[0]):
        line = jnp.sum(blend_ref[k], axis=0, keepdims=True)
        blend = blend + jnp.where(rows == k, line + swap(line), 0.0)

    def tap_of(tap):
        block = grads[tap // 3][:, (tap % 3) * LANES : (tap % 3 + 1) * LANES]
        return block[:HALF] + swap(block[HALF:])

    for pair in range(5):
        even = tap_of(2 * pair)
        odd = tap_of(2 * pair + 1) if pair < 4 else even
        both = jnp.transpose(jnp.where(first, even, swap(odd)))
        value = jnp.concatenate([both[:HALF], both[HALF:]], axis=1)
        if pair == 4:
            value = jnp.where(first, value, blend)
        pay_ref[pl.ds(pair * HALF, HALF), :] = value.astype(pay_ref.dtype)


def gate(h):
    t = jnp.tanh(h) + 1.0
    s = 0.5 * t
    act = h * t
    return act, s + act * (1.0 - s)


def halves():
    return (lanes_of((1, 8, LANES)) >= HALF).astype(jnp.int32)


def h_forward(ready, shear, beta_ref, w_ref, fm, base, fl, fr, hfeat, pre_ref, f0, fmi, fpl, beta, stage, taps, wt):
    shears = shear.shape[0]
    ready()
    spread(beta_ref, beta)
    fill_weights(w_ref, wt, 0.5)
    first16 = low((16, LANES))

    @pl.loop(0, 16, unroll=2)
    def _(y):
        for start, rows, ref in ((4, 4, fl), (8, 8, fm), (16, 4, fr)):
            for q in range(8):
                stage[q, pl.ds(y * 24 + start, rows), :] = ref[y, :, pl.ds(q * LANES, LANES)].astype(F32)

    @pl.loop(0, WIDE, unroll=2)
    def _(x):
        own = [stage[q, pl.ds(x + 8 - REACH, 16, stride=24), :] for q in range(8)]
        turned = [swap(a) for a in own]
        zero = jnp.zeros((16, LANES), F32)
        moved = [
            jnp.where(first16, turned[q - 1] if q > 0 else zero, turned[q] if q < 8 else zero).astype(BF)
            for q in range(9)
        ]
        for q in range(8):
            at = pl.ds(pl.multiple_of(x * LANES + q * 16, 16), 16)
            f0[at, :] = own[q].astype(BF)
            fmi[at, :] = moved[q]
            fpl[at, :] = moved[q + 1]

    @pl.loop(0, 4)
    def _(n):
        at = pl.ds(pl.multiple_of(n * 448, 448), 448)
        for side, ref in enumerate((fmi, f0, fpl)):
            product = mm(ref[at, :], wt[pl.ds(side * 384, 384), :], NT)
            for j in range(3):
                part = product[:, j * LANES : (j + 1) * LANES].reshape(28, 2, 8, LANES)
                taps[pl.ds((3 * side + j) * PLANE + n * 28, 28)] = part

    half = halves()

    @pl.loop(0, 8)
    def _(x):
        for q in range(8):
            n = x * 8 + q
            here = n + REACH * 8
            vrel = half + (2 * q - 8)
            xg = base[0] + x
            mid = taps[4 * PLANE + here]
            left = taps[3 * PLANE - 8 + here]
            right = taps[5 * PLANE + 8 + here]
            branch = jnp.zeros((2, 8, LANES), F32)
            for k in range(shears):
                d = shear[k]
                xs = xg - d * vrel
                a, b = here - d * 8, here + d * 8
                main = mid + (taps[PLANE + a] + taps[7 * PLANE + b])
                minus = left + (taps[a - 8] + taps[6 * PLANE - 8 + b])
                plus = right + (taps[2 * PLANE + 8 + a] + taps[8 * PLANE + 8 + b])
                pre = main + jnp.where(xs >= 1, minus, 0.0) + jnp.where(xs <= LANES - 2, plus, 0.0)
                pre_ref[k * 64 + n] = pre
                keep = xs.astype(jnp.uint32) < LANES
                branch = branch + jnp.where(keep, beta[k] * gate(pre)[0], 0.0)
            own = f0[pl.ds(pl.multiple_of(here * 16, 16), 16), :].astype(F32)
            hfeat[q, x] = (own + branch.reshape(16, LANES)).astype(BF)


def h_backward(ready, shear, beta_ref, base, pre_ref, f0, fmi, fpl, gm, pay_v, pay, rim0, rim1, rim2, out0, out1, out2, beta, dps, sums, edges, blend, edges_sem):
    shears = shear.shape[0]
    ready()
    spread(beta_ref, beta)
    half = halves()
    blend[...] = jnp.zeros(blend.shape, F32)

    @pl.loop(0, 8)
    def _(x):
        for q in range(8):
            n = x * 8 + q
            dps[pl.ds((x * 2 + q // 4) * PLANE + (q % 4) * 12, 12)] = jnp.zeros((12, 2, 8, LANES), F32)
            sums[pl.ds((x // 2) * 96 + (x % 2) * 16 + q * 2, 2)] = jnp.zeros((2, 2, 8, LANES), F32)
            g = gm[q, x].astype(F32).reshape(2, 8, LANES)
            vrel = half + (2 * q - 8)
            xg = base[0] + x
            total = [jnp.zeros((2, 8, LANES), F32) for _ in range(3)]
            for k in range(shears):
                xs = xg - shear[k] * vrel
                act, slope = gate(pre_ref[k * 64 + n])
                gk = jnp.where(xs.astype(jnp.uint32) < LANES, g, 0.0)
                dp = (beta[k] * gk * slope).astype(BF).astype(F32)
                parts = (jnp.where(xs >= 1, dp, 0.0), dp, jnp.where(xs <= LANES - 2, dp, 0.0))
                for j in range(3):
                    dps[(j * shears + k) * PLANE + 48 + n] = parts[j]
                    total[j] = total[j] + parts[j]
                blend[k] += jnp.sum(gk * act, axis=0)
            for j in range(3):
                sums[j * 96 + 32 + n] = total[j]

    @pl.loop(0, WIDE * 8, unroll=8)
    def _(n):
        at = pl.ds(pl.multiple_of(n * 16, 16), 16)
        below = [jnp.zeros((2, 8, LANES), F32) for _ in range(3)]
        above = [jnp.zeros((2, 8, LANES), F32) for _ in range(3)]
        for k in range(shears):
            d = shear[k]
            up, down = n + d * 8, n - d * 8
            for j in range(3):
                offset = (j * shears + k) * PLANE + 48 - REACH * 8 - (j - 1) * 8
                below[j] = below[j] + dps[offset + up]
                above[j] = above[j] + dps[offset + down]
        for j in range(3):
            lanes = pl.ds(j * LANES, LANES)
            middle = sums[j * 96 + 32 - REACH * 8 - (j - 1) * 8 + n]
            for side, value in enumerate((below[j], middle, above[j])):
                edges[side, at, lanes] = value.reshape(16, LANES).astype(BF)

    side = REACH * LANES
    copies = []
    for i, (rim, out) in enumerate(((rim0, out0), (rim1, out1), (rim2, out2))):
        pieces = ((0, side, rim.at[pl.ds(0, side)]), (side + 1024, side, rim.at[pl.ds(side, side)]), (side, 1024, out))
        for e, (start, rows, target) in enumerate(pieces):
            copies.append(pltpu.make_async_copy(edges.at[i, pl.ds(start, rows)], target, edges_sem.at[3 * i + e]))
    for copy in copies:
        copy.start()
    pack_grads([mm(ref[...], edges[side], TN) for side, ref in enumerate((fmi, f0, fpl))], blend, pay)
    pay[pl.ds(5 * HALF, 5 * HALF), :] = pay_v[...]
    for copy in copies:
        copy.wait()


def back_through(ready, w_ref, edges, dfs, wt, chunk):
    ready(0)
    fill_weights(w_ref, wt)
    for side in range(3):
        ready(side + 1)
        for start in range(0, dfs.shape[1], chunk):
            rows = pl.ds(start, chunk)
            dfs[side, rows, :] = mm(edges[side][rows, :], wt[pl.ds(side * 384, 384), :], NN)


def column(dfs, x):
    first16 = low((16, LANES))

    def piece(side, q):
        if q < 0 or q > 7:
            return jnp.zeros((16, LANES), F32)
        return dfs[side, pl.ds(pl.multiple_of(x * LANES + q * 16, 16), 16), :]

    found = []
    for q in range(8):
        upper = piece(0, q) + piece(2, q - 1)
        lower = piece(0, q + 1) + piece(2, q)
        found.append(piece(1, q) + swap(jnp.where(first16, lower, upper)))
    return found


def h_rims(ready, w_ref, edges0, edges1, edges2, to_left, to_right, token, dfs, wt):
    token[...] = jnp.zeros(token.shape, F32)
    back_through(ready, w_ref, (edges0, edges1, edges2), dfs, wt, 768)
    for x in range(REACH):
        for q, value in enumerate(column(dfs, x)):
            to_left[x, q] = value
        for q, value in enumerate(column(dfs, x + REACH)):
            to_right[x, q] = value


def h_finish(ready, w_ref, edges0, edges1, edges2, gm, from_left, from_right, out, dfs, stage, wt):
    back_through(ready, w_ref, (edges0, edges1, edges2), dfs, wt, 512)
    ready(4)
    for x in range(8):
        for q, value in enumerate(column(dfs, x)):
            total = gm[q, x].astype(F32) + value
            if x < REACH:
                total = total + from_left[x, q]
            if x >= 8 - REACH:
                total = total + from_right[x - 8 + REACH, q]
            stage[q, pl.ds(x * 16, 16), :] = total

    @pl.loop(0, 16, unroll=2)
    def _(y):
        for q in range(8):
            out[y, :, pl.ds(q * LANES, LANES)] = stage[q, pl.ds(y, 8, stride=16), :].astype(BF)


def v_both(ready, shear, beta_ref, w_ref, cot, h_ref, out, dvert, pay, beta, own, fv, taps, dps, sums, grads, outs, edges, blend, wt):
    shears = shear.shape[0]
    wide = 22
    plane = 10 * wide
    blend[...] = jnp.zeros(blend.shape, F32)
    first8 = low((8, LANES))

    for u in (0, 9):
        sheet = jnp.zeros((wide, 8, LANES), F32)
        for tap in (0, 1, 2) if u == 0 else (6, 7, 8):
            taps[pl.ds(tap * plane + u * wide, wide)] = sheet
        for jk in range(3 * shears):
            dps[pl.ds(jk * plane + u * wide, wide)] = sheet

    @pl.loop(1, 9)
    def _(u):
        rim = jnp.zeros((REACH, 8, LANES), F32)
        for side in (0, 16 + REACH):
            for tap in range(TAPS):
                taps[pl.ds(tap * plane + side + u * wide, REACH)] = rim
            for j in range(3):
                sums[pl.ds(j * plane + side + u * wide, REACH)] = rim
            for jk in range(3 * shears):
                dps[pl.ds(jk * plane + side + u * wide, REACH)] = rim

    ready()
    spread(beta_ref, beta)
    fill_weights(w_ref, wt, 0.5)

    @pl.loop(0, 8, unroll=2)
    def _(u):
        for x in range(8):
            own[u, pl.ds(x * 16, 16), :] = h_ref[u, x].astype(F32)
        for y in range(0, 16, 2):
            pair = [own[u, pl.ds(y + e, 8, stride=16), :] for e in range(2)]
            fv[pl.ds(pl.multiple_of(u * LANES + y * 8, 16), 16), :] = jnp.concatenate(pair, axis=0).astype(BF)
        for q in range(8):
            lanes = pl.ds(pl.multiple_of((u * 8 + q) * LANES, LANES), LANES)
            a, b = cot[0, :, lanes].astype(F32), cot[1, :, lanes].astype(F32)
            grads[u, 2 * q] = jnp.where(first8, a, swap(b))
            grads[u, 2 * q + 1] = jnp.where(first8, swap(a), b)

    @pl.loop(0, 2)
    def _(n):
        rows = pl.ds(pl.multiple_of(n * 512, 512), 512)
        for side in range(3):
            product = mm(fv[rows, :], wt[pl.ds(side * 384, 384), :], NT)
            for j in range(3):
                part = product[:, j * LANES : (j + 1) * LANES].reshape(4, 16, 8, LANES)
                for e in range(4):
                    taps[pl.ds((3 * side + j) * plane + (e + 1) * wide + REACH + n * 4 * wide, 16)] = part[e]

    def body(u, y):
        here = (u + 1) * wide + REACH + y
        g = grads[u, y]
        mid = taps[4 * plane + here]
        left = taps[3 * plane - 1 + here]
        right = taps[5 * plane + 1 + here]
        branch = jnp.zeros((8, LANES), F32)
        total = [jnp.zeros((8, LANES), F32) for _ in range(3)]
        shared = []
        for k in range(shears):
            d = shear[k]
            ys = jnp.full((8, LANES), y - d * (u - 4), jnp.int32)
            keep = ys.astype(jnp.uint32) < 16
            has_minus, has_plus = ys >= 1, ys <= 14
            a, b = here - d, here + d
            main = mid + (taps[plane - wide + a] + taps[7 * plane + wide + b])
            minus = left + (taps[-wide - 1 + a] + taps[6 * plane + wide - 1 + b])
            plus = right + (taps[2 * plane - wide + 1 + a] + taps[8 * plane + wide + 1 + b])
            act, slope = gate(main + jnp.where(has_minus, minus, 0.0) + jnp.where(has_plus, plus, 0.0))
            act = jnp.where(keep, act, 0.0)
            bk = beta[k]
            branch = branch + bk * act
            shared.append(g * act)
            dp = jnp.where(keep, bk * g * slope, 0.0).astype(BF).astype(F32)
            parts = (jnp.where(has_minus, dp, 0.0), dp, jnp.where(has_plus, dp, 0.0))
            for j in range(3):
                dps[(j * shears + k) * plane + here] = parts[j]
                total[j] = total[j] + parts[j]
        for j in range(3):
            sums[j * plane + here] = total[j]
        outs[u, y] = own[u, pl.ds(y, 8, stride=16), :] + branch
        return shared

    @pl.loop(0, 64, unroll=8)
    def _(n):
        u, y = n // 8, (n % 8) * 2
        first, second = body(u, y), body(u, y + 1)
        for k in range(shears):
            blend[k] += first[k] + second[k]

    @pl.loop(0, 8)
    def _(u):
        for step in range(8):
            here = (u + 1) * wide + (REACH + 2 * step)
            at = pl.ds(pl.multiple_of(u * LANES + step * 16, 16), 16)
            below = [jnp.zeros((2, 8, LANES), F32) for _ in range(3)]
            above = [jnp.zeros((2, 8, LANES), F32) for _ in range(3)]
            for k in range(shears):
                d = shear[k]
                up, down = here + d, here - d
                for j in range(3):
                    offset = (j * shears + k) * plane - (j - 1)
                    below[j] = below[j] + dps[pl.ds(offset + wide + up, 2)]
                    above[j] = above[j] + dps[pl.ds(offset - wide + down, 2)]
            for j in range(3):
                middle = sums[pl.ds(j * plane - (j - 1) + here, 2)]
                for side, value in enumerate((below[j], middle, above[j])):
                    edges[at, pl.ds((3 * side + j) * LANES, LANES)] = value.reshape(16, LANES).astype(BF)

    pack_grads([mm(fv[...], edges[:, pl.ds(side * 384, 384)], TN) for side in range(3)], blend, pay)

    @pl.loop(0, 2)
    def _(n):
        rows = pl.ds(pl.multiple_of(n * 512, 512), 512)
        back = 2.0 * mm(edges[rows, :], wt[...], NN).reshape(4, LANES, LANES)
        for e in range(4):
            u = 4 * n + e
            own[u] = grads[u].reshape(LANES, LANES) + back[e]
            for x in range(8):
                dvert[u, x] = own[u, pl.ds(x, 16, stride=8), :].astype(BF)
            for q in range(8):
                lanes = pl.ds(pl.multiple_of((u * 8 + q) * LANES, LANES), LANES)
                a, b = outs[u, 2 * q], outs[u, 2 * q + 1]
                out[0, :, lanes] = jnp.where(first8, a, swap(b)).astype(BF)
                out[1, :, lanes] = jnp.where(first8, swap(a), b).astype(BF)


def call(body, fetched, operands, out_shapes, scratch, cost, vmem_mib, far=()):
    vmem = pl.BlockSpec(memory_space=pltpu.VMEM)
    specs = [pl.BlockSpec(memory_space=pltpu.HBM)] * len(fetched)
    specs += [pl.BlockSpec(memory_space=pltpu.SMEM if op.dtype == jnp.int32 else pltpu.VMEM) for op in operands]
    held = [(pltpu.SMEM if op.dtype == jnp.int32 else pltpu.VMEM)(op.shape, op.dtype) for op in fetched]
    count = len(fetched)

    def kernel(*refs):
        sources, others = refs[:count], refs[count : -count - 1]
        targets, sem = refs[-count - 1 : -1], refs[-1]
        copies = [pltpu.make_async_copy(sources[i], targets[i], sem.at[i]) for i in range(count)]
        for copy in copies:
            copy.start()

        def ready(*which):
            for i in which or range(count):
                copies[i].wait()

        body(ready, *targets, *others)

    return pl.pallas_call(
        kernel,
        out_shape=out_shapes,
        in_specs=specs,
        out_specs=[pl.BlockSpec(memory_space=pltpu.HBM) if i in far else vmem for i in range(len(out_shapes))],
        scratch_shapes=list(scratch) + held + [pltpu.SemaphoreType.DMA((count,))],
        compiler_params=pltpu.CompilerParams(vmem_limit_bytes=int(vmem_mib * MIB)),
        cost_estimate=pl.CostEstimate(flops=cost, bytes_accessed=4_000_000, transcendentals=1_000_000),
    )(*[pltpu.with_memory_space_constraint(op, pltpu.HBM) for op in fetched], *operands)


def unpack(total, w_h, w_v, b_h, b_v):
    scale = 262144.0**-0.5
    for at, weight, blend in ((0, w_h, b_h), (5 * HALF, w_v, b_v)):
        for pair in range(5):
            block = total[pl.ds(at + pair * HALF, HALF), :] * scale
            weight[2 * pair] = block[:, :HALF]
            other = swap(block)[:, :HALF]
            if pair < 4:
                weight[2 * pair + 1] = other
            else:
                blend[...] = other[: blend.shape[0]]


def added(parts):
    total = parts[0]
    for i in range(1, parts.shape[0]):
        total = total + parts[i]
    return total


def reduce_all(pay, zero):
    part = lax.all_to_all(pay.reshape(16, 40, LANES), "img", 0, 0, tiled=True)
    part = jnp.broadcast_to((added(part.astype(F32)) + zero)[None], (8, 40, LANES))
    part = lax.all_to_all(part, "vrow", 0, 0, tiled=True)
    part = jnp.broadcast_to(added(part)[None], (16, 40, LANES))
    return lax.all_to_all(part, "img", 0, 0, tiled=True).reshape(640, LANES)


def whole_step(features, weight_h, weight_v, beta_h, beta_v, shear_set, cotangent):
    shears = shear_set.shape[0]
    img = lax.axis_size("img")
    sds = jax.ShapeDtypeStruct
    own = features.reshape(16, 8, 1024)
    to_right = [(i, i + 1) for i in range(img - 1)]
    to_left = [(i + 1, i) for i in range(img - 1)]
    from_left = lax.ppermute(own[:, 4:], "img", to_right)
    from_right = lax.ppermute(own[:, :4], "img", to_left)
    base = (lax.axis_index("img") * 8).astype(jnp.int32).reshape(1)
    w_h = jnp.transpose(weight_h, (2, 3, 0, 1)).reshape(TAPS, HALF, HALF)
    w_v = jnp.transpose(weight_v, (2, 3, 0, 1)).reshape(TAPS, HALF, HALF)

    hfeat, pre, f0, fmi, fpl = call(
        h_forward,
        (shear_set, beta_h, w_h, own),
        (base, from_left, from_right),
        [sds((8, 8, 16, LANES), BF), sds((shears * 64, 2, 8, LANES), F32)] + [sds((WIDE * LANES, LANES), BF)] * 3,
        [
            pltpu.VMEM((shears, 8, LANES), F32),
            pltpu.VMEM((8, 384, LANES), F32),
            pltpu.VMEM((TAPS * PLANE, 2, 8, LANES), F32),
            pltpu.VMEM((TAPS * LANES, LANES), BF),
        ],
        2 * WIDE * LANES * LANES * TAPS * LANES,
        GRANT[0],
    )
    moved = lax.all_to_all(hfeat, "vrow", 0, 0, tiled=True)
    output, dvert, pay_v = call(
        v_both,
        (shear_set, beta_v, w_v, cotangent),
        (moved,),
        [sds((2, 8, 8192), BF), sds((8, 8, 16, LANES), BF), sds((320, LANES), BF)],
        [
            pltpu.VMEM((shears, 8, LANES), F32),
            pltpu.VMEM((8, LANES, LANES), F32),
            pltpu.VMEM((1024, LANES), BF),
            pltpu.VMEM((TAPS * 220, 8, LANES), F32),
            pltpu.VMEM((3 * shears * 220, 8, LANES), F32),
            pltpu.VMEM((3 * 220, 8, LANES), F32),
            pltpu.VMEM((8, 16, 8, LANES), F32),
            pltpu.VMEM((8, 16, 8, LANES), F32),
            pltpu.VMEM((1024, TAPS * LANES), BF),
            pltpu.VMEM((shears, 8, LANES), F32),
            pltpu.VMEM((TAPS * LANES, LANES), BF),
        ],
        6 * 1024 * LANES * TAPS * LANES,
        GRANT[1],
    )
    grad = lax.all_to_all(dvert, "vrow", 0, 0, tiled=True)
    pay, rim0, rim1, rim2, *edges_h = call(
        h_backward,
        (shear_set, beta_h),
        (base, pre, f0, fmi, fpl, grad, pay_v),
        [sds((640, LANES), BF)] + [pltpu.HBM((2 * REACH * LANES, 384), BF)] * 3 + [pltpu.HBM((1024, 384), BF)] * 3,
        [
            pltpu.VMEM((shears, 8, LANES), F32),
            pltpu.VMEM((3 * shears * PLANE + 48, 2, 8, LANES), F32),
            pltpu.VMEM((3 * 96 + 32, 2, 8, LANES), F32),
            pltpu.VMEM((3, WIDE * LANES, 384), BF),
            pltpu.VMEM((shears, 8, LANES), F32),
            pltpu.SemaphoreType.DMA((9,)),
        ],
        2 * WIDE * LANES * LANES * TAPS * LANES,
        GRANT[2],
        (1, 2, 3, 4, 5, 6),
    )
    halo_left, halo_right, rims_done = call(
        h_rims,
        (w_h, rim0, rim1, rim2),
        (),
        [pltpu.HBM((REACH, 8, 16, LANES), F32)] * 2 + [sds((40, LANES), F32)],
        [pltpu.VMEM((3, 2 * REACH * LANES, LANES), F32), pltpu.VMEM((TAPS * LANES, LANES), BF)],
        2 * 2 * REACH * LANES * LANES * TAPS * LANES,
        GRANT[3],
    )
    halo_from_right = lax.ppermute(halo_left, "img", to_left)
    halo_from_left = lax.ppermute(halo_right, "img", to_right)
    (grad_features,) = call(
        h_finish,
        (w_h, *edges_h, grad),
        (halo_from_left, halo_from_right),
        [sds((16, 8, 1024), BF)],
        [pltpu.VMEM((3, 1024, LANES), F32), pltpu.VMEM((8, LANES, LANES), F32), pltpu.VMEM((TAPS * LANES, LANES), BF)],
        2 * 1024 * LANES * TAPS * LANES,
        GRANT[4],
    )
    vmem = pl.BlockSpec(memory_space=pltpu.VMEM)
    weights = sds((TAPS, HALF, HALF), F32)
    w_grad_h, w_grad_v, beta_grad_h, beta_grad_v = pl.pallas_call(
        unpack,
        out_shape=[weights, weights] + [sds((shears, HALF), F32)] * 2,
        in_specs=[vmem],
        out_specs=[vmem] * 4,
        compiler_params=pltpu.CompilerParams(vmem_limit_bytes=6 * MIB),
    )(reduce_all(pay, rims_done))

    def placed(weight):
        return jnp.transpose(weight.reshape(3, 3, HALF, HALF), (2, 3, 0, 1))

    return output, grad_features.reshape(features.shape), placed(w_grad_h), placed(w_grad_v), beta_grad_h, beta_grad_v


def solution(mesh):
    placed = (P("vrow", None, "img", None), P(), P(), P(), P(), P(), P("vrow", "img", None))
    return jax.shard_map(
        whole_step,
        mesh=mesh,
        in_specs=placed,
        out_specs=(P("vrow", "img", None), P("vrow", None, "img", None), P(), P(), P(), P()),
        check_vma=False,
    )
```
